512 devices in a mesh: dp: 4 (over y), expert: 8 (over x, core), ctx: 16 (over z).
Axes of the slice: x: 4, y: 4, z: 16, core: 2. Of those that a mesh axis runs over, the one named last changes fastest.
Arguments:
- mamba_in: bfloat16 [4, 4096, 4096], P('dp', 'ctx', 'expert'), may hold values from -6 to 6
- shared_in: bfloat16 [4, 4096, 256], P('dp', 'ctx'), may hold values from -6 to 6
- dt_raw: float32 [4, 64, 4096], P('dp', 'expert', 'ctx'), may hold values from -3 to 3
- dt_bias: float32 [64], P('expert'), may hold values from -1 to 0.5
- a_log: float32 [64], P('expert'), as said below
- d_skip: float32 [64], P('expert'), may hold values from 0.5 to 1.5
- conv_x: float32 [4, 4096], P(None, 'expert'), may hold values from -3 to 3
- conv_bc: float32 [4, 256], replicated, may hold values from -1.5 to 1.5
- mamba_cot: bfloat16 [4, 4096, 4096], P('dp', 'ctx', 'expert'), may hold values from -6 to 6
- moe_in: bfloat16 [4, 4096, 4096], P('dp', 'expert', 'ctx'), may hold values from -6 to 6
- moe_cot: bfloat16 [4, 4096, 4096], P('dp', 'expert', 'ctx'), may hold values from -6 to 6
- slot_tok: int32 [4, 8, 8, 128], P('dp', 'expert'), may hold values from 0 to 511, as said below
- slot_count: int32 [4, 8, 8], P('dp', 'expert'), may hold values from 32 to 128, as said below
- route_w: bfloat16 [4, 8, 8, 128], P('dp', 'expert'), may hold values from 0.049804688 to 0.5
- w_gate: bfloat16 [8, 4096, 768], P('expert', 'ctx'), may hold values from -0.09375 to 0.09375
- w_up: bfloat16 [8, 4096, 768], P('expert', 'ctx'), may hold values from -0.09375 to 0.09375
- w_down: bfloat16 [8, 768, 4096], P('expert', None, 'ctx'), may hold values from -0.21875 to 0.21875
- gate_act: bfloat16 [4, 8, 1024, 768], P('dp', 'expert', 'ctx'), may hold values from -6 to 6
- up_act: bfloat16 [4, 8, 1024, 768], P('dp', 'expert', 'ctx'), may hold values from -6 to 6
Outputs:
- d_mamba_in: bfloat16 [4, 4096, 4096], P('dp', 'ctx', 'expert')
- d_shared_in: bfloat16 [4, 4096, 256], P('dp', 'ctx')
- d_dt_raw: float32 [4, 64, 4096], P('dp', 'expert', 'ctx')
- d_conv_x: float32 [4, 4096], P('dp', 'expert')
- d_conv_bc: float32 [4, 256], P('dp')
- d_a_log: float32 [64], P('expert')
- d_moe_in: bfloat16 [4, 4096, 4096], P('dp', 'expert', 'ctx')
- d_route: float32 [4, 8, 8, 128], P('dp', 'expert')
- d_w_gate: bfloat16 [8, 4096, 768], P('expert', 'ctx', 'dp')
- d_w_up: bfloat16 [8, 4096, 768], P('expert', 'ctx', 'dp')
- d_w_down: bfloat16 [8, 768, 4096], P('expert', 'dp', 'ctx')
The draws below stay inside these ranges and needn't reach their ends.
Inputs may be any that keep to these rules, and one draw needn't show every extreme that they name: slot_tok[r, s, e, k] is a token of source s's 512 tokens; the live slots of one group name distinct tokens; slots at k >= slot_count[r, s, e] are padding and are ignored; a token may be live in the groups of several experts. `slot_count`: in every replica one expert receives a full group of 128 live slots from every source. exp(a_log) lies between 0.2 / 4096 and 0.1.
All inputs are finite; a program needn't handle non-finite values.
Results may differ from the reference program's by a relative error of at most 0.02.
Values may be sent and summed in bfloat16 or wider, within the bound.
No kernel may reach another device: no remote copies, remote signals or barrier semaphores. Data moves between devices by JAX's collectives and lax.ppermute only.
A program may use at most 128 MiB of HBM per device.

```python
import math
import jax
import jax.numpy as jnp
from jax import lax

D = 4096
FF = 768
HDIM = 64
NSTATE = 128
KCONV = 4
TOK_CTX = 256
TOK_EXP = 512
CAP = 128
HEADS = 64
SEQ = 4096
EXPERTS = 8
SOURCES = 8
ROWS = 1024
MOE_TOKENS = 4096
REPLICAS = 4
N_CTX = 16


def routing_tables(key):
    score_key, count_key, full_key = jax.random.split(key, 3)
    scores = jax.random.randint(score_key, (REPLICAS, SOURCES, EXPERTS, TOK_EXP), 0, 1 << 20)
    scores = scores * TOK_EXP + jnp.arange(TOK_EXP, dtype=jnp.int32)
    ordering = jnp.argsort(scores, axis=-1)
    slot_ids = ordering[..., :CAP].astype(jnp.int32)
    counts = jax.random.randint(count_key, (REPLICAS, SOURCES, EXPERTS), CAP // 4, CAP + 1)
    full_expert = jax.random.randint(full_key, (REPLICAS,), 0, EXPERTS)
    counts = jnp.where(jnp.arange(EXPERTS, dtype=jnp.int32)[None, None, :] == full_expert[:, None, None], CAP, counts)
    return (slot_ids, counts.astype(jnp.int32))


def draw_slot_tok(key, part):
    return routing_tables(jax.random.fold_in(key, 11))[0]


def draw_slot_count(key, part):
    return routing_tables(jax.random.fold_in(key, 11))[1]


def draw_a_log(key, part):
    pick_key, slow_key, fast_key = jax.random.split(key, 3)
    slow_share = 0.5
    slow_heads = jax.random.uniform(pick_key, (HEADS,), jnp.float32) < slow_share
    slow_rate = jax.random.uniform(slow_key, (HEADS,), jnp.float32, math.log(0.2 / SEQ), math.log(2.0 / SEQ))
    fast_rate = jax.random.uniform(fast_key, (HEADS,), jnp.float32, math.log(0.03), math.log(0.1))
    return jnp.where(slow_heads, slow_rate, fast_rate).astype(jnp.float32)


def levels(stream_key, dims, cuts, smallest, top_value):
    loudness, own = 1.0, jax.random.fold_in(stream_key, 6)
    for axis_at, parts in cuts:
        steps = jnp.exp(jax.random.uniform(jax.random.fold_in(own, axis_at), (parts,), jnp.float32, smallest / len(cuts), top_value / len(cuts)))
        loudness = loudness * jnp.repeat(steps, dims[axis_at] // parts).reshape([-1 if axis == axis_at else 1 for axis in range(len(dims))])
    return loudness


def gaussian(key, shape, width, reach, cuts=(), held_as=jnp.bfloat16):
    array = width * jax.random.normal(key, shape, jnp.float32)
    if cuts:
        array = array * levels(key, shape, cuts, -0.22, 0.18)
    return jnp.clip(array, -reach, reach).astype(held_as)


def setup_inputs(seed: int = 0) -> dict:
    keys = jax.random.split(jax.random.key(seed), 20)
    mamba_in = gaussian(keys[0], (REPLICAS, SEQ, HEADS * HDIM), 1.0, 6.0, ((0, 4), (1, 16), (2, 8)))
    shared_in = gaussian(keys[1], (REPLICAS, SEQ, 2 * NSTATE), 1.0, 6.0, ((0, 4), (1, 16)))
    dt_raw = gaussian(keys[2], (REPLICAS, HEADS, SEQ), 0.5, 3.0, ((0, 4), (1, 8), (2, 16)), jnp.float32)
    dt_bias = jnp.clip(-1.0 + 1.5 * jax.random.uniform(keys[3], (HEADS,), jnp.float32) ** levels(keys[3], (HEADS,), ((0, 8),), -0.2, 0.2), -1.0, 0.5)
    a_log = draw_a_log(jax.random.fold_in(keys[19], 71), 0)
    d_skip = jnp.clip(0.5 + 1.0 * jax.random.uniform(keys[5], (HEADS,), jnp.float32) ** levels(keys[5], (HEADS,), ((0, 8),), -0.2, 0.2), 0.5, 1.5)
    conv_x = gaussian(keys[6], (KCONV, HEADS * HDIM), KCONV ** -0.5, 3.0, ((1, 8),), jnp.float32)
    conv_bc = gaussian(keys[7], (KCONV, 2 * NSTATE), (4 * KCONV) ** -0.5, 1.5, (), jnp.float32)
    mamba_cot = gaussian(keys[8], (REPLICAS, SEQ, HEADS * HDIM), 1.0, 6.0, ((0, 4), (1, 16), (2, 8)))
    moe_in = gaussian(keys[9], (REPLICAS, MOE_TOKENS, D), 1.0, 6.0, ((0, 4), (1, 8), (2, 16)))
    moe_cot = gaussian(keys[10], (REPLICAS, MOE_TOKENS, D), 1.0, 6.0, ((0, 4), (1, 8), (2, 16)))
    slot_tok = draw_slot_tok(jax.random.fold_in(keys[19], 71), 0)
    slot_count = draw_slot_count(jax.random.fold_in(keys[19], 71), 0)
    route_w = jnp.clip(0.049804688 + 0.4501953 * jax.random.uniform(keys[13], (REPLICAS, SOURCES, EXPERTS, CAP), jnp.float32) ** levels(keys[13], (REPLICAS, SOURCES, EXPERTS, CAP), ((0, 4), (1, 8)), -0.2, 0.2), 0.049804688, 0.5).astype(jnp.bfloat16)
    w_gate = gaussian(keys[14], (EXPERTS, D, FF), D ** -0.5, 0.09375, ((0, 8), (1, 16)))
    w_up = gaussian(keys[15], (EXPERTS, D, FF), D ** -0.5, 0.09375, ((0, 8), (1, 16)))
    w_down = gaussian(keys[16], (EXPERTS, FF, D), FF ** -0.5, 0.21875, ((0, 8), (2, 16)))
    gate_act = gaussian(keys[17], (REPLICAS, EXPERTS, ROWS, FF), 1.0, 6.0, ((0, 4), (1, 8), (2, 16)))
    up_act = gaussian(keys[18], (REPLICAS, EXPERTS, ROWS, FF), 1.0, 6.0, ((0, 4), (1, 8), (2, 16)))
    return dict(mamba_in=mamba_in, shared_in=shared_in, dt_raw=dt_raw, dt_bias=dt_bias, a_log=a_log, d_skip=d_skip, conv_x=conv_x, conv_bc=conv_bc, mamba_cot=mamba_cot, moe_in=moe_in, moe_cot=moe_cot, slot_tok=slot_tok, slot_count=slot_count, route_w=route_w, w_gate=w_gate, w_up=w_up, w_down=w_down, gate_act=gate_act, up_act=up_act)


PRECISE = lax.Precision.HIGHEST

def causal_taps(padded_values, kernel):
    taps_count = kernel.shape[0]
    length = padded_values.shape[0] - taps_count + 1
    summed = kernel[0][None, :] * padded_values[0:length]
    for offset in range(1, taps_count):
        summed = summed + kernel[offset][None, :] * padded_values[offset:offset + length]
    return summed

def state_block(heads_in, b_rows, c_rows, step_size, log_decay, skip_gain, state_in):
    length = heads_in.shape[0]
    cumulative = jnp.cumsum(log_decay, axis=1)
    lower_mask = jnp.tril(jnp.ones((length, length), dtype=bool))
    spacing = jnp.where(lower_mask[None], cumulative[:, :, None] - cumulative[:, None, :], 0.0)
    decays = jnp.where(lower_mask[None], jnp.exp(spacing), 0.0)
    scores = jnp.dot(c_rows, b_rows.T, precision=PRECISE)
    mixing = decays * scores[None] * step_size[:, None, :]
    output = jnp.einsum('hts,shp->thp', mixing, heads_in, precision=PRECISE)
    carried = jnp.einsum('tn,hpn->thp', c_rows, state_in, precision=PRECISE)
    output = output + jnp.exp(cumulative).T[:, :, None] * carried + skip_gain[None, :, None] * heads_in
    ending = cumulative[:, -1]
    tail_weight = jnp.exp(ending[:, None] - cumulative) * step_size
    fresh_state = jnp.einsum('ht,thp,tn->hpn', tail_weight, heads_in, b_rows, precision=PRECISE)
    return (output, jnp.exp(ending)[:, None, None] * state_in + fresh_state)

def mamba_forward(raw_heads, raw_shared, raw_step, step_bias, log_rate, skip_gain, kernel_heads, kernel_shared):
    taps_count = kernel_heads.shape[0]
    pad_heads = jnp.concatenate([jnp.zeros((taps_count - 1, raw_heads.shape[1]), raw_heads.dtype), raw_heads], axis=0)
    pad_shared = jnp.concatenate([jnp.zeros((taps_count - 1, raw_shared.shape[1]), raw_shared.dtype), raw_shared], axis=0)
    conv_heads = jax.nn.silu(causal_taps(pad_heads, kernel_heads))
    conv_shared = jax.nn.silu(causal_taps(pad_shared, kernel_shared))
    step_size = jax.nn.softplus(raw_step + step_bias[:, None])
    log_decay = -jnp.exp(log_rate)[:, None] * step_size
    heads_in = conv_heads.reshape(N_CTX, TOK_CTX, HEADS, HDIM)
    b_blocks = conv_shared[:, :NSTATE].reshape(N_CTX, TOK_CTX, NSTATE)
    c_blocks = conv_shared[:, NSTATE:].reshape(N_CTX, TOK_CTX, NSTATE)
    step_blocks = step_size.reshape(HEADS, N_CTX, TOK_CTX).transpose(1, 0, 2)
    decay_blocks = log_decay.reshape(HEADS, N_CTX, TOK_CTX).transpose(1, 0, 2)

    def advance(state_in, pieces):
        output, state_out = state_block(pieces[0], pieces[1], pieces[2], pieces[3], pieces[4], skip_gain, state_in)
        return (state_out, output)
    start_state = jnp.zeros((HEADS, HDIM, NSTATE), conv_heads.dtype)
    _, outputs = lax.scan(advance, start_state, (heads_in, b_blocks, c_blocks, step_blocks, decay_blocks))
    return outputs.reshape(SEQ, HEADS, HDIM)

def reference(mamba_in, shared_in, dt_raw, dt_bias, a_log, d_skip, conv_x, conv_bc, mamba_cot, moe_in, moe_cot, slot_tok, slot_count, route_w, w_gate, w_up, w_down, gate_act, up_act):

    def mamba_replica(carry_sums, items):
        raw_heads, raw_shared, raw_step, cotangent = items

        def forward(heads_arg, shared_arg, step_arg, rate_arg, kernel_first, kernel_second):
            return mamba_forward(heads_arg, shared_arg, step_arg, dt_bias, rate_arg, d_skip, kernel_first, kernel_second)
        _, pullback = jax.vjp(forward, raw_heads.astype(jnp.float32), raw_shared.astype(jnp.float32), raw_step, a_log, conv_x, conv_bc)
        grads = pullback(cotangent.astype(jnp.float32).reshape(SEQ, HEADS, HDIM))
        carry_sums = (carry_sums[0] + grads[4], carry_sums[1] + grads[5], carry_sums[2] + grads[3])
        return (carry_sums, (grads[0].astype(jnp.bfloat16), grads[1].astype(jnp.bfloat16), grads[2]))
    mamba_start = (jnp.zeros_like(conv_x), jnp.zeros_like(conv_bc), jnp.zeros_like(a_log))
    mamba_sums, mamba_rows = lax.scan(mamba_replica, mamba_start, (mamba_in, shared_in, dt_raw, mamba_cot))

    def moe_replica(carry_sums, items):
        tokens_in, cotangent, slot_ids, slot_counts, route_weights, gate_saved, up_saved = items
        offsets = (jnp.arange(SOURCES, dtype=jnp.int32) * TOK_EXP)[:, None, None]
        global_ids = slot_ids + offsets
        live_slots = jnp.arange(CAP, dtype=jnp.int32)[None, None, :] < slot_counts[:, :, None]
        zero_half = jnp.zeros((), jnp.bfloat16)

        def per_expert(grad_tokens, expert_index):
            row_ids = global_ids[:, expert_index, :].reshape(ROWS)
            keep_rows = live_slots[:, expert_index, :].reshape(ROWS)
            rows_in = jnp.where(keep_rows[:, None], tokens_in[row_ids], zero_half)
            rows_cot = jnp.where(keep_rows[:, None], cotangent[row_ids], zero_half)
            rows_weight = jnp.where(keep_rows, route_weights[:, expert_index, :].reshape(ROWS), zero_half)
            gate_vals = gate_saved[expert_index].astype(jnp.float32)
            up_vals = up_saved[expert_index].astype(jnp.float32)
            sigmoid_vals = jax.nn.sigmoid(gate_vals)
            activated = gate_vals * sigmoid_vals
            hidden = (jax.nn.silu(gate_vals) * up_vals).astype(jnp.bfloat16)
            down_weight = w_down[expert_index]
            expert_out = jnp.dot(hidden, down_weight, preferred_element_type=jnp.float32)
            route_grad = lax.optimization_barrier(jnp.sum(rows_cot.astype(jnp.float32) * expert_out, axis=1))
            scaled_cot = (rows_weight.astype(jnp.float32)[:, None] * rows_cot.astype(jnp.float32)).astype(jnp.bfloat16)
            grad_down = jnp.dot(hidden.T, scaled_cot, preferred_element_type=jnp.float32)
            grad_hidden = jnp.dot(scaled_cot, down_weight.T, preferred_element_type=jnp.float32)
            slope = sigmoid_vals * (1.0 + gate_vals * (1.0 - sigmoid_vals))
            grad_gate_rows = (grad_hidden * up_vals * slope).astype(jnp.bfloat16)
            grad_up_rows = (grad_hidden * activated).astype(jnp.bfloat16)
            grad_gate = jnp.dot(rows_in.T, grad_gate_rows, preferred_element_type=jnp.float32)
            grad_up = jnp.dot(rows_in.T, grad_up_rows, preferred_element_type=jnp.float32)
            rows_grad = jnp.dot(grad_gate_rows, w_gate[expert_index].T, preferred_element_type=jnp.float32)
            rows_grad = rows_grad + jnp.dot(grad_up_rows, w_up[expert_index].T, preferred_element_type=jnp.float32)
            grad_tokens = grad_tokens.at[row_ids].add(jnp.where(keep_rows[:, None], rows_grad, 0.0))
            return (grad_tokens, (route_grad.reshape(SOURCES, CAP), grad_gate, grad_up, grad_down))
        tokens_zero = jnp.zeros((MOE_TOKENS, D), jnp.float32)
        grad_tokens, stacked = lax.scan(per_expert, tokens_zero, jnp.arange(EXPERTS, dtype=jnp.int32))
        route_grads, grad_gate, grad_up, grad_down = stacked
        carry_sums = (carry_sums[0] + grad_gate, carry_sums[1] + grad_up, carry_sums[2] + grad_down)
        return (carry_sums, (grad_tokens.astype(jnp.bfloat16), route_grads.transpose(1, 0, 2)))
    moe_start = (jnp.zeros((EXPERTS, D, FF), jnp.float32), jnp.zeros((EXPERTS, D, FF), jnp.float32), jnp.zeros((EXPERTS, FF, D), jnp.float32))
    moe_sums, moe_rows = lax.scan(moe_replica, moe_start, (moe_in, moe_cot, slot_tok, slot_count, route_w, gate_act, up_act))
    return (mamba_rows[0], mamba_rows[1], mamba_rows[2], mamba_sums[0], mamba_sums[1], mamba_sums[2], moe_rows[0], moe_rows[1], moe_sums[0].astype(jnp.bfloat16), moe_sums[1].astype(jnp.bfloat16), moe_sums[2].astype(jnp.bfloat16))
```

```python
import jax
import jax.numpy as jnp
from jax import lax
from jax.experimental import pallas as pl
from jax.experimental.pallas import tpu as pltpu
from jax.sharding import PartitionSpec as P

PRECISE = lax.Precision.HIGHEST
F32 = jnp.float32
BF16 = jnp.bfloat16


def passed_along(value, axis, steps):
    count = lax.axis_size(axis)
    first, last = (max(0, -steps), min(count, count - steps))
    return lax.ppermute(value, axis, [(source, source + steps) for source in range(first, last)])


def exchange(value, axis):
    return lax.all_to_all(value, axis, split_axis=0, concat_axis=0, tiled=True)


def copies(value, count):
    return jnp.broadcast_to(value[None], (count,) + value.shape)


def causal_taps(padded_values, kernel):
    taps_count = kernel.shape[0]
    length = padded_values.shape[0] - taps_count + 1
    summed = kernel[0][None, :] * padded_values[0:length]
    for offset in range(1, taps_count):
        summed = summed + kernel[offset][None, :] * padded_values[offset : offset + length]
    return summed


def conv_front(padded_values, kernel):
    return jax.nn.silu(causal_taps(padded_values, kernel))


def state_block(heads_in, b_rows, c_rows, step_size, log_decay, skip_gain, state_in):
    length = heads_in.shape[0]
    cumulative = jnp.cumsum(log_decay, axis=1)
    lower_mask = jnp.tril(jnp.ones((length, length), dtype=bool))
    spacing = jnp.where(lower_mask[None], cumulative[:, :, None] - cumulative[:, None, :], 0.0)
    decays = jnp.where(lower_mask[None], jnp.exp(spacing), 0.0)
    scores = jnp.dot(c_rows, b_rows.T, precision=PRECISE)
    mixing = decays * scores[None] * step_size[:, None, :]
    output = jnp.einsum("hts,shp->thp", mixing, heads_in, precision=PRECISE)
    carried = jnp.einsum("tn,hpn->thp", c_rows, state_in, precision=PRECISE)
    output = (
        output + jnp.exp(cumulative).T[:, :, None] * carried + skip_gain[None, :, None] * heads_in
    )
    ending = cumulative[:, -1]
    tail_weight = jnp.exp(ending[:, None] - cumulative) * step_size
    fresh_state = jnp.einsum("ht,thp,tn->hpn", tail_weight, heads_in, b_rows, precision=PRECISE)
    return (output, jnp.exp(ending)[:, None, None] * state_in + fresh_state)


def scan_kernel(got_ref, out_ref):
    places, half = got_ref.shape[0], out_ref.shape[1] // 2
    width = got_ref.shape[2]
    decay = [
        jnp.exp(
            got_ref[j, 2 * half : 2 * half + 1, :].astype(F32)
            + got_ref[j, 2 * half + 1 : 2 * half + 2, :].astype(F32)
        )
        for j in range(places)
    ]
    state = jnp.zeros((half, width), F32)
    for j in range(places):
        out_ref[j, :half, :] = state.astype(BF16)
        state = decay[j] * state + got_ref[j, :half, :].astype(F32)
    state = jnp.zeros((half, width), F32)
    for j in reversed(range(places)):
        out_ref[j, half:, :] = state.astype(BF16)
        state = decay[j] * state + got_ref[j, half : 2 * half, :].astype(F32)


def states_across(local_state, local_pull, ending):
    heads, width, state_width = local_state.shape
    count = lax.axis_size("ctx")
    rows = heads * width // count
    fresh = local_state.astype(BF16).reshape(count, rows, state_width)
    pulls = local_pull.astype(BF16).reshape(count, rows, state_width)
    coarse = ending.astype(BF16)
    fine = (ending - coarse.astype(F32)).astype(BF16)
    per_head = count // heads
    marks = jnp.stack([jnp.repeat(coarse, per_head), jnp.repeat(fine, per_head)], axis=1)
    marks = jnp.broadcast_to(marks[:, :, None], (count, 2, state_width))
    marks = jnp.pad(marks, ((0, 0), (0, 14), (0, 0)))
    got = exchange(jnp.concatenate([fresh, pulls, marks], axis=1), "ctx")
    entered = pl.pallas_call(
        scan_kernel,
        out_shape=jax.ShapeDtypeStruct((count, 2 * rows, state_width), BF16),
    )(got)
    back = exchange(entered, "ctx").astype(F32)
    shape = (heads, width, state_width)
    return back[:, :rows].reshape(shape), back[:, rows:].reshape(shape)


def body(
    mamba_in,
    shared_in,
    dt_raw,
    dt_bias,
    a_log,
    d_skip,
    conv_x,
    conv_bc,
    mamba_cot,
    moe_in,
    moe_cot,
    slot_tok,
    slot_count,
    route_w,
    w_gate,
    w_up,
    w_down,
    gate_act,
    up_act,
):
    col_width = moe_in.shape[2]
    token_count = moe_in.shape[1]
    expert_count = slot_tok.shape[2]
    slot_width = slot_tok.shape[3]
    hidden_width = w_gate.shape[2]
    slot_ids = slot_tok[0, 0]
    live_slots = jnp.arange(slot_width, dtype=jnp.int32)[None, :] < slot_count[0, 0][:, None]
    chosen = jnp.where(live_slots, slot_ids, -1).reshape(-1)
    token_index = jnp.arange(token_count, dtype=jnp.int32)
    table = jnp.where(chosen[:, None] == token_index[None, :], 1.0, 0.0).astype(BF16)
    send_cot = jnp.dot(table, moe_cot[0], preferred_element_type=F32).astype(BF16)
    send_weight = jnp.where(live_slots, route_w[0, 0], jnp.zeros((), BF16))
    send_weight = jnp.pad(send_weight[:, None, :], ((0, 0), (0, 15), (0, col_width - slot_width)))
    send_cot = send_cot.reshape(expert_count, slot_width, col_width)
    got_cot = exchange(jnp.concatenate([send_cot, send_weight], axis=1), "expert")
    rows_cot = got_cot[:, :slot_width].reshape(-1, col_width)
    rows_weight = got_cot[:, slot_width, :slot_width].reshape(-1).astype(F32)
    unscaled = jnp.dot(rows_cot, w_down[0].T, preferred_element_type=F32)
    mine = lax.psum_scatter(unscaled.astype(BF16), "ctx", scatter_dimension=0, tiled=True)
    send_in = jnp.dot(table, moe_in[0], preferred_element_type=F32).astype(BF16)
    rows_in = exchange(send_in.reshape(expert_count, slot_width, col_width), "expert")
    rows_in = rows_in.reshape(-1, col_width)
    scaled_cot = (rows_weight[:, None] * rows_cot.astype(F32)).astype(BF16)

    rim_rows = conv_x.shape[0] - 1
    head_rows = mamba_in[0]
    shared_rows = shared_in[0]
    length = head_rows.shape[0]
    heads_here = dt_bias.shape[0]
    head_width = head_rows.shape[1] // heads_here
    state_width = shared_rows.shape[1] // 2
    both_rows = jnp.concatenate([head_rows, shared_rows], axis=1)
    before = passed_along(both_rows[length - rim_rows :], "ctx", 1)
    split_at = head_rows.shape[1]
    padded_heads = jnp.concatenate([before[:, :split_at], head_rows], axis=0).astype(F32)
    padded_shared = jnp.concatenate([before[:, split_at:], shared_rows], axis=0).astype(F32)
    conv_heads, pull_heads = jax.vjp(conv_front, padded_heads, conv_x)
    conv_shared, pull_shared = jax.vjp(conv_front, padded_shared, conv_bc)
    b_rows = conv_shared[:, :state_width]
    c_rows = conv_shared[:, state_width:]
    heads_in = conv_heads.reshape(length, heads_here, head_width)
    raw_step = dt_raw[0]
    step_size = jax.nn.softplus(raw_step + dt_bias[:, None])
    log_decay = -jnp.exp(a_log)[:, None] * step_size
    cumulative = jnp.cumsum(log_decay, axis=1)
    tail_weight = jnp.exp(cumulative[:, -1:] - cumulative) * step_size
    local_state = jnp.einsum("ht,thp,tn->hpn", tail_weight, heads_in, b_rows)
    cotangent = mamba_cot[0].astype(F32).reshape(length, heads_here, head_width)
    local_pull = jnp.einsum("ht,thp,tn->hpn", jnp.exp(cumulative), cotangent, c_rows)
    entering, leaving_grad = states_across(local_state, local_pull, cumulative[:, -1])

    def core(heads_arg, b_arg, c_arg, step_arg, rate_arg, state_arg):
        sizes_now = jax.nn.softplus(step_arg + dt_bias[:, None])
        decay_now = -jnp.exp(rate_arg)[:, None] * sizes_now
        return state_block(heads_arg, b_arg, c_arg, sizes_now, decay_now, d_skip, state_arg)

    _, pull_core = jax.vjp(core, heads_in, b_rows, c_rows, raw_step, a_log, entering)
    grad_heads, grad_b, grad_c, grad_step, grad_rate, _ = pull_core((cotangent, leaving_grad))
    grad_bc = jnp.concatenate([grad_b, grad_c], axis=1).astype(BF16)
    total_bc = jnp.sum(
        exchange(copies(grad_bc, lax.axis_size("expert")), "expert").astype(F32), axis=0
    )
    grad_padded_heads, grad_kernel_heads = pull_heads(
        grad_heads.reshape(length, heads_here * head_width)
    )
    grad_padded_shared, grad_kernel_shared = pull_shared(total_bc)
    after = passed_along(
        jnp.concatenate([grad_padded_heads[:rim_rows], grad_padded_shared[:rim_rows]], axis=1),
        "ctx",
        -1,
    )
    edge_pad = ((length - rim_rows, 0), (0, 0))
    grad_mamba_in = (
        grad_padded_heads[rim_rows:] + jnp.pad(after[:, :split_at], edge_pad)
    ).astype(BF16)[None]
    grad_shared_in = (
        grad_padded_shared[rim_rows:] + jnp.pad(after[:, split_at:], edge_pad)
    ).astype(BF16)[None]
    taps = jnp.concatenate([grad_kernel_heads, grad_kernel_shared], axis=1)
    dp_count = lax.axis_size("dp")
    rates = jnp.broadcast_to(jnp.pad(grad_rate, (0, 128 - heads_here))[None], (dp_count, 128))
    small = jnp.concatenate([taps, rates, jnp.zeros((dp_count, 128), F32)], axis=1)
    small = jnp.sum(exchange(small.reshape(dp_count, 8, 128), "dp"), axis=0)
    small = jnp.sum(exchange(copies(small, lax.axis_size("ctx")), "ctx"), axis=0).reshape(1, -1)
    taps_heads = small[:, :split_at]
    taps_shared = small[:, split_at : split_at + 2 * state_width]
    rate_total = small[0, split_at + 2 * state_width :][:heads_here]

    gate_vals = gate_act[0, 0].astype(F32)
    up_vals = up_act[0, 0].astype(F32)
    own = gate_vals.shape[0]
    unscaled_own = mine.astype(F32)
    weight_own = lax.dynamic_slice_in_dim(rows_weight, lax.axis_index("ctx") * own, own, 0)
    grad_hidden = weight_own[:, None] * unscaled_own
    sigmoid_vals = jax.nn.sigmoid(gate_vals)
    activated = gate_vals * sigmoid_vals
    hidden_own = (activated * up_vals).astype(BF16)
    slope = sigmoid_vals * (1.0 + gate_vals * (1.0 - sigmoid_vals))
    gate_own = (grad_hidden * up_vals * slope).astype(BF16)
    up_own = (grad_hidden * activated).astype(BF16)
    route_own = jnp.sum(hidden_own.astype(F32) * unscaled_own, axis=1)
    route_coarse = route_own.astype(BF16)
    route_fine = (route_own - route_coarse.astype(F32)).astype(BF16)
    route_cols = jnp.pad(jnp.stack([route_coarse, route_fine], axis=1), ((0, 0), (0, 126)))
    everything = lax.all_gather(
        jnp.concatenate([gate_own, up_own, hidden_own, route_cols], axis=1),
        "ctx",
        axis=0,
        tiled=True,
    )
    gate_rows = everything[:, :hidden_width]
    up_rows = everything[:, hidden_width : 2 * hidden_width]
    hidden = everything[:, 2 * hidden_width : 3 * hidden_width]
    route_pair = everything[:, 3 * hidden_width : 3 * hidden_width + 2]
    rows_grad = jnp.dot(gate_rows, w_gate[0].T, preferred_element_type=F32)
    rows_grad = rows_grad + jnp.dot(up_rows, w_up[0].T, preferred_element_type=F32)
    route_back = route_pair.reshape(expert_count, slot_width, 2).transpose(0, 2, 1)
    route_back = jnp.pad(
        route_back.reshape(expert_count, 1, 2 * slot_width), ((0, 0), (0, 15), (0, 0))
    )
    back = exchange(
        jnp.concatenate(
            [rows_grad.astype(BF16).reshape(expert_count, slot_width, col_width), route_back],
            axis=1,
        ),
        "expert",
    )
    grad_tokens = lax.dot_general(
        table,
        back[:, :slot_width].reshape(-1, col_width),
        (((0,), (0,)), ((), ())),
        preferred_element_type=F32,
    )
    route_got = back[:, slot_width].astype(F32)
    route_total = jnp.where(
        live_slots, route_got[:, :slot_width] + route_got[:, slot_width:], 0.0
    )
    share = hidden_width // dp_count

    def weight_grad(left, right):
        full = lax.dot_general(
            left, right, (((0,), (0,)), ((), ())), preferred_element_type=F32
        )
        return full.astype(BF16).reshape(dp_count, share, col_width)

    parts = exchange(
        jnp.concatenate(
            [
                weight_grad(gate_rows, rows_in),
                weight_grad(up_rows, rows_in),
                weight_grad(hidden, scaled_cot),
            ],
            axis=1,
        ),
        "dp",
    )
    totals = jnp.sum(parts.astype(F32), axis=0).astype(BF16)
    return (
        grad_mamba_in,
        grad_shared_in,
        grad_step[None],
        taps_heads,
        taps_shared,
        rate_total,
        grad_tokens.astype(BF16)[None],
        route_total[None, None],
        totals[:share].T[None],
        totals[share : 2 * share].T[None],
        totals[2 * share :][None],
    )


def solution(mesh):
    placed = (
        P("dp", "ctx", "expert"),
        P("dp", "ctx", None),
        P("dp", "expert", "ctx"),
        P("expert"),
        P("expert"),
        P("expert"),
        P(None, "expert"),
        P(),
        P("dp", "ctx", "expert"),
        P("dp", "expert", "ctx"),
        P("dp", "expert", "ctx"),
        P("dp", "expert", None, None),
        P("dp", "expert", None),
        P("dp", "expert", None, None),
        P("expert", "ctx", None),
        P("expert", "ctx", None),
        P("expert", None, "ctx"),
        P("dp", "expert", "ctx", None),
        P("dp", "expert", "ctx", None),
    )
    return jax.shard_map(
        body,
        mesh=mesh,
        in_specs=placed,
        out_specs=(
            P("dp", "ctx", "expert"),
            P("dp", "ctx", None),
            P("dp", "expert", "ctx"),
            P("dp", "expert"),
            P("dp", None),
            P("expert"),
            P("dp", "expert", "ctx"),
            P("dp", "expert", None, None),
            P("expert", "ctx", "dp"),
            P("expert", "ctx", "dp"),
            P("expert", "dp", "ctx"),
        ),
        check_vma=False,
    )
```

```python
import jax
import jax.numpy as jnp
from jax import lax
from jax.experimental import pallas as pl
from jax.experimental.pallas import tpu as pltpu
from jax.sharding import PartitionSpec as P

PRECISE = lax.Precision.HIGHEST
F32 = jnp.float32
BF16 = jnp.bfloat16


def passed_along(value, axis, steps):
    count = lax.axis_size(axis)
    first, last = (max(0, -steps), min(count, count - steps))
    return lax.ppermute(value, axis, [(source, source + steps) for source in range(first, last)])


def exchange(value, axis):
    return lax.all_to_all(value, axis, split_axis=0, concat_axis=0, tiled=True)


def copies(value, count):
    return jnp.broadcast_to(value[None], (count,) + value.shape)


def dot(a, b, ca, cb, precise=False):
    return lax.dot_general(
        a,
        b,
        (((ca,), (cb,)), ((), ())),
        precision=PRECISE if precise else None,
        preferred_element_type=F32,
    )


def iota(shape, axis):
    return lax.broadcasted_iota(jnp.int32, shape, axis)


def conv_pre(rows_ref, before_ref, taps_ref, pad_ref):
    length, width = rows_ref.shape
    taps = taps_ref.shape[0]
    pad_ref[0:8, :] = jnp.zeros((8, width), F32)
    pad_ref[8 - (taps - 1) : 8, :] = before_ref[...].astype(F32)
    pad_ref[8:, :] = rows_ref[...].astype(F32)
    pre = None
    for k in range(taps):
        start = 8 - (taps - 1) + k
        term = taps_ref[k : k + 1, :] * pad_ref[start : start + length, :]
        pre = term if pre is None else pre + term
    sig = jax.nn.sigmoid(pre)
    return pre, sig


def conv_pull(grad_pre, taps_ref, pad_ref, dv_ref):
    length, width = grad_pre.shape
    taps = taps_ref.shape[0]
    dv_ref[0:8, :] = jnp.zeros((8, width), F32)
    dv_ref[8 : 8 + length, :] = grad_pre
    dv_ref[8 + length :, :] = jnp.zeros((8, width), F32)
    rows = None
    rim = None
    sums = []
    for k in range(taps):
        weight = taps_ref[k : k + 1, :]
        start = 8 + (taps - 1) - k
        term = weight * dv_ref[start : start + length, :]
        rows = term if rows is None else rows + term
        edge = weight * dv_ref[8 - k : 16 - k, :]
        rim = edge if rim is None else rim + edge
        start = 8 - (taps - 1) + k
        sums.append(jnp.sum(grad_pre * pad_ref[start : start + length, :], axis=0, keepdims=True))
    rim = jnp.where(iota(rim.shape, 0) < taps - 1, rim, 0.0)
    return rows, rim, sums


def steps_of(raw_ref, bias_ref, rate_ref):
    shifted = raw_ref[...] + bias_ref[...]
    step = jnp.maximum(shifted, 0.0) + jnp.log1p(jnp.exp(-jnp.abs(shifted)))
    rate = jnp.exp(rate_ref[...])
    log_decay = -rate * step
    length = shifted.shape[1]
    square = (length, length)
    upto = jnp.where(iota(square, 0) <= iota(square, 1), 1.0, 0.0)
    cumulative = dot(log_decay, upto, 1, 0, True)
    return shifted, step, rate, log_decay, upto, cumulative


def head_spread(heads, width):
    spread = (heads, heads * width)
    return jnp.where(iota(spread, 1) // width == iota(spread, 0), 1.0, 0.0)


def front_kernel(
    rows_ref, shared_ref, beforeh_ref, befores_ref, raw_ref, bias_ref, rate_ref, tapsx_ref,
    tapsbc_ref, cot_ref, out_ref, padh_ref, pads_ref,
):
    heads = raw_ref.shape[0]
    width = rows_ref.shape[1] // heads
    states = shared_ref.shape[1] // 2
    places = out_ref.shape[0]
    part = heads * width // places
    pre, sig = conv_pre(rows_ref, beforeh_ref, tapsx_ref, padh_ref)
    x = pre * sig
    pre_s, sig_s = conv_pre(shared_ref, befores_ref, tapsbc_ref, pads_ref)
    bc = (pre_s * sig_s).astype(BF16)
    _, step, _, _, _, cumulative = steps_of(raw_ref, bias_ref, rate_ref)
    length = step.shape[1]
    ending = cumulative[:, length - 1 :]
    spread = head_spread(heads, width)
    weight = dot(jnp.exp(ending - cumulative) * step, spread, 0, 0, True)
    grown = dot(jnp.exp(cumulative), spread, 0, 0, True)
    fresh = dot((x * weight).astype(BF16), bc[:, :states], 0, 0)
    pulls = dot((cot_ref[...].astype(F32) * grown).astype(BF16), bc[:, states:], 0, 0)
    out_ref[:, :part, :] = fresh.astype(BF16).reshape(places, part, states)
    out_ref[:, part : 2 * part, :] = pulls.astype(BF16).reshape(places, part, states)
    coarse = ending.astype(BF16).astype(F32)
    fine = ending - coarse
    per_head = places // heads
    mark = (16, states)
    for place in range(places):
        head = place // per_head
        marks = jnp.where(
            iota(mark, 0) == 0,
            jnp.broadcast_to(coarse[head : head + 1], mark),
            jnp.broadcast_to(fine[head : head + 1], mark),
        )
        out_ref[place, 2 * part :, :] = marks.astype(BF16)


def back_kernel(
    rows_ref, shared_ref, beforeh_ref, befores_ref, raw_ref, bias_ref, rate_ref, skip_ref,
    tapsx_ref, tapsbc_ref, cot_ref, got_ref,
    main_ref, tail_ref, rim_ref, bc_ref, raw_out_ref, taps_out_ref, rate_out_ref,
    padh_ref, pads_ref, dv_ref, sums_ref,
):
    heads, length = raw_ref.shape
    width = rows_ref.shape[1] // heads
    states = shared_ref.shape[1] // 2
    part = got_ref.shape[1] // 2
    pre, sig = conv_pre(rows_ref, beforeh_ref, tapsx_ref, padh_ref)
    x = pre * sig
    pre_s, sig_s = conv_pre(shared_ref, befores_ref, tapsbc_ref, pads_ref)
    bc = (pre_s * sig_s).astype(BF16)
    b_rows, c_rows = bc[:, :states], bc[:, states:]
    shifted, step, rate, log_decay, upto, cumulative = steps_of(raw_ref, bias_ref, rate_ref)
    ending = cumulative[:, length - 1 :]
    spread = head_spread(heads, width)
    weight = dot(jnp.exp(ending - cumulative) * step, spread, 0, 0, True)
    grown = dot(jnp.exp(cumulative), spread, 0, 0, True)
    step_cols = dot(step, spread, 0, 0, True)
    skip_cols = jnp.sum(skip_ref[...] * spread, axis=0, keepdims=True)
    state_in = got_ref[:, :part, :].reshape(heads * width, states)
    pull_out = got_ref[:, part:, :].reshape(heads * width, states)
    cot = cot_ref[...]
    cot_wide = cot.astype(F32)
    b_pull = dot(b_rows, pull_out, 1, 1)
    c_state = dot(c_rows, state_in, 1, 1)
    cot_grown = cot_wide * grown
    x_weight = x * weight
    grad_c = dot(cot_grown.astype(BF16), state_in, 1, 0)
    grad_b = dot(x_weight.astype(BF16), pull_out, 1, 0)
    lane = (heads * width, 128)
    lane_of, head_of = iota(lane, 1), iota(lane, 0) // width
    pick = jnp.where((lane_of == head_of) | (lane_of == 2 * heads + head_of), 1.0, 0.0)
    pick_next = jnp.where(lane_of == heads + head_of, 1.0, 0.0)
    columns = dot(x_weight * b_pull, pick, 1, 0, True)
    columns = columns + dot(cot_grown * c_state, pick_next, 1, 0, True)
    scores = dot(b_rows, c_rows, 1, 1)
    square = (length, length)
    earlier = iota(square, 0) <= iota(square, 1)
    cumulative_cols = dot(upto, log_decay, 0, 1, True)
    x_step = (x * step_cols).astype(BF16)
    pair = max(1, 128 // width)
    block = pair * width
    lane_head = iota((length, block), 1) // width
    column_lane = iota((length, 128), 1)
    grad_scores = jnp.zeros(square, F32)
    inner = []
    for base in range(0, heads, pair):
        at = base * width
        x_pair = x_step[:, at : at + block]
        cot_pair = cot[:, at : at + block]
        sum_pair = None
        for i in range(pair):
            head = base + i
            cot_one = jnp.where(lane_head == i, cot_pair, jnp.zeros((), BF16))
            grad_mix = dot(x_pair, cot_one, 1, 1)
            gap = cumulative[head : head + 1, :] - cumulative_cols[:, head : head + 1]
            decay = jnp.exp(jnp.where(earlier, gap, -1e30))
            mix = decay * scores
            grad_scores = grad_scores + decay * grad_mix
            moved = mix * grad_mix
            sums_ref[head : head + 1, :] = jnp.sum(moved, axis=0, keepdims=True)
            columns = columns + jnp.where(
                column_lane == head, jnp.sum(moved, axis=1, keepdims=True), 0.0
            )
            term = dot(mix.astype(BF16), cot_one, 1, 0)
            sum_pair = term if sum_pair is None else sum_pair + term
        inner.append(sum_pair)
    inner = jnp.concatenate(inner, axis=1)
    grad_scores = grad_scores.astype(BF16)
    grad_b = grad_b + dot(grad_scores, c_rows, 1, 0)
    grad_c = grad_c + dot(grad_scores, b_rows, 0, 0)
    grad_bc = jnp.concatenate([grad_b, grad_c], axis=1).astype(BF16)
    for copy in range(bc_ref.shape[0]):
        bc_ref[copy] = grad_bc
    turned = columns.T
    left = turned[:heads]
    came = sums_ref[...] + turned[heads : 2 * heads]
    state_pull = state_in.astype(F32) * pull_out.astype(F32)
    state_pull = jnp.sum(state_pull.reshape(heads, width, states), axis=1)
    state_pull = jnp.exp(ending) * jnp.sum(state_pull, axis=1, keepdims=True)
    to_last = jnp.sum(turned[2 * heads : 3 * heads], axis=1, keepdims=True)
    grad_decay = dot(came - left, upto, 1, 1, True) + to_last + state_pull
    grad_step = left / step - rate * grad_decay
    raw_out_ref[...] = grad_step * jax.nn.sigmoid(shifted)
    grad_rate = jnp.sum(grad_decay * log_decay, axis=1, keepdims=True)
    eye = jnp.where(iota((heads, 128), 0) == iota((heads, 128), 1), 1.0, 0.0)
    rate_out_ref[...] = jnp.sum(grad_rate * eye, axis=0, keepdims=True)
    grad_x = inner * step_cols + skip_cols * cot_wide + weight * b_pull
    grad_pre = grad_x * (sig * (1.0 + pre * (1.0 - sig)))
    rows, rim, sums = conv_pull(grad_pre, tapsx_ref, padh_ref, dv_ref)
    main_ref[...] = rows.astype(BF16)
    tail_ref[...] = rows[length - 16 :]
    rim_ref[...] = rim
    for k, total in enumerate(sums):
        taps_out_ref[k : k + 1, :] = total


def shared_kernel(
    shared_ref, befores_ref, tapsbc_ref, got_ref,
    main_ref, tail_ref, rim_ref, taps_out_ref, pads_ref, dv_ref,
):
    length = shared_ref.shape[0]
    pre, sig = conv_pre(shared_ref, befores_ref, tapsbc_ref, pads_ref)
    total = got_ref[0].astype(F32)
    for source in range(1, got_ref.shape[0]):
        total = total + got_ref[source].astype(F32)
    grad_pre = total * (sig * (1.0 + pre * (1.0 - sig)))
    rows, rim, sums = conv_pull(grad_pre, tapsbc_ref, pads_ref, dv_ref)
    main_ref[...] = rows.astype(BF16)
    tail_ref[...] = rows[length - 16 :]
    rim_ref[...] = rim
    for k, value in enumerate(sums):
        taps_out_ref[k : k + 1, :] = value


def own_rows_kernel(mine_ref, weight_ref, gate_ref, up_ref, after_ref, out_ref):
    del after_ref
    width = mine_ref.shape[1]
    unscaled = mine_ref[...].astype(F32)
    gate = gate_ref[...].astype(F32)
    up = up_ref[...].astype(F32)
    grad_hidden = weight_ref[...] * unscaled
    sig = jax.nn.sigmoid(gate)
    activated = gate * sig
    hidden = (activated * up).astype(BF16)
    slope = sig * (1.0 + gate * (1.0 - sig))
    out_ref[:, :width] = (grad_hidden * up * slope).astype(BF16)
    out_ref[:, width : 2 * width] = (grad_hidden * activated).astype(BF16)
    out_ref[:, 2 * width : 3 * width] = hidden
    route = jnp.sum(hidden.astype(F32) * unscaled, axis=1, keepdims=True)
    coarse = route.astype(BF16).astype(F32)
    lanes = (mine_ref.shape[0], 128)
    out_ref[:, 3 * width :] = jnp.where(
        iota(lanes, 1) == 0, coarse, jnp.where(iota(lanes, 1) == 1, route - coarse, 0.0)
    ).astype(BF16)


def rows_kernel(all_ref, in_ref, cot_ref, gatew_ref, upw_ref, after_ref, back_ref, parts_ref):
    del after_ref
    groups, slots, cols = in_ref.shape
    width = gatew_ref.shape[1]
    owners, share3 = parts_ref.shape[0], parts_ref.shape[1]
    share = share3 // 3
    rows_grad = dot(all_ref[:, :width], gatew_ref[...], 1, 1)
    rows_grad = rows_grad + dot(all_ref[:, width : 2 * width], upw_ref[...], 1, 1)
    back_ref[:, :slots, :] = rows_grad.astype(BF16).reshape(groups, slots, cols)
    route = all_ref[:, 3 * width :].astype(F32)
    scaled = []
    for group in range(groups):
        turned = route[group * slots : (group + 1) * slots].T
        line = jnp.concatenate([turned[0:1], turned[1:2]], axis=1)
        back_ref[group, slots:, :] = jnp.broadcast_to(line, (16, cols)).astype(BF16)
        weight = cot_ref[group, slots:, :slots].astype(F32).T[:, 0:1]
        scaled.append((cot_ref[group, :slots, :].astype(F32) * weight).astype(BF16))
    scaled = jnp.concatenate(scaled, axis=0)
    rows_in = in_ref[...].reshape(groups * slots, cols)
    grads = [
        dot(all_ref[:, :width], rows_in, 0, 0).astype(BF16),
        dot(all_ref[:, width : 2 * width], rows_in, 0, 0).astype(BF16),
        dot(all_ref[:, 2 * width : 3 * width], scaled, 0, 0).astype(BF16),
    ]
    for owner in range(owners):
        for kind in range(3):
            parts_ref[owner, kind * share : (kind + 1) * share, :] = grads[kind][
                owner * share : (owner + 1) * share
            ]


def scan_kernel(got_ref, out_ref):
    places, half = got_ref.shape[0], out_ref.shape[1] // 2
    width = got_ref.shape[2]
    decay = [
        jnp.exp(
            got_ref[j, 2 * half : 2 * half + 1, :].astype(F32)
            + got_ref[j, 2 * half + 1 : 2 * half + 2, :].astype(F32)
        )
        for j in range(places)
    ]
    state = jnp.zeros((half, width), F32)
    for j in range(places):
        out_ref[j, :half, :] = state.astype(BF16)
        state = decay[j] * state + got_ref[j, :half, :].astype(F32)
    state = jnp.zeros((half, width), F32)
    for j in reversed(range(places)):
        out_ref[j, half:, :] = state.astype(BF16)
        state = decay[j] * state + got_ref[j, half : 2 * half, :].astype(F32)


def whole(kernel, outs, scratch=(), late=0, inputs=0, limit=None):
    specs = [pl.BlockSpec(memory_space=pltpu.VMEM)] * inputs
    specs += [pl.BlockSpec(memory_space=pl.ANY)] * late
    return pl.pallas_call(
        kernel,
        out_shape=[jax.ShapeDtypeStruct(shape, kind) for shape, kind in outs],
        in_specs=specs,
        out_specs=[pl.BlockSpec(memory_space=pltpu.VMEM)] * len(outs),
        scratch_shapes=[pltpu.VMEM(shape, kind) for shape, kind in scratch],
        compiler_params=pltpu.CompilerParams(vmem_limit_bytes=limit),
    )


def with_last_rows(main, tail, after):
    rows = tail.shape[0]
    given = jnp.pad(after, ((rows - after.shape[0], 0), (0, 0)))
    return lax.dynamic_update_slice(
        main, (tail + given).astype(BF16), (main.shape[0] - rows, 0)
    )


def body(
    mamba_in,
    shared_in,
    dt_raw,
    dt_bias,
    a_log,
    d_skip,
    conv_x,
    conv_bc,
    mamba_cot,
    moe_in,
    moe_cot,
    slot_tok,
    slot_count,
    route_w,
    w_gate,
    w_up,
    w_down,
    gate_act,
    up_act,
):
    dp_count, expert_places, ctx_places = (
        lax.axis_size("dp"),
        lax.axis_size("expert"),
        lax.axis_size("ctx"),
    )
    col_width = moe_in.shape[2]
    token_count = moe_in.shape[1]
    expert_count = slot_tok.shape[2]
    slot_width = slot_tok.shape[3]
    hidden_width = w_gate.shape[2]
    slot_ids = slot_tok[0, 0]
    live_slots = jnp.arange(slot_width, dtype=jnp.int32)[None, :] < slot_count[0, 0][:, None]
    chosen = jnp.where(live_slots, slot_ids, -1).reshape(-1)
    token_index = jnp.arange(token_count, dtype=jnp.int32)
    table = jnp.where(chosen[:, None] == token_index[None, :], 1.0, 0.0).astype(BF16)
    send_cot = jnp.dot(table, moe_cot[0], preferred_element_type=F32).astype(BF16)
    send_weight = jnp.where(live_slots, route_w[0, 0], jnp.zeros((), BF16))
    send_weight = jnp.pad(send_weight[:, None, :], ((0, 0), (0, 15), (0, col_width - slot_width)))
    send_cot = send_cot.reshape(expert_count, slot_width, col_width)
    got_cot = exchange(jnp.concatenate([send_cot, send_weight], axis=1), "expert")
    rows_cot = got_cot[:, :slot_width].reshape(-1, col_width)
    rows_weight = got_cot[:, slot_width, :slot_width].reshape(-1).astype(F32)
    unscaled = jnp.dot(rows_cot, w_down[0].T, preferred_element_type=F32)
    mine = lax.psum_scatter(unscaled.astype(BF16), "ctx", scatter_dimension=0, tiled=True)
    send_in = jnp.dot(table, moe_in[0], preferred_element_type=F32).astype(BF16)
    rows_in = exchange(send_in.reshape(expert_count, slot_width, col_width), "expert")

    rim_rows = conv_x.shape[0] - 1
    head_rows = mamba_in[0]
    shared_rows = shared_in[0]
    cot_rows = mamba_cot[0]
    raw_step = dt_raw[0]
    length, split_at = head_rows.shape
    shared_width = shared_rows.shape[1]
    state_width = shared_width // 2
    heads_here = dt_bias.shape[0]
    part = split_at // ctx_places
    bias, rate, skip = dt_bias[:, None], a_log[:, None], d_skip[:, None]
    before = passed_along(
        jnp.concatenate([head_rows[length - rim_rows :], shared_rows[length - rim_rows :]], axis=1),
        "ctx",
        1,
    )
    before_heads, before_shared = before[:, :split_at], before[:, split_at:]
    pad_heads = ((8 + length, split_at), F32)
    pad_shared = ((8 + length, shared_width), F32)
    (states,) = whole(
        front_kernel,
        [((ctx_places, 2 * part + 16, state_width), BF16)],
        [pad_heads, pad_shared],
        inputs=10,
    )(
        head_rows, shared_rows, before_heads, before_shared, raw_step, bias, rate, conv_x,
        conv_bc, cot_rows,
    )
    (entered,) = whole(
        scan_kernel, [((ctx_places, 2 * part, state_width), BF16)], inputs=1
    )(exchange(states, "ctx"))
    main_heads, tail_heads, rim_heads, grad_bc, grad_step, taps_heads, grad_rate = whole(
        back_kernel,
        [
            ((length, split_at), BF16),
            ((16, split_at), F32),
            ((8, split_at), F32),
            ((expert_places, length, shared_width), BF16),
            ((heads_here, length), F32),
            ((rim_rows + 1, split_at), F32),
            ((1, 128), F32),
        ],
        [pad_heads, pad_shared, ((16 + length, split_at), F32), ((heads_here, length), F32)],
        inputs=12,
        limit=48 * 2**20,
    )(
        head_rows, shared_rows, before_heads, before_shared, raw_step, bias, rate, skip, conv_x,
        conv_bc, cot_rows, exchange(entered, "ctx"),
    )
    after_heads = passed_along(rim_heads[:rim_rows], "ctx", -1)
    grad_mamba_in = with_last_rows(main_heads, tail_heads, after_heads)
    main_shared, tail_shared, rim_shared, taps_shared = whole(
        shared_kernel,
        [
            ((length, shared_width), BF16),
            ((16, shared_width), F32),
            ((8, shared_width), F32),
            ((rim_rows + 1, shared_width), F32),
        ],
        [pad_shared, ((16 + length, shared_width), F32)],
        inputs=4,
    )(shared_rows, before_shared, conv_bc, exchange(grad_bc, "expert"))
    after_shared = passed_along(rim_shared[:rim_rows], "ctx", -1)
    grad_shared_in = with_last_rows(main_shared, tail_shared, after_shared)
    small = jnp.concatenate(
        [
            taps_heads,
            taps_shared,
            jnp.broadcast_to(grad_rate, (dp_count, 128)),
            jnp.zeros((dp_count, 128), F32),
        ],
        axis=1,
    )
    small = jnp.sum(exchange(small.reshape(dp_count, 8, 128), "dp"), axis=0)
    small = jnp.sum(exchange(copies(small, ctx_places), "ctx"), axis=0).reshape(1, -1)
    taps_heads = small[:, :split_at]
    taps_shared = small[:, split_at : split_at + shared_width]
    rate_total = small[0, split_at + shared_width :][:heads_here]

    own = gate_act.shape[2]
    weight_own = lax.dynamic_slice_in_dim(rows_weight, lax.axis_index("ctx") * own, own, 0)
    (own_rows,) = whole(
        own_rows_kernel,
        [((own, 3 * hidden_width + 128), BF16)],
        inputs=4,
        late=1,
    )(mine, weight_own[:, None], gate_act[0, 0], up_act[0, 0], grad_step)
    everything = lax.all_gather(own_rows, "ctx", axis=0, tiled=True)
    share = hidden_width // dp_count
    back, parts = whole(
        rows_kernel,
        [
            ((expert_count, slot_width + 16, col_width), BF16),
            ((dp_count, 3 * share, col_width), BF16),
        ],
        inputs=5,
        late=1,
        limit=56 * 2**20,
    )(everything, rows_in, got_cot, w_gate[0], w_up[0], small)
    back = exchange(back, "expert")
    parts = exchange(parts, "dp")
    grad_tokens = lax.dot_general(
        table,
        back[:, :slot_width].reshape(-1, col_width),
        (((0,), (0,)), ((), ())),
        preferred_element_type=F32,
    )
    route_got = back[:, slot_width].astype(F32)
    route_total = jnp.where(
        live_slots, route_got[:, :slot_width] + route_got[:, slot_width:], 0.0
    )
    totals = jnp.sum(parts.astype(F32), axis=0).astype(BF16)
    return (
        grad_mamba_in[None],
        grad_shared_in[None],
        grad_step[None],
        taps_heads,
        taps_shared,
        rate_total,
        grad_tokens.astype(BF16)[None],
        route_total[None, None],
        totals[:share].T[None],
        totals[share : 2 * share].T[None],
        totals[2 * share :][None],
    )


def solution(mesh):
    placed = (
        P("dp", "ctx", "expert"),
        P("dp", "ctx", None),
        P("dp", "expert", "ctx"),
        P("expert"),
        P("expert"),
        P("expert"),
        P(None, "expert"),
        P(),
        P("dp", "ctx", "expert"),
        P("dp", "expert", "ctx"),
        P("dp", "expert", "ctx"),
        P("dp", "expert", None, None),
        P("dp", "expert", None),
        P("dp", "expert", None, None),
        P("expert", "ctx", None),
        P("expert", "ctx", None),
        P("expert", None, "ctx"),
        P("dp", "expert", "ctx", None),
        P("dp", "expert", "ctx", None),
    )
    return jax.shard_map(
        body,
        mesh=mesh,
        in_specs=placed,
        out_specs=(
            P("dp", "ctx", "expert"),
            P("dp", "ctx", None),
            P("dp", "expert", "ctx"),
            P("dp", "expert"),
            P("dp", None),
            P("expert"),
            P("dp", "expert", "ctx"),
            P("dp", "expert", None, None),
            P("expert", "ctx", "dp"),
            P("expert", "ctx", "dp"),
            P("expert", "dp", "ctx"),
        ),
        check_vma=False,
    )
```

```python
import jax
import jax.numpy as jnp
from jax import lax
from jax.experimental import pallas as pl
from jax.experimental.pallas import tpu as pltpu
from jax.sharding import PartitionSpec as P

PRECISE = lax.Precision.HIGHEST
F32 = jnp.float32
BF16 = jnp.bfloat16


def passed_along(value, axis, steps):
    count = lax.axis_size(axis)
    first, last = (max(0, -steps), min(count, count - steps))
    return lax.ppermute(value, axis, [(source, source + steps) for source in range(first, last)])


def exchange(value, axis):
    return lax.all_to_all(value, axis, split_axis=0, concat_axis=0, tiled=True)


def shift(value, distance):
    count = lax.axis_size("ctx")
    return lax.ppermute(value, "ctx", [(i, (i + distance) % count) for i in range(count)])


def copies(value, count):
    return jnp.broadcast_to(value[None], (count,) + value.shape)


def dot(a, b, ca, cb, precise=False):
    return lax.dot_general(
        a,
        b,
        (((ca,), (cb,)), ((), ())),
        precision=PRECISE if precise else None,
        preferred_element_type=F32,
    )


def iota(shape, axis):
    return lax.broadcasted_iota(jnp.int32, shape, axis)


def conv_pre(rows_ref, before, taps_ref, pad_ref):
    length, width = rows_ref.shape
    taps = taps_ref.shape[0]
    pad_ref[0:8, :] = jnp.zeros((8, width), F32)
    pad_ref[8 - (taps - 1) : 8, :] = before.astype(F32)
    pad_ref[8:, :] = rows_ref[...].astype(F32)
    pre = None
    for k in range(taps):
        start = 8 - (taps - 1) + k
        term = taps_ref[k : k + 1, :] * pad_ref[start : start + length, :]
        pre = term if pre is None else pre + term
    sig = jax.nn.sigmoid(pre)
    return pre, sig


def conv_pull(grad_pre, taps_ref, pad_ref, dv_ref):
    length, width = grad_pre.shape
    taps = taps_ref.shape[0]
    dv_ref[0:8, :] = jnp.zeros((8, width), F32)
    dv_ref[8 : 8 + length, :] = grad_pre
    dv_ref[8 + length :, :] = jnp.zeros((8, width), F32)
    rows = None
    rim = None
    sums = []
    for k in range(taps):
        weight = taps_ref[k : k + 1, :]
        start = 8 + (taps - 1) - k
        term = weight * dv_ref[start : start + length, :]
        rows = term if rows is None else rows + term
        edge = weight * dv_ref[8 - k : 16 - k, :]
        rim = edge if rim is None else rim + edge
        start = 8 - (taps - 1) + k
        sums.append(jnp.sum(grad_pre * pad_ref[start : start + length, :], axis=0, keepdims=True))
    rim = jnp.where(iota(rim.shape, 0) < taps - 1, rim, 0.0)
    return rows, rim, sums


def gain_column(gains_ref, which):
    heads = gains_ref.shape[1]
    eye = iota((heads, heads), 0) == iota((heads, heads), 1)
    return jnp.sum(jnp.where(eye, gains_ref[which : which + 1, :], 0.0), axis=1, keepdims=True)


def steps_of(raw_ref, gains_ref):
    shifted = raw_ref[...] + gain_column(gains_ref, 0)
    step = jnp.maximum(shifted, 0.0) + jnp.log1p(jnp.exp(-jnp.abs(shifted)))
    rate = jnp.exp(gain_column(gains_ref, 1))
    log_decay = -rate * step
    length = shifted.shape[1]
    square = (length, length)
    upto = jnp.where(iota(square, 0) <= iota(square, 1), 1.0, 0.0)
    cumulative = dot(log_decay, upto, 1, 0, True)
    return shifted, step, rate, log_decay, upto, cumulative


def head_spread(heads, width):
    spread = (heads, heads * width)
    return jnp.where(iota(spread, 1) // width == iota(spread, 0), 1.0, 0.0)


def front_kernel(
    rows_ref, shared_ref, before_ref, raw_ref, gains_ref, tapsx_ref,
    tapsbc_ref, cot_ref, out_ref, padh_ref, pads_ref,
):
    heads = raw_ref.shape[0]
    width = rows_ref.shape[1] // heads
    states = shared_ref.shape[1] // 2
    places = out_ref.shape[0]
    part = heads * width // places
    pre, sig = conv_pre(rows_ref, before_ref[:, : rows_ref.shape[1]], tapsx_ref, padh_ref)
    x = pre * sig
    before_s = before_ref[:, rows_ref.shape[1] :]
    pre_s, sig_s = conv_pre(shared_ref, before_s, tapsbc_ref, pads_ref)
    bc = (pre_s * sig_s).astype(BF16)
    _, step, _, _, _, cumulative = steps_of(raw_ref, gains_ref)
    length = step.shape[1]
    ending = cumulative[:, length - 1 :]
    spread = head_spread(heads, width)
    weight = dot(jnp.exp(ending - cumulative) * step, spread, 0, 0, True)
    grown = dot(jnp.exp(cumulative), spread, 0, 0, True)
    fresh = dot((x * weight).astype(BF16), bc[:, :states], 0, 0)
    pulls = dot((cot_ref[...].astype(F32) * grown).astype(BF16), bc[:, states:], 0, 0)
    out_ref[:, :part, :] = fresh.astype(BF16).reshape(places, part, states)
    out_ref[:, part : 2 * part, :] = pulls.astype(BF16).reshape(places, part, states)
    coarse = ending.astype(BF16).astype(F32)
    fine = ending - coarse
    per_head = places // heads
    mark = (16, states)
    for place in range(places):
        head = place // per_head
        marks = jnp.where(
            iota(mark, 0) == 0,
            jnp.broadcast_to(coarse[head : head + 1], mark),
            jnp.broadcast_to(fine[head : head + 1], mark),
        )
        out_ref[place, 2 * part :, :] = marks.astype(BF16)


def back_kernel(
    rows_ref, shared_ref, before_ref, raw_ref, gains_ref,
    tapsx_ref, tapsbc_ref, cot_ref, got_ref,
    main_ref, tail_ref, rim_ref, bc_ref, raw_out_ref, taps_out_ref, rate_out_ref,
    padh_ref, pads_ref, dv_ref, sums_ref,
):
    heads, length = raw_ref.shape
    width = rows_ref.shape[1] // heads
    states = shared_ref.shape[1] // 2
    part = got_ref.shape[1] // 2
    pre, sig = conv_pre(rows_ref, before_ref[:, : rows_ref.shape[1]], tapsx_ref, padh_ref)
    x = pre * sig
    before_s = before_ref[:, rows_ref.shape[1] :]
    pre_s, sig_s = conv_pre(shared_ref, before_s, tapsbc_ref, pads_ref)
    bc = (pre_s * sig_s).astype(BF16)
    b_rows, c_rows = bc[:, :states], bc[:, states:]
    shifted, step, rate, log_decay, upto, cumulative = steps_of(raw_ref, gains_ref)
    ending = cumulative[:, length - 1 :]
    spread = head_spread(heads, width)
    weight = dot(jnp.exp(ending - cumulative) * step, spread, 0, 0, True)
    grown = dot(jnp.exp(cumulative), spread, 0, 0, True)
    step_cols = dot(step, spread, 0, 0, True)
    skip_cols = jnp.sum(gain_column(gains_ref, 2) * spread, axis=0, keepdims=True)
    state_in = got_ref[:, :part, :].reshape(heads * width, states)
    pull_out = got_ref[:, part:, :].reshape(heads * width, states)
    cot = cot_ref[...]
    cot_wide = cot.astype(F32)
    b_pull = dot(b_rows, pull_out, 1, 1)
    c_state = dot(c_rows, state_in, 1, 1)
    cot_grown = cot_wide * grown
    x_weight = x * weight
    grad_c = dot(cot_grown.astype(BF16), state_in, 1, 0)
    grad_b = dot(x_weight.astype(BF16), pull_out, 1, 0)
    lane = (heads * width, 128)
    lane_of, head_of = iota(lane, 1), iota(lane, 0) // width
    pick = jnp.where((lane_of == head_of) | (lane_of == 2 * heads + head_of), 1.0, 0.0)
    pick_next = jnp.where(lane_of == heads + head_of, 1.0, 0.0)
    columns = dot(x_weight * b_pull, pick, 1, 0, True)
    columns = columns + dot(cot_grown * c_state, pick_next, 1, 0, True)
    scores = dot(b_rows, c_rows, 1, 1)
    square = (length, length)
    earlier = iota(square, 0) <= iota(square, 1)
    cumulative_cols = dot(upto, log_decay, 0, 1, True)
    x_step = (x * step_cols).astype(BF16)
    pair = max(1, 128 // width)
    block = pair * width
    lane_head = iota((length, block), 1) // width
    column_lane = iota((length, 128), 1)
    grad_scores = jnp.zeros(square, F32)
    inner = []
    for base in range(0, heads, pair):
        at = base * width
        x_pair = x_step[:, at : at + block]
        cot_pair = cot[:, at : at + block]
        sum_pair = None
        for i in range(pair):
            head = base + i
            cot_one = jnp.where(lane_head == i, cot_pair, jnp.zeros((), BF16))
            grad_mix = dot(x_pair, cot_one, 1, 1)
            gap = cumulative[head : head + 1, :] - cumulative_cols[:, head : head + 1]
            decay = jnp.exp(jnp.where(earlier, gap, -1e30))
            mix = decay * scores
            grad_scores = grad_scores + decay * grad_mix
            moved = mix * grad_mix
            sums_ref[head : head + 1, :] = jnp.sum(moved, axis=0, keepdims=True)
            columns = columns + jnp.where(
                column_lane == head, jnp.sum(moved, axis=1, keepdims=True), 0.0
            )
            term = dot(mix.astype(BF16), cot_one, 1, 0)
            sum_pair = term if sum_pair is None else sum_pair + term
        inner.append(sum_pair)
    inner = jnp.concatenate(inner, axis=1)
    grad_scores = grad_scores.astype(BF16)
    grad_b = grad_b + dot(grad_scores, c_rows, 1, 0)
    grad_c = grad_c + dot(grad_scores, b_rows, 0, 0)
    grad_bc = jnp.concatenate([grad_b, grad_c], axis=1).astype(BF16)
    for copy in range(bc_ref.shape[0]):
        bc_ref[copy] = grad_bc
    turned = columns.T
    left = turned[:heads]
    came = sums_ref[...] + turned[heads : 2 * heads]
    state_pull = state_in.astype(F32) * pull_out.astype(F32)
    state_pull = jnp.sum(state_pull.reshape(heads, width, states), axis=1)
    state_pull = jnp.exp(ending) * jnp.sum(state_pull, axis=1, keepdims=True)
    to_last = jnp.sum(turned[2 * heads : 3 * heads], axis=1, keepdims=True)
    grad_decay = dot(came - left, upto, 1, 1, True) + to_last + state_pull
    grad_step = left / step - rate * grad_decay
    raw_out_ref[...] = grad_step * jax.nn.sigmoid(shifted)
    grad_rate = jnp.sum(grad_decay * log_decay, axis=1, keepdims=True)
    eye = jnp.where(iota((heads, 128), 0) == iota((heads, 128), 1), 1.0, 0.0)
    rate_out_ref[...] = jnp.sum(grad_rate * eye, axis=0, keepdims=True)
    grad_x = inner * step_cols + skip_cols * cot_wide + weight * b_pull
    grad_pre = grad_x * (sig * (1.0 + pre * (1.0 - sig)))
    rows, rim, sums = conv_pull(grad_pre, tapsx_ref, padh_ref, dv_ref)
    main_ref[...] = rows.astype(BF16)
    tail_ref[...] = rows[length - 16 :]
    rim_ref[...] = rim
    for k, total in enumerate(sums):
        taps_out_ref[k : k + 1, :] = total


def shared_kernel(
    shared_ref, before_ref, tapsbc_ref, got_ref,
    main_ref, tail_ref, rim_ref, taps_out_ref, pads_ref, dv_ref,
):
    length = shared_ref.shape[0]
    before = before_ref[:, before_ref.shape[1] - shared_ref.shape[1] :]
    pre, sig = conv_pre(shared_ref, before, tapsbc_ref, pads_ref)
    total = got_ref[0].astype(F32)
    for source in range(1, got_ref.shape[0]):
        total = total + got_ref[source].astype(F32)
    grad_pre = total * (sig * (1.0 + pre * (1.0 - sig)))
    rows, rim, sums = conv_pull(grad_pre, tapsbc_ref, pads_ref, dv_ref)
    main_ref[...] = rows.astype(BF16)
    tail_ref[...] = rows[length - 16 :]
    rim_ref[...] = rim
    for k, value in enumerate(sums):
        taps_out_ref[k : k + 1, :] = value


FAR = 5
CENTRE = (-FAR, 0, FAR)
OPPOSITE = 8


def shifted_by(distance):
    return tuple(distance + step for step in CENTRE)


def rows_of(cot_ref, block, rows):
    per_group = (cot_ref.shape[1] - 16) // rows
    start = pl.multiple_of((block % per_group) * rows, rows)
    return cot_ref[block // per_group, pl.ds(start, rows), :]


def unscaled_kernel(place_ref, cot_ref, down_ref, *refs):
    out_refs, rows_ref = refs[:-1], refs[-1]
    places = rows_ref.shape[0] // out_refs[-1].shape[0]
    rows = out_refs[-1].shape[0]
    place = place_ref[0]
    at = 0
    for distances in (shifted_by(-2), shifted_by(2), shifted_by(-1), shifted_by(1), CENTRE, (OPPOSITE,)):
        for distance in distances:
            block = lax.rem(place + distance + places, places)
            rows_ref[at : at + rows, :] = rows_of(cot_ref, block, rows)
            at += rows
    product = dot(rows_ref[...], down_ref[...], 1, 1).astype(BF16)
    at = 0
    for out_ref in out_refs:
        out_ref[...] = product[at : at + out_ref.shape[0]]
        at += out_ref.shape[0]


def scaled_rows(cot_ref, group):
    slots = cot_ref.shape[1] - 16
    weight = cot_ref[group, slots:, :slots].astype(F32).T[:, 0:1]
    return weight, (cot_ref[group, :slots, :].astype(F32) * weight).astype(BF16)


def down_kernel(acts_ref, cot_ref, parts_ref):
    width = acts_ref.shape[1] // 2
    gate = acts_ref[:, :width].astype(F32)
    up = acts_ref[:, width:].astype(F32)
    hidden = (gate * jax.nn.sigmoid(gate) * up).astype(BF16)
    groups = cot_ref.shape[0]
    scaled = jnp.concatenate([scaled_rows(cot_ref, group)[1] for group in range(groups)], axis=0)
    parts_ref[...] = dot(hidden, scaled, 0, 0).astype(BF16).reshape(parts_ref.shape)


def rows_kernel(
    place_ref, centre_ref, left1_ref, right1_ref, left2_ref, right2_ref, opposite_ref,
    acts_ref, in_ref, cot_ref, gatew_ref, upw_ref, *refs,
):
    back_ref, parts_ref, all_ref, gate_ref, up_ref = refs[-5:]
    groups, slots, cols = in_ref.shape
    total, width = all_ref.shape
    owners = parts_ref.shape[0]
    share = parts_ref.shape[1] // 2
    rows = opposite_ref.shape[0]
    places = total // rows
    place = place_ref[0]
    pieces = (
        (centre_ref, 0), (left1_ref, -1), (right1_ref, 1), (left2_ref, -2), (right2_ref, 2)
    )
    for piece_ref, distance in pieces:
        for i, step in enumerate(shifted_by(distance)):
            block = lax.rem(place + step + places, places)
            start = pl.multiple_of(block * rows, rows)
            all_ref[pl.ds(start, rows), :] = piece_ref[i * rows : (i + 1) * rows, :]
    block = lax.rem(place + OPPOSITE, places)
    all_ref[pl.ds(pl.multiple_of(block * rows, rows), rows), :] = opposite_ref[...]
    for group in range(groups):
        span = slice(group * slots, (group + 1) * slots)
        unscaled = all_ref[span, :].astype(F32)
        gate = acts_ref[span, :width].astype(F32)
        up = acts_ref[span, width:].astype(F32)
        weight = cot_ref[group, slots:, :slots].astype(F32).T[:, 0:1]
        sig = jax.nn.sigmoid(gate)
        activated = gate * sig
        hidden = (activated * up).astype(BF16).astype(F32)
        grad_hidden = weight * unscaled
        slope = sig * (1.0 + gate * (1.0 - sig))
        gate_ref[span, :] = (grad_hidden * up * slope).astype(BF16)
        up_ref[span, :] = (grad_hidden * activated).astype(BF16)
        route = jnp.sum(hidden * unscaled, axis=1, keepdims=True)
        line = jnp.broadcast_to(route, (slots, 128)).T[0:1]
        coarse = line.astype(BF16).astype(F32)
        line = jnp.concatenate([coarse, line - coarse], axis=1)
        back_ref[group, slots:, :] = jnp.broadcast_to(line, (16, cols)).astype(BF16)
    rows_grad = dot(gate_ref[...], gatew_ref[...], 1, 1) + dot(up_ref[...], upw_ref[...], 1, 1)
    back_ref[:, :slots, :] = rows_grad.astype(BF16).reshape(groups, slots, cols)
    rows_in = in_ref[...].reshape(total, cols)
    parts_ref[:, :share, :] = (
        dot(gate_ref[...], rows_in, 0, 0).astype(BF16).reshape(owners, share, cols)
    )
    parts_ref[:, share:, :] = (
        dot(up_ref[...], rows_in, 0, 0).astype(BF16).reshape(owners, share, cols)
    )


def scan_kernel(got_ref, out_ref):
    places, half = got_ref.shape[0], out_ref.shape[1] // 2
    width = got_ref.shape[2]
    decay = [
        jnp.exp(
            got_ref[j, 2 * half : 2 * half + 1, :].astype(F32)
            + got_ref[j, 2 * half + 1 : 2 * half + 2, :].astype(F32)
        )
        for j in range(places)
    ]
    state = jnp.zeros((half, width), F32)
    for j in range(places):
        out_ref[j, :half, :] = state.astype(BF16)
        state = decay[j] * state + got_ref[j, :half, :].astype(F32)
    state = jnp.zeros((half, width), F32)
    for j in reversed(range(places)):
        out_ref[j, half:, :] = state.astype(BF16)
        state = decay[j] * state + got_ref[j, half : 2 * half, :].astype(F32)


def whole(kernel, outs, scratch=(), inputs=0, scalars=0, late=0, limit=None):
    specs = [pl.BlockSpec(memory_space=pltpu.SMEM)] * scalars
    specs += [pl.BlockSpec(memory_space=pltpu.VMEM)] * inputs
    specs += [pl.BlockSpec(memory_space=pl.ANY)] * late
    return pl.pallas_call(
        kernel,
        out_shape=[jax.ShapeDtypeStruct(shape, kind) for shape, kind in outs],
        in_specs=specs,
        out_specs=[pl.BlockSpec(memory_space=pltpu.VMEM)] * len(outs),
        scratch_shapes=[pltpu.VMEM(shape, kind) for shape, kind in scratch],
        compiler_params=pltpu.CompilerParams(vmem_limit_bytes=limit),
    )


def with_last_rows(main, tail, after):
    rows = tail.shape[0]
    given = jnp.pad(after, ((rows - after.shape[0], 0), (0, 0)))
    return lax.dynamic_update_slice(
        main, (tail + given).astype(BF16), (main.shape[0] - rows, 0)
    )


def body(
    mamba_in,
    shared_in,
    dt_raw,
    dt_bias,
    a_log,
    d_skip,
    conv_x,
    conv_bc,
    mamba_cot,
    moe_in,
    moe_cot,
    slot_tok,
    slot_count,
    route_w,
    w_gate,
    w_up,
    w_down,
    gate_act,
    up_act,
):
    dp_count, expert_places, ctx_places = (
        lax.axis_size("dp"),
        lax.axis_size("expert"),
        lax.axis_size("ctx"),
    )
    place = lax.axis_index("ctx").astype(jnp.int32).reshape(1)
    rim_rows = conv_x.shape[0] - 1
    head_rows = mamba_in[0]
    shared_rows = shared_in[0]
    cot_rows = mamba_cot[0]
    raw_step = dt_raw[0]
    length, split_at = head_rows.shape
    shared_width = shared_rows.shape[1]
    state_width = shared_width // 2
    heads_here = dt_bias.shape[0]
    part = split_at // ctx_places
    before = passed_along(
        jnp.concatenate([head_rows[length - rim_rows :], shared_rows[length - rim_rows :]], axis=1),
        "ctx",
        1,
    )
    acts = lax.all_gather(
        jnp.concatenate([gate_act[0, 0], up_act[0, 0]], axis=1), "ctx", axis=0, tiled=True
    )

    col_width = moe_in.shape[2]
    token_count = moe_in.shape[1]
    expert_count = slot_tok.shape[2]
    slot_width = slot_tok.shape[3]
    hidden_width = w_gate.shape[2]
    own = gate_act.shape[2]
    slot_ids = slot_tok[0, 0]
    live_slots = jnp.arange(slot_width, dtype=jnp.int32)[None, :] < slot_count[0, 0][:, None]
    chosen = jnp.where(live_slots, slot_ids, -1).reshape(-1)
    token_index = jnp.arange(token_count, dtype=jnp.int32)
    table = jnp.where(chosen[:, None] == token_index[None, :], 1.0, 0.0).astype(BF16)
    send_cot = jnp.dot(table, moe_cot[0], preferred_element_type=F32).astype(BF16)
    send_weight = jnp.where(live_slots, route_w[0, 0], jnp.zeros((), BF16))
    send_weight = jnp.pad(send_weight[:, None, :], ((0, 0), (0, 15), (0, col_width - slot_width)))
    send_cot = send_cot.reshape(expert_count, slot_width, col_width)
    got_cot = exchange(jnp.concatenate([send_cot, send_weight], axis=1), "expert")
    send_in = jnp.dot(table, moe_in[0], preferred_element_type=F32).astype(BF16)
    rows_in = exchange(send_in.reshape(expert_count, slot_width, col_width), "expert")

    gains = jnp.stack([dt_bias, a_log, d_skip])
    pad_heads = ((8 + length, split_at), F32)
    pad_shared = ((8 + length, shared_width), F32)
    (states,) = whole(
        front_kernel,
        [((ctx_places, 2 * part + 16, state_width), BF16)],
        [pad_heads, pad_shared],
        inputs=8,
    )(head_rows, shared_rows, before, raw_step, gains, conv_x, conv_bc, cot_rows)
    (entered,) = whole(
        scan_kernel, [((ctx_places, 2 * part, state_width), BF16)], inputs=1
    )(exchange(states, "ctx"))

    three, one = (3 * own, hidden_width), (own, hidden_width)
    left2, right2, left1, right1, centre, opposite = whole(
        unscaled_kernel,
        [(three, BF16)] * 5 + [(one, BF16)],
        [((ctx_places * own, col_width), BF16)],
        inputs=2,
        scalars=1,
    )(place, got_cot, w_down[0])
    opposite = shift(opposite, 3)
    left1 = (left1.astype(F32) + shift(left2, -1).astype(F32)).astype(BF16)
    right1 = (right1.astype(F32) + shift(right2, 1).astype(F32)).astype(BF16)
    centre = centre.astype(F32) + shift(left1, -1).astype(F32) + shift(right1, 1).astype(F32)
    far_left = shift(centre[:own].astype(BF16), -FAR)
    far_right = shift((centre[2 * own :] + opposite.astype(F32)).astype(BF16), FAR)
    mine = centre[own : 2 * own] + far_left.astype(F32) + far_right.astype(F32)
    mine = mine.astype(BF16)

    from_left, from_right = shift(mine, FAR), shift(mine, -FAR)
    opposite = shift(from_right, -3)
    centre = jnp.concatenate([from_left, mine, from_right], axis=0)
    left1, right1 = shift(centre, 1), shift(centre, -1)
    left2, right2 = shift(left1, 1), shift(right1, -1)

    main_heads, tail_heads, rim_heads, grad_bc, grad_step, taps_heads, grad_rate = whole(
        back_kernel,
        [
            ((length, split_at), BF16),
            ((16, split_at), F32),
            ((8, split_at), F32),
            ((expert_places, length, shared_width), BF16),
            ((heads_here, length), F32),
            ((rim_rows + 1, split_at), F32),
            ((1, 128), F32),
        ],
        [pad_heads, pad_shared, ((16 + length, split_at), F32), ((heads_here, length), F32)],
        inputs=9,
        limit=48 * 2**20,
    )(
        head_rows, shared_rows, before, raw_step, gains, conv_x, conv_bc, cot_rows,
        exchange(entered, "ctx"),
    )
    after_heads = passed_along(rim_heads[:rim_rows], "ctx", -1)
    grad_mamba_in = with_last_rows(main_heads, tail_heads, after_heads)
    main_shared, tail_shared, rim_shared, taps_shared = whole(
        shared_kernel,
        [
            ((length, shared_width), BF16),
            ((16, shared_width), F32),
            ((8, shared_width), F32),
            ((rim_rows + 1, shared_width), F32),
        ],
        [pad_shared, ((16 + length, shared_width), F32)],
        inputs=4,
    )(shared_rows, before, conv_bc, exchange(grad_bc, "expert"))
    after_shared = passed_along(rim_shared[:rim_rows], "ctx", -1)
    grad_shared_in = with_last_rows(main_shared, tail_shared, after_shared)
    small = jnp.concatenate(
        [
            taps_heads,
            taps_shared,
            jnp.broadcast_to(grad_rate, (dp_count, 128)),
            jnp.zeros((dp_count, 128), F32),
        ],
        axis=1,
    )
    small = jnp.sum(exchange(small.reshape(dp_count, 8, 128), "dp"), axis=0)
    small = jnp.sum(exchange(copies(small, ctx_places), "ctx"), axis=0).reshape(1, -1)
    taps_heads = small[:, :split_at]
    taps_shared = small[:, split_at : split_at + shared_width]
    rate_total = small[0, split_at + shared_width :][:heads_here]

    share = hidden_width // dp_count
    (down_parts,) = whole(
        down_kernel, [((dp_count, share, col_width), BF16)], inputs=2, limit=48 * 2**20
    )(acts, got_cot)
    down_total = jnp.sum(exchange(down_parts, "dp").astype(F32), axis=0).astype(BF16)
    all_rows = ((ctx_places * own, hidden_width), BF16)
    back, parts = whole(
        rows_kernel,
        [
            ((expert_count, slot_width + 16, col_width), BF16),
            ((dp_count, 2 * share, col_width), BF16),
        ],
        [all_rows] * 3,
        inputs=11,
        scalars=1,
        limit=56 * 2**20,
    )(
        place, centre, left1, right1, left2, right2, opposite, acts, rows_in, got_cot,
        w_gate[0], w_up[0],
    )
    back = exchange(back, "expert")
    parts = exchange(parts, "dp")
    grad_tokens = lax.dot_general(
        table,
        back[:, :slot_width].reshape(-1, col_width),
        (((0,), (0,)), ((), ())),
        preferred_element_type=F32,
    )
    route_got = back[:, slot_width].astype(F32)
    route_total = jnp.where(
        live_slots, route_got[:, :slot_width] + route_got[:, slot_width:], 0.0
    )
    totals = jnp.sum(parts.astype(F32), axis=0).astype(BF16)
    return (
        grad_mamba_in[None],
        grad_shared_in[None],
        grad_step[None],
        taps_heads,
        taps_shared,
        rate_total,
        grad_tokens.astype(BF16)[None],
        route_total[None, None],
        totals[:share].T[None],
        totals[share:].T[None],
        down_total[None],
    )


def solution(mesh):
    placed = (
        P("dp", "ctx", "expert"),
        P("dp", "ctx", None),
        P("dp", "expert", "ctx"),
        P("expert"),
        P("expert"),
        P("expert"),
        P(None, "expert"),
        P(),
        P("dp", "ctx", "expert"),
        P("dp", "expert", "ctx"),
        P("dp", "expert", "ctx"),
        P("dp", "expert", None, None),
        P("dp", "expert", None),
        P("dp", "expert", None, None),
        P("expert", "ctx", None),
        P("expert", "ctx", None),
        P("expert", None, "ctx"),
        P("dp", "expert", "ctx", None),
        P("dp", "expert", "ctx", None),
    )
    return jax.shard_map(
        body,
        mesh=mesh,
        in_specs=placed,
        out_specs=(
            P("dp", "ctx", "expert"),
            P("dp", "ctx", None),
            P("dp", "expert", "ctx"),
            P("dp", "expert"),
            P("dp", None),
            P("expert"),
            P("dp", "expert", "ctx"),
            P("dp", "expert", None, None),
            P("expert", "ctx", "dp"),
            P("expert", "ctx", "dp"),
            P("expert", "dp", "ctx"),
        ),
        check_vma=False,
    )
```

```python
import jax
import jax.numpy as jnp
from jax import lax
from jax.experimental import pallas as pl
from jax.experimental.pallas import tpu as pltpu
from jax.sharding import PartitionSpec as P

PRECISE = lax.Precision.HIGHEST
F32 = jnp.float32
BF16 = jnp.bfloat16


def passed_along(value, axis, steps):
    count = lax.axis_size(axis)
    first, last = (max(0, -steps), min(count, count - steps))
    return lax.ppermute(value, axis, [(source, source + steps) for source in range(first, last)])


def exchange(value, axis):
    return lax.all_to_all(value, axis, split_axis=0, concat_axis=0, tiled=True)


def shift(value, distance):
    count = lax.axis_size("ctx")
    return lax.ppermute(value, "ctx", [(i, (i + distance) % count) for i in range(count)])


def after(value, *earlier):
    return lax.optimization_barrier((value,) + earlier)[0]


def copies(value, count):
    return jnp.broadcast_to(value[None], (count,) + value.shape)


def dot(a, b, ca, cb, precise=False):
    return lax.dot_general(
        a,
        b,
        (((ca,), (cb,)), ((), ())),
        precision=PRECISE if precise else None,
        preferred_element_type=F32,
    )


def iota(shape, axis):
    return lax.broadcasted_iota(jnp.int32, shape, axis)


def conv_pre(rows_ref, before, taps_ref, pad_ref):
    length, width = rows_ref.shape
    taps = taps_ref.shape[0]
    pad_ref[0:8, :] = jnp.zeros((8, width), F32)
    pad_ref[8 - (taps - 1) : 8, :] = before.astype(F32)
    pad_ref[8:, :] = rows_ref[...].astype(F32)
    pre = None
    for k in range(taps):
        start = 8 - (taps - 1) + k
        term = taps_ref[k : k + 1, :] * pad_ref[start : start + length, :]
        pre = term if pre is None else pre + term
    sig = jax.nn.sigmoid(pre)
    return pre, sig


def conv_pull(grad_pre, taps_ref, pad_ref, dv_ref):
    length, width = grad_pre.shape
    taps = taps_ref.shape[0]
    dv_ref[0:8, :] = jnp.zeros((8, width), F32)
    dv_ref[8 : 8 + length, :] = grad_pre
    dv_ref[8 + length :, :] = jnp.zeros((8, width), F32)
    rows = None
    rim = None
    sums = []
    for k in range(taps):
        weight = taps_ref[k : k + 1, :]
        start = 8 + (taps - 1) - k
        term = weight * dv_ref[start : start + length, :]
        rows = term if rows is None else rows + term
        edge = weight * dv_ref[8 - k : 16 - k, :]
        rim = edge if rim is None else rim + edge
        start = 8 - (taps - 1) + k
        sums.append(jnp.sum(grad_pre * pad_ref[start : start + length, :], axis=0, keepdims=True))
    rim = jnp.where(iota(rim.shape, 0) < taps - 1, rim, 0.0)
    return rows, rim, sums


def gain_column(gains_ref, which):
    heads = gains_ref.shape[1]
    eye = iota((heads, heads), 0) == iota((heads, heads), 1)
    return jnp.sum(jnp.where(eye, gains_ref[which : which + 1, :], 0.0), axis=1, keepdims=True)


def steps_of(raw_ref, gains_ref):
    shifted = raw_ref[...] + gain_column(gains_ref, 0)
    step = jnp.maximum(shifted, 0.0) + jnp.log1p(jnp.exp(-jnp.abs(shifted)))
    rate = jnp.exp(gain_column(gains_ref, 1))
    log_decay = -rate * step
    length = shifted.shape[1]
    square = (length, length)
    upto = jnp.where(iota(square, 0) <= iota(square, 1), 1.0, 0.0)
    cumulative = dot(log_decay, upto, 1, 0, True)
    return shifted, step, rate, log_decay, upto, cumulative


def head_spread(heads, width):
    spread = (heads, heads * width)
    return jnp.where(iota(spread, 1) // width == iota(spread, 0), 1.0, 0.0)


def front_kernel(
    rows_ref, shared_ref, before_ref, raw_ref, gains_ref, tapsx_ref,
    tapsbc_ref, cot_ref, out_ref, padh_ref, pads_ref,
):
    heads = raw_ref.shape[0]
    width = rows_ref.shape[1] // heads
    states = shared_ref.shape[1] // 2
    places = out_ref.shape[0]
    part = heads * width // places
    pre, sig = conv_pre(rows_ref, before_ref[:, : rows_ref.shape[1]], tapsx_ref, padh_ref)
    x = pre * sig
    before_s = before_ref[:, rows_ref.shape[1] :]
    pre_s, sig_s = conv_pre(shared_ref, before_s, tapsbc_ref, pads_ref)
    bc = (pre_s * sig_s).astype(BF16)
    _, step, _, _, _, cumulative = steps_of(raw_ref, gains_ref)
    length = step.shape[1]
    ending = cumulative[:, length - 1 :]
    spread = head_spread(heads, width)
    weight = dot(jnp.exp(ending - cumulative) * step, spread, 0, 0, True)
    grown = dot(jnp.exp(cumulative), spread, 0, 0, True)
    fresh = dot((x * weight).astype(BF16), bc[:, :states], 0, 0)
    pulls = dot((cot_ref[...].astype(F32) * grown).astype(BF16), bc[:, states:], 0, 0)
    out_ref[:, :part, :] = fresh.astype(BF16).reshape(places, part, states)
    out_ref[:, part : 2 * part, :] = pulls.astype(BF16).reshape(places, part, states)
    coarse = ending.astype(BF16).astype(F32)
    fine = ending - coarse
    per_head = places // heads
    mark = (16, states)
    for place in range(places):
        head = place // per_head
        marks = jnp.where(
            iota(mark, 0) == 0,
            jnp.broadcast_to(coarse[head : head + 1], mark),
            jnp.broadcast_to(fine[head : head + 1], mark),
        )
        out_ref[place, 2 * part :, :] = marks.astype(BF16)


def back_kernel(
    rows_ref, shared_ref, before_ref, raw_ref, gains_ref,
    tapsx_ref, tapsbc_ref, cot_ref, got_ref,
    main_ref, tail_ref, rim_ref, bc_ref, raw_out_ref, taps_out_ref, rate_out_ref,
    padh_ref, pads_ref, dv_ref, sums_ref,
):
    heads, length = raw_ref.shape
    width = rows_ref.shape[1] // heads
    states = shared_ref.shape[1] // 2
    part = got_ref.shape[1] // 2
    pre, sig = conv_pre(rows_ref, before_ref[:, : rows_ref.shape[1]], tapsx_ref, padh_ref)
    x = pre * sig
    before_s = before_ref[:, rows_ref.shape[1] :]
    pre_s, sig_s = conv_pre(shared_ref, before_s, tapsbc_ref, pads_ref)
    bc = (pre_s * sig_s).astype(BF16)
    b_rows, c_rows = bc[:, :states], bc[:, states:]
    shifted, step, rate, log_decay, upto, cumulative = steps_of(raw_ref, gains_ref)
    ending = cumulative[:, length - 1 :]
    spread = head_spread(heads, width)
    weight = dot(jnp.exp(ending - cumulative) * step, spread, 0, 0, True)
    grown = dot(jnp.exp(cumulative), spread, 0, 0, True)
    step_cols = dot(step, spread, 0, 0, True)
    skip_cols = jnp.sum(gain_column(gains_ref, 2) * spread, axis=0, keepdims=True)
    state_in = got_ref[:, :part, :].reshape(heads * width, states)
    pull_out = got_ref[:, part:, :].reshape(heads * width, states)
    cot = cot_ref[...]
    cot_wide = cot.astype(F32)
    b_pull = dot(b_rows, pull_out, 1, 1)
    c_state = dot(c_rows, state_in, 1, 1)
    cot_grown = cot_wide * grown
    x_weight = x * weight
    grad_c = dot(cot_grown.astype(BF16), state_in, 1, 0)
    grad_b = dot(x_weight.astype(BF16), pull_out, 1, 0)
    lane = (heads * width, 128)
    lane_of, head_of = iota(lane, 1), iota(lane, 0) // width
    pick = jnp.where((lane_of == head_of) | (lane_of == 2 * heads + head_of), 1.0, 0.0)
    pick_next = jnp.where(lane_of == heads + head_of, 1.0, 0.0)
    columns = dot(x_weight * b_pull, pick, 1, 0, True)
    columns = columns + dot(cot_grown * c_state, pick_next, 1, 0, True)
    scores = dot(b_rows, c_rows, 1, 1)
    square = (length, length)
    earlier = iota(square, 0) <= iota(square, 1)
    cumulative_cols = dot(upto, log_decay, 0, 1, True)
    x_step = (x * step_cols).astype(BF16)
    pair = max(1, 128 // width)
    block = pair * width
    lane_head = iota((length, block), 1) // width
    column_lane = iota((length, 128), 1)
    grad_scores = jnp.zeros(square, F32)
    inner = []
    for base in range(0, heads, pair):
        at = base * width
        x_pair = x_step[:, at : at + block]
        cot_pair = cot[:, at : at + block]
        sum_pair = None
        for i in range(pair):
            head = base + i
            cot_one = jnp.where(lane_head == i, cot_pair, jnp.zeros((), BF16))
            grad_mix = dot(x_pair, cot_one, 1, 1)
            gap = cumulative[head : head + 1, :] - cumulative_cols[:, head : head + 1]
            decay = jnp.exp(jnp.where(earlier, gap, -1e30))
            mix = decay * scores
            grad_scores = grad_scores + decay * grad_mix
            moved = mix * grad_mix
            sums_ref[head : head + 1, :] = jnp.sum(moved, axis=0, keepdims=True)
            columns = columns + jnp.where(
                column_lane == head, jnp.sum(moved, axis=1, keepdims=True), 0.0
            )
            term = dot(mix.astype(BF16), cot_one, 1, 0)
            sum_pair = term if sum_pair is None else sum_pair + term
        inner.append(sum_pair)
    inner = jnp.concatenate(inner, axis=1)
    grad_scores = grad_scores.astype(BF16)
    grad_b = grad_b + dot(grad_scores, c_rows, 1, 0)
    grad_c = grad_c + dot(grad_scores, b_rows, 0, 0)
    grad_bc = jnp.concatenate([grad_b, grad_c], axis=1).astype(BF16)
    for copy in range(bc_ref.shape[0]):
        bc_ref[copy] = grad_bc
    turned = columns.T
    left = turned[:heads]
    came = sums_ref[...] + turned[heads : 2 * heads]
    state_pull = state_in.astype(F32) * pull_out.astype(F32)
    state_pull = jnp.sum(state_pull.reshape(heads, width, states), axis=1)
    state_pull = jnp.exp(ending) * jnp.sum(state_pull, axis=1, keepdims=True)
    to_last = jnp.sum(turned[2 * heads : 3 * heads], axis=1, keepdims=True)
    grad_decay = dot(came - left, upto, 1, 1, True) + to_last + state_pull
    grad_step = left / step - rate * grad_decay
    raw_out_ref[...] = grad_step * jax.nn.sigmoid(shifted)
    grad_rate = jnp.sum(grad_decay * log_decay, axis=1, keepdims=True)
    eye = jnp.where(iota((heads, 128), 0) == iota((heads, 128), 1), 1.0, 0.0)
    rate_out_ref[...] = jnp.sum(grad_rate * eye, axis=0, keepdims=True)
    grad_x = inner * step_cols + skip_cols * cot_wide + weight * b_pull
    grad_pre = grad_x * (sig * (1.0 + pre * (1.0 - sig)))
    rows, rim, sums = conv_pull(grad_pre, tapsx_ref, padh_ref, dv_ref)
    main_ref[...] = rows.astype(BF16)
    tail_ref[...] = rows[length - 16 :]
    rim_ref[...] = rim
    for k, total in enumerate(sums):
        taps_out_ref[k : k + 1, :] = total


def shared_kernel(
    shared_ref, before_ref, tapsbc_ref, got_ref,
    main_ref, tail_ref, rim_ref, taps_out_ref, pads_ref, dv_ref,
):
    length = shared_ref.shape[0]
    before = before_ref[:, before_ref.shape[1] - shared_ref.shape[1] :]
    pre, sig = conv_pre(shared_ref, before, tapsbc_ref, pads_ref)
    total = got_ref[0].astype(F32)
    for source in range(1, got_ref.shape[0]):
        total = total + got_ref[source].astype(F32)
    grad_pre = total * (sig * (1.0 + pre * (1.0 - sig)))
    rows, rim, sums = conv_pull(grad_pre, tapsbc_ref, pads_ref, dv_ref)
    main_ref[...] = rows.astype(BF16)
    tail_ref[...] = rows[length - 16 :]
    rim_ref[...] = rim
    for k, value in enumerate(sums):
        taps_out_ref[k : k + 1, :] = value


FAR = 5
CENTRE = (-FAR, 0, FAR)
OPPOSITE = 8


def shifted_by(distance):
    return tuple(distance + step for step in CENTRE)


def rows_of(cot_ref, block, rows):
    per_group = (cot_ref.shape[1] - 16) // rows
    start = pl.multiple_of((block % per_group) * rows, rows)
    return cot_ref[block // per_group, pl.ds(start, rows), :]


def unscaled_kernel(place_ref, cot_ref, down_ref, earlier_ref, *refs):
    del earlier_ref
    out_refs, rows_ref = refs[:-1], refs[-1]
    places = rows_ref.shape[0] // out_refs[-1].shape[0]
    rows = out_refs[-1].shape[0]
    place = place_ref[0]
    at = 0
    for distances in (shifted_by(-2), shifted_by(2), shifted_by(-1), shifted_by(1), CENTRE, (OPPOSITE,)):
        for distance in distances:
            block = lax.rem(place + distance + places, places)
            rows_ref[at : at + rows, :] = rows_of(cot_ref, block, rows)
            at += rows
    product = dot(rows_ref[...], down_ref[...], 1, 1).astype(BF16)
    at = 0
    for out_ref in out_refs:
        out_ref[...] = product[at : at + out_ref.shape[0]]
        at += out_ref.shape[0]


def scaled_rows(cot_ref, group):
    slots = cot_ref.shape[1] - 16
    weight = cot_ref[group, slots:, :slots].astype(F32).T[:, 0:1]
    return (cot_ref[group, :slots, :].astype(F32) * weight).astype(BF16)


def own_rows_kernel(mine_ref, weight_ref, gate_ref, up_ref, earlier_ref, out_ref):
    del earlier_ref
    width = mine_ref.shape[1]
    unscaled = mine_ref[...].astype(F32)
    gate = gate_ref[...].astype(F32)
    up = up_ref[...].astype(F32)
    grad_hidden = weight_ref[...] * unscaled
    sig = jax.nn.sigmoid(gate)
    activated = gate * sig
    hidden = (activated * up).astype(BF16)
    slope = sig * (1.0 + gate * (1.0 - sig))
    out_ref[:, :width] = (grad_hidden * up * slope).astype(BF16)
    out_ref[:, width : 2 * width] = (grad_hidden * activated).astype(BF16)
    out_ref[:, 2 * width : 3 * width] = hidden
    route = jnp.sum(hidden.astype(F32) * unscaled, axis=1, keepdims=True)
    coarse = route.astype(BF16).astype(F32)
    lanes = (mine_ref.shape[0], 128)
    out_ref[:, 3 * width :] = jnp.where(
        iota(lanes, 1) == 0, coarse, jnp.where(iota(lanes, 1) == 1, route - coarse, 0.0)
    ).astype(BF16)


def weights_kernel(place_ref, all_ref, in_ref, cot_ref, small_ref, *refs):
    out_refs, grads_ref = refs[:-1], refs[-1]
    groups, slots, cols = in_ref.shape
    width = grads_ref.shape[1]
    owners = len(out_refs)
    share = width // owners
    rows_in = in_ref[...].reshape(groups * slots, cols)
    scaled = jnp.concatenate([scaled_rows(cot_ref, group) for group in range(groups)], axis=0)
    grads_ref[0] = dot(all_ref[:, :width], rows_in, 0, 0).astype(BF16)
    grads_ref[1] = dot(all_ref[:, width : 2 * width], rows_in, 0, 0).astype(BF16)
    grads_ref[2] = dot(all_ref[:, 2 * width : 3 * width], scaled, 0, 0).astype(BF16)
    for ahead in range(owners):
        owner = lax.rem(place_ref[0] + ahead, owners)
        start = pl.multiple_of(owner * share, 64)
        for kind in range(3):
            out_refs[ahead][kind * share : (kind + 1) * share, :] = grads_ref[
                kind, pl.ds(start, share), :
            ]
        line = small_ref[pl.ds(owner, 1), :]
        coarse = line.astype(BF16).astype(F32)
        fine = line - coarse
        lines = [
            value[:, i * cols : (i + 1) * cols] for value in (coarse, fine) for i in range(4)
        ]
        lines.append(jnp.zeros((8, cols), F32))
        out_refs[ahead][3 * share :, :] = jnp.concatenate(lines, axis=0).astype(BF16)


def rows_kernel(all_ref, gatew_ref, upw_ref, back_ref):
    width = gatew_ref.shape[1]
    groups, slots, cols = back_ref.shape
    slots = slots - 16
    rows_grad = dot(all_ref[:, :width], gatew_ref[...], 1, 1)
    rows_grad = rows_grad + dot(all_ref[:, width : 2 * width], upw_ref[...], 1, 1)
    back_ref[:, :slots, :] = rows_grad.astype(BF16).reshape(groups, slots, cols)
    route = all_ref[:, 3 * width :].astype(F32)
    for group in range(groups):
        turned = route[group * slots : (group + 1) * slots].T
        line = jnp.concatenate([turned[0:1], turned[1:2]], axis=1)
        back_ref[group, slots:, :] = jnp.broadcast_to(line, (16, cols)).astype(BF16)


def totals_kernel(*refs):
    part_refs, (gate_ref, up_ref, down_ref, small_ref) = refs[:-4], refs[-4:]
    share = down_ref.shape[0]

    def total(first, last):
        value = part_refs[0][first:last, :].astype(F32)
        for part_ref in part_refs[1:]:
            value = value + part_ref[first:last, :].astype(F32)
        return value

    gate_ref[...] = total(0, share).T.astype(BF16)
    up_ref[...] = total(share, 2 * share).T.astype(BF16)
    down_ref[...] = total(2 * share, 3 * share).astype(BF16)
    small = total(3 * share, 3 * share + 16)
    small_ref[...] = small[:4] + small[4:8]


def scan_kernel(got_ref, out_ref):
    places, half = got_ref.shape[0], out_ref.shape[1] // 2
    width = got_ref.shape[2]
    decay = [
        jnp.exp(
            got_ref[j, 2 * half : 2 * half + 1, :].astype(F32)
            + got_ref[j, 2 * half + 1 : 2 * half + 2, :].astype(F32)
        )
        for j in range(places)
    ]
    state = jnp.zeros((half, width), F32)
    for j in range(places):
        out_ref[j, :half, :] = state.astype(BF16)
        state = decay[j] * state + got_ref[j, :half, :].astype(F32)
    state = jnp.zeros((half, width), F32)
    for j in reversed(range(places)):
        out_ref[j, half:, :] = state.astype(BF16)
        state = decay[j] * state + got_ref[j, half : 2 * half, :].astype(F32)


def whole(kernel, outs, scratch=(), inputs=0, scalars=0, late=0, limit=None):
    specs = [pl.BlockSpec(memory_space=pltpu.SMEM)] * scalars
    specs += [pl.BlockSpec(memory_space=pltpu.VMEM)] * inputs
    specs += [pl.BlockSpec(memory_space=pl.ANY)] * late
    return pl.pallas_call(
        kernel,
        out_shape=[jax.ShapeDtypeStruct(shape, kind) for shape, kind in outs],
        in_specs=specs,
        out_specs=[pl.BlockSpec(memory_space=pltpu.VMEM)] * len(outs),
        scratch_shapes=[pltpu.VMEM(shape, kind) for shape, kind in scratch],
        compiler_params=pltpu.CompilerParams(vmem_limit_bytes=limit),
    )


def with_last_rows(main, tail, after):
    rows = tail.shape[0]
    given = jnp.pad(after, ((rows - after.shape[0], 0), (0, 0)))
    return lax.dynamic_update_slice(
        main, (tail + given).astype(BF16), (main.shape[0] - rows, 0)
    )


def body(
    mamba_in,
    shared_in,
    dt_raw,
    dt_bias,
    a_log,
    d_skip,
    conv_x,
    conv_bc,
    mamba_cot,
    moe_in,
    moe_cot,
    slot_tok,
    slot_count,
    route_w,
    w_gate,
    w_up,
    w_down,
    gate_act,
    up_act,
):
    dp_count, expert_places, ctx_places = (
        lax.axis_size("dp"),
        lax.axis_size("expert"),
        lax.axis_size("ctx"),
    )
    place = lax.axis_index("ctx").astype(jnp.int32).reshape(1)
    rim_rows = conv_x.shape[0] - 1
    head_rows = mamba_in[0]
    shared_rows = shared_in[0]
    cot_rows = mamba_cot[0]
    raw_step = dt_raw[0]
    length, split_at = head_rows.shape
    shared_width = shared_rows.shape[1]
    state_width = shared_width // 2
    heads_here = dt_bias.shape[0]
    part = split_at // ctx_places
    before = passed_along(
        jnp.concatenate([head_rows[length - rim_rows :], shared_rows[length - rim_rows :]], axis=1),
        "ctx",
        1,
    )
    col_width = moe_in.shape[2]
    token_count = moe_in.shape[1]
    expert_count = slot_tok.shape[2]
    slot_width = slot_tok.shape[3]
    hidden_width = w_gate.shape[2]
    own = gate_act.shape[2]
    slot_ids = slot_tok[0, 0]
    live_slots = jnp.arange(slot_width, dtype=jnp.int32)[None, :] < slot_count[0, 0][:, None]
    chosen = jnp.where(live_slots, slot_ids, -1).reshape(-1)
    token_index = jnp.arange(token_count, dtype=jnp.int32)
    table = jnp.where(chosen[:, None] == token_index[None, :], 1.0, 0.0).astype(BF16)
    send_cot = jnp.dot(table, moe_cot[0], preferred_element_type=F32).astype(BF16)
    send_weight = jnp.where(live_slots, route_w[0, 0], jnp.zeros((), BF16))
    send_weight = jnp.pad(send_weight[:, None, :], ((0, 0), (0, 15), (0, col_width - slot_width)))
    send_cot = send_cot.reshape(expert_count, slot_width, col_width)
    got_cot = exchange(jnp.concatenate([send_cot, send_weight], axis=1), "expert")
    send_in = jnp.dot(table, moe_in[0], preferred_element_type=F32).astype(BF16)
    rows_in = exchange(send_in.reshape(expert_count, slot_width, col_width), "expert")

    gains = jnp.stack([dt_bias, a_log, d_skip])
    pad_heads = ((8 + length, split_at), F32)
    pad_shared = ((8 + length, shared_width), F32)
    (states,) = whole(
        front_kernel,
        [((ctx_places, 2 * part + 16, state_width), BF16)],
        [pad_heads, pad_shared],
        inputs=8,
    )(head_rows, shared_rows, before, raw_step, gains, conv_x, conv_bc, cot_rows)
    (entered,) = whole(
        scan_kernel, [((ctx_places, 2 * part, state_width), BF16)], inputs=1
    )(exchange(after(states, got_cot), "ctx"))

    three, one = (3 * own, hidden_width), (own, hidden_width)
    left2, right2, left1, right1, centre, opposite = whole(
        unscaled_kernel,
        [(three, BF16)] * 5 + [(one, BF16)],
        [((ctx_places * own, col_width), BF16)],
        inputs=2,
        scalars=1,
        late=1,
    )(place, got_cot, w_down[0], states)
    opposite = shift(opposite, 3)
    left1 = (left1.astype(F32) + shift(left2, -1).astype(F32)).astype(BF16)
    right1 = (right1.astype(F32) + shift(right2, 1).astype(F32)).astype(BF16)
    centre = centre.astype(F32) + shift(left1, -1).astype(F32) + shift(right1, 1).astype(F32)
    far_left = shift(centre[:own].astype(BF16), -FAR)
    far_right = shift((centre[2 * own :] + opposite.astype(F32)).astype(BF16), FAR)
    mine = centre[own : 2 * own] + far_left.astype(F32) + far_right.astype(F32)
    rows_weight = got_cot[:, slot_width, :slot_width].reshape(-1).astype(F32)
    weight_own = lax.dynamic_slice_in_dim(rows_weight, place[0] * own, own, 0)
    (own_rows,) = whole(
        own_rows_kernel, [((own, 3 * hidden_width + 128), BF16)], inputs=4, late=1
    )(mine, weight_own[:, None], gate_act[0, 0], up_act[0, 0], entered)
    everything = lax.all_gather(own_rows, "ctx", axis=0, tiled=True)

    main_heads, tail_heads, rim_heads, grad_bc, grad_step, taps_heads, grad_rate = whole(
        back_kernel,
        [
            ((length, split_at), BF16),
            ((16, split_at), F32),
            ((8, split_at), F32),
            ((expert_places, length, shared_width), BF16),
            ((heads_here, length), F32),
            ((rim_rows + 1, split_at), F32),
            ((1, 128), F32),
        ],
        [pad_heads, pad_shared, ((16 + length, split_at), F32), ((heads_here, length), F32)],
        inputs=9,
        limit=48 * 2**20,
    )(
        head_rows, shared_rows, before, raw_step, gains, conv_x, conv_bc, cot_rows,
        exchange(entered, "ctx"),
    )
    after_heads = passed_along(rim_heads[:rim_rows], "ctx", -1)
    grad_mamba_in = with_last_rows(main_heads, tail_heads, after_heads)
    main_shared, tail_shared, rim_shared, taps_shared = whole(
        shared_kernel,
        [
            ((length, shared_width), BF16),
            ((16, shared_width), F32),
            ((8, shared_width), F32),
            ((rim_rows + 1, shared_width), F32),
        ],
        [pad_shared, ((16 + length, shared_width), F32)],
        inputs=4,
    )(shared_rows, before, conv_bc, exchange(grad_bc, "expert"))
    after_shared = passed_along(rim_shared[:rim_rows], "ctx", -1)
    grad_shared_in = with_last_rows(main_shared, tail_shared, after_shared)
    small = jnp.concatenate(
        [
            taps_heads,
            taps_shared,
            jnp.broadcast_to(grad_rate, (dp_count, 128)),
            jnp.zeros((dp_count, 128), F32),
        ],
        axis=1,
    )
    small = small.reshape(dp_count * 8, 128)
    small = jnp.sum(exchange(copies(small, ctx_places), "ctx"), axis=0).reshape(dp_count, -1)

    share = hidden_width // dp_count
    block = ((3 * share + 16, col_width), BF16)
    owner = lax.axis_index("dp").astype(jnp.int32).reshape(1)
    parts = whole(
        weights_kernel,
        [block] * dp_count,
        [((3, hidden_width, col_width), BF16)],
        inputs=4,
        scalars=1,
        limit=56 * 2**20,
    )(owner, everything, rows_in, got_cot, small)
    parts = [parts[0]] + [
        lax.ppermute(parts[k], "dp", [(i, (i + k) % dp_count) for i in range(dp_count)])
        for k in range(1, dp_count)
    ]
    (back,) = whole(
        rows_kernel,
        [((expert_count, slot_width + 16, col_width), BF16)],
        inputs=3,
        limit=48 * 2**20,
    )(everything, w_gate[0], w_up[0])
    back = exchange(back, "expert")
    gate_total, up_total, down_total, small = whole(
        totals_kernel,
        [
            ((col_width, share), BF16),
            ((col_width, share), BF16),
            ((share, col_width), BF16),
            ((4, col_width), F32),
        ],
        inputs=dp_count,
    )(*parts)
    small = small.reshape(1, -1)
    taps_heads = small[:, :split_at]
    taps_shared = small[:, split_at : split_at + shared_width]
    rate_total = small[0, split_at + shared_width :][:heads_here]
    grad_tokens = lax.dot_general(
        table,
        back[:, :slot_width].reshape(-1, col_width),
        (((0,), (0,)), ((), ())),
        preferred_element_type=F32,
    )
    route_got = back[:, slot_width].astype(F32)
    route_total = jnp.where(
        live_slots, route_got[:, :slot_width] + route_got[:, slot_width:], 0.0
    )
    return (
        grad_mamba_in[None],
        grad_shared_in[None],
        grad_step[None],
        taps_heads,
        taps_shared,
        rate_total,
        grad_tokens.astype(BF16)[None],
        route_total[None, None],
        gate_total[None],
        up_total[None],
        down_total[None],
    )


def solution(mesh):
    placed = (
        P("dp", "ctx", "expert"),
        P("dp", "ctx", None),
        P("dp", "expert", "ctx"),
        P("expert"),
        P("expert"),
        P("expert"),
        P(None, "expert"),
        P(),
        P("dp", "ctx", "expert"),
        P("dp", "expert", "ctx"),
        P("dp", "expert", "ctx"),
        P("dp", "expert", None, None),
        P("dp", "expert", None),
        P("dp", "expert", None, None),
        P("expert", "ctx", None),
        P("expert", "ctx", None),
        P("expert", None, "ctx"),
        P("dp", "expert", "ctx", None),
        P("dp", "expert", "ctx", None),
    )
    return jax.shard_map(
        body,
        mesh=mesh,
        in_specs=placed,
        out_specs=(
            P("dp", "ctx", "expert"),
            P("dp", "ctx", None),
            P("dp", "expert", "ctx"),
            P("dp", "expert"),
            P("dp", None),
            P("expert"),
            P("dp", "expert", "ctx"),
            P("dp", "expert", None, None),
            P("expert", "ctx", "dp"),
            P("expert", "ctx", "dp"),
            P("expert", "dp", "ctx"),
        ),
        check_vma=False,
    )
```

```python
import jax
import jax.numpy as jnp
from jax import lax
from jax.experimental import pallas as pl
from jax.experimental.pallas import tpu as pltpu
from jax.sharding import PartitionSpec as P

PRECISE = lax.Precision.HIGHEST
F32 = jnp.float32
BF16 = jnp.bfloat16


def passed_along(value, axis, steps):
    count = lax.axis_size(axis)
    first, last = (max(0, -steps), min(count, count - steps))
    return lax.ppermute(value, axis, [(source, source + steps) for source in range(first, last)])


def exchange(value, axis):
    return lax.all_to_all(value, axis, split_axis=0, concat_axis=0, tiled=True)


def shift(value, distance):
    count = lax.axis_size("ctx")
    return lax.ppermute(value, "ctx", [(i, (i + distance) % count) for i in range(count)])


def after(value, *earlier):
    return lax.optimization_barrier((value,) + earlier)[0]


def copies(value, count):
    return jnp.broadcast_to(value[None], (count,) + value.shape)


def dot(a, b, ca, cb, precise=False):
    return lax.dot_general(
        a,
        b,
        (((ca,), (cb,)), ((), ())),
        precision=PRECISE if precise else None,
        preferred_element_type=F32,
    )


def iota(shape, axis):
    return lax.broadcasted_iota(jnp.int32, shape, axis)


def conv_pre(rows_ref, before, taps_ref, pad_ref):
    length, width = rows_ref.shape
    taps = taps_ref.shape[0]
    pad_ref[0:8, :] = jnp.zeros((8, width), F32)
    pad_ref[8 - (taps - 1) : 8, :] = before.astype(F32)
    pad_ref[8:, :] = rows_ref[...].astype(F32)
    pre = None
    for k in range(taps):
        start = 8 - (taps - 1) + k
        term = taps_ref[k : k + 1, :] * pad_ref[start : start + length, :]
        pre = term if pre is None else pre + term
    sig = jax.nn.sigmoid(pre)
    return pre, sig


def conv_pull(grad_pre, taps_ref, pad_ref, dv_ref):
    length, width = grad_pre.shape
    taps = taps_ref.shape[0]
    dv_ref[0:8, :] = jnp.zeros((8, width), F32)
    dv_ref[8 : 8 + length, :] = grad_pre
    dv_ref[8 + length :, :] = jnp.zeros((8, width), F32)
    rows = None
    rim = None
    sums = []
    for k in range(taps):
        weight = taps_ref[k : k + 1, :]
        start = 8 + (taps - 1) - k
        term = weight * dv_ref[start : start + length, :]
        rows = term if rows is None else rows + term
        edge = weight * dv_ref[8 - k : 16 - k, :]
        rim = edge if rim is None else rim + edge
        start = 8 - (taps - 1) + k
        sums.append(jnp.sum(grad_pre * pad_ref[start : start + length, :], axis=0, keepdims=True))
    rim = jnp.where(iota(rim.shape, 0) < taps - 1, rim, 0.0)
    return rows, rim, sums


def gain_column(gains_ref, which):
    heads = gains_ref.shape[1]
    eye = iota((heads, heads), 0) == iota((heads, heads), 1)
    return jnp.sum(jnp.where(eye, gains_ref[which : which + 1, :], 0.0), axis=1, keepdims=True)


def steps_of(raw_ref, gains_ref):
    shifted = raw_ref[...] + gain_column(gains_ref, 0)
    step = jnp.maximum(shifted, 0.0) + jnp.log1p(jnp.exp(-jnp.abs(shifted)))
    rate = jnp.exp(gain_column(gains_ref, 1))
    log_decay = -rate * step
    length = shifted.shape[1]
    square = (length, length)
    upto = jnp.where(iota(square, 0) <= iota(square, 1), 1.0, 0.0)
    cumulative = dot(log_decay, upto, 1, 0, True)
    return shifted, step, rate, log_decay, upto, cumulative


def head_spread(heads, width):
    spread = (heads, heads * width)
    return jnp.where(iota(spread, 1) // width == iota(spread, 0), 1.0, 0.0)


def front_kernel(
    rows_ref, shared_ref, before_ref, raw_ref, gains_ref, tapsx_ref,
    tapsbc_ref, cot_ref, out_ref, padh_ref, pads_ref,
):
    heads = raw_ref.shape[0]
    width = rows_ref.shape[1] // heads
    states = shared_ref.shape[1] // 2
    places = out_ref.shape[0]
    part = heads * width // places
    pre, sig = conv_pre(rows_ref, before_ref[:, : rows_ref.shape[1]], tapsx_ref, padh_ref)
    x = pre * sig
    before_s = before_ref[:, rows_ref.shape[1] :]
    pre_s, sig_s = conv_pre(shared_ref, before_s, tapsbc_ref, pads_ref)
    bc = (pre_s * sig_s).astype(BF16)
    _, step, _, _, _, cumulative = steps_of(raw_ref, gains_ref)
    length = step.shape[1]
    ending = cumulative[:, length - 1 :]
    spread = head_spread(heads, width)
    weight = dot(jnp.exp(ending - cumulative) * step, spread, 0, 0, True)
    grown = dot(jnp.exp(cumulative), spread, 0, 0, True)
    fresh = dot((x * weight).astype(BF16), bc[:, :states], 0, 0)
    pulls = dot((cot_ref[...].astype(F32) * grown).astype(BF16), bc[:, states:], 0, 0)
    out_ref[:, :part, :] = fresh.astype(BF16).reshape(places, part, states)
    out_ref[:, part : 2 * part, :] = pulls.astype(BF16).reshape(places, part, states)
    coarse = ending.astype(BF16).astype(F32)
    fine = ending - coarse
    per_head = places // heads
    mark = (16, states)
    for place in range(places):
        head = place // per_head
        marks = jnp.where(
            iota(mark, 0) == 0,
            jnp.broadcast_to(coarse[head : head + 1], mark),
            jnp.broadcast_to(fine[head : head + 1], mark),
        )
        out_ref[place, 2 * part :, :] = marks.astype(BF16)


def back_kernel(
    rows_ref, shared_ref, before_ref, raw_ref, gains_ref,
    tapsx_ref, tapsbc_ref, cot_ref, got_ref,
    main_ref, tail_ref, rim_ref, bc_ref, raw_out_ref, taps_out_ref, rate_out_ref,
    padh_ref, pads_ref, dv_ref, sums_ref,
):
    heads, length = raw_ref.shape
    width = rows_ref.shape[1] // heads
    states = shared_ref.shape[1] // 2
    part = got_ref.shape[1] // 2
    pre, sig = conv_pre(rows_ref, before_ref[:, : rows_ref.shape[1]], tapsx_ref, padh_ref)
    x = pre * sig
    before_s = before_ref[:, rows_ref.shape[1] :]
    pre_s, sig_s = conv_pre(shared_ref, before_s, tapsbc_ref, pads_ref)
    bc = (pre_s * sig_s).astype(BF16)
    b_rows, c_rows = bc[:, :states], bc[:, states:]
    shifted, step, rate, log_decay, upto, cumulative = steps_of(raw_ref, gains_ref)
    ending = cumulative[:, length - 1 :]
    spread = head_spread(heads, width)
    weight = dot(jnp.exp(ending - cumulative) * step, spread, 0, 0, True)
    grown = dot(jnp.exp(cumulative), spread, 0, 0, True)
    step_cols = dot(step, spread, 0, 0, True)
    skip_cols = jnp.sum(gain_column(gains_ref, 2) * spread, axis=0, keepdims=True)
    state_in = got_ref[:, :part, :].reshape(heads * width, states)
    pull_out = got_ref[:, part:, :].reshape(heads * width, states)
    cot = cot_ref[...]
    cot_wide = cot.astype(F32)
    b_pull = dot(b_rows, pull_out, 1, 1)
    c_state = dot(c_rows, state_in, 1, 1)
    cot_grown = cot_wide * grown
    x_weight = x * weight
    grad_c = dot(cot_grown.astype(BF16), state_in, 1, 0)
    grad_b = dot(x_weight.astype(BF16), pull_out, 1, 0)
    lane = (heads * width, 128)
    lane_of, head_of = iota(lane, 1), iota(lane, 0) // width
    pick = jnp.where((lane_of == head_of) | (lane_of == 2 * heads + head_of), 1.0, 0.0)
    pick_next = jnp.where(lane_of == heads + head_of, 1.0, 0.0)
    columns = dot(x_weight * b_pull, pick, 1, 0, True)
    columns = columns + dot(cot_grown * c_state, pick_next, 1, 0, True)
    scores = dot(b_rows, c_rows, 1, 1)
    square = (length, length)
    earlier = iota(square, 0) <= iota(square, 1)
    cumulative_cols = dot(upto, log_decay, 0, 1, True)
    x_step = (x * step_cols).astype(BF16)
    pair = max(1, 128 // width)
    block = pair * width
    lane_head = iota((length, block), 1) // width
    column_lane = iota((length, 128), 1)
    grad_scores = jnp.zeros(square, F32)
    inner = []
    for base in range(0, heads, pair):
        at = base * width
        x_pair = x_step[:, at : at + block]
        cot_pair = cot[:, at : at + block]
        sum_pair = None
        for i in range(pair):
            head = base + i
            cot_one = jnp.where(lane_head == i, cot_pair, jnp.zeros((), BF16))
            grad_mix = dot(x_pair, cot_one, 1, 1)
            gap = cumulative[head : head + 1, :] - cumulative_cols[:, head : head + 1]
            decay = jnp.exp(jnp.where(earlier, gap, -1e30))
            mix = decay * scores
            grad_scores = grad_scores + decay * grad_mix
            moved = mix * grad_mix
            sums_ref[head : head + 1, :] = jnp.sum(moved, axis=0, keepdims=True)
            columns = columns + jnp.where(
                column_lane == head, jnp.sum(moved, axis=1, keepdims=True), 0.0
            )
            term = dot(mix.astype(BF16), cot_one, 1, 0)
            sum_pair = term if sum_pair is None else sum_pair + term
        inner.append(sum_pair)
    inner = jnp.concatenate(inner, axis=1)
    grad_scores = grad_scores.astype(BF16)
    grad_b = grad_b + dot(grad_scores, c_rows, 1, 0)
    grad_c = grad_c + dot(grad_scores, b_rows, 0, 0)
    grad_bc = jnp.concatenate([grad_b, grad_c], axis=1).astype(BF16)
    for copy in range(bc_ref.shape[0]):
        bc_ref[copy] = grad_bc
    turned = columns.T
    left = turned[:heads]
    came = sums_ref[...] + turned[heads : 2 * heads]
    state_pull = state_in.astype(F32) * pull_out.astype(F32)
    state_pull = jnp.sum(state_pull.reshape(heads, width, states), axis=1)
    state_pull = jnp.exp(ending) * jnp.sum(state_pull, axis=1, keepdims=True)
    to_last = jnp.sum(turned[2 * heads : 3 * heads], axis=1, keepdims=True)
    grad_decay = dot(came - left, upto, 1, 1, True) + to_last + state_pull
    grad_step = left / step - rate * grad_decay
    raw_out_ref[...] = grad_step * jax.nn.sigmoid(shifted)
    grad_rate = jnp.sum(grad_decay * log_decay, axis=1, keepdims=True)
    eye = jnp.where(iota((heads, 128), 0) == iota((heads, 128), 1), 1.0, 0.0)
    rate_out_ref[...] = jnp.sum(grad_rate * eye, axis=0, keepdims=True)
    grad_x = inner * step_cols + skip_cols * cot_wide + weight * b_pull
    grad_pre = grad_x * (sig * (1.0 + pre * (1.0 - sig)))
    rows, rim, sums = conv_pull(grad_pre, tapsx_ref, padh_ref, dv_ref)
    main_ref[...] = rows.astype(BF16)
    tail_ref[...] = rows[length - 16 :]
    rim_ref[...] = rim
    for k, total in enumerate(sums):
        taps_out_ref[k : k + 1, :] = total


def shared_kernel(
    shared_ref, before_ref, tapsbc_ref, got_ref,
    main_ref, tail_ref, rim_ref, taps_out_ref, pads_ref, dv_ref,
):
    length = shared_ref.shape[0]
    before = before_ref[:, before_ref.shape[1] - shared_ref.shape[1] :]
    pre, sig = conv_pre(shared_ref, before, tapsbc_ref, pads_ref)
    total = got_ref[0].astype(F32)
    for source in range(1, got_ref.shape[0]):
        total = total + got_ref[source].astype(F32)
    grad_pre = total * (sig * (1.0 + pre * (1.0 - sig)))
    rows, rim, sums = conv_pull(grad_pre, tapsbc_ref, pads_ref, dv_ref)
    main_ref[...] = rows.astype(BF16)
    tail_ref[...] = rows[length - 16 :]
    rim_ref[...] = rim
    for k, value in enumerate(sums):
        taps_out_ref[k : k + 1, :] = value


FAR = 5
CENTRE = (-FAR, 0, FAR)
OPPOSITE = 8


def shifted_by(distance):
    return tuple(distance + step for step in CENTRE)


def rows_of(cot_ref, block, rows):
    per_group = (cot_ref.shape[1] - 16) // rows
    start = pl.multiple_of((block % per_group) * rows, rows)
    return cot_ref[block // per_group, pl.ds(start, rows), :]


def unscaled_kernel(place_ref, cot_ref, down_ref, earlier_ref, *refs):
    del earlier_ref
    out_refs, rows_ref = refs[:-1], refs[-1]
    places = rows_ref.shape[0] // out_refs[-1].shape[0]
    rows = out_refs[-1].shape[0]
    place = place_ref[0]
    at = 0
    for distances in (shifted_by(-2), shifted_by(2), shifted_by(-1), shifted_by(1), CENTRE, (OPPOSITE,)):
        for distance in distances:
            block = lax.rem(place + distance + places, places)
            rows_ref[at : at + rows, :] = rows_of(cot_ref, block, rows)
            at += rows
    product = dot(rows_ref[...], down_ref[...], 1, 1).astype(BF16)
    at = 0
    for out_ref in out_refs:
        out_ref[...] = product[at : at + out_ref.shape[0]]
        at += out_ref.shape[0]


def scaled_rows(cot_ref, group):
    slots = cot_ref.shape[1] - 16
    weight = cot_ref[group, slots:, :slots].astype(F32).T[:, 0:1]
    return (cot_ref[group, :slots, :].astype(F32) * weight).astype(BF16)


def own_rows_kernel(mine_ref, weight_ref, gate_ref, up_ref, earlier_ref, out_ref):
    del earlier_ref
    width = mine_ref.shape[1]
    unscaled = mine_ref[...].astype(F32)
    gate = gate_ref[...].astype(F32)
    up = up_ref[...].astype(F32)
    grad_hidden = weight_ref[...] * unscaled
    sig = jax.nn.sigmoid(gate)
    activated = gate * sig
    hidden = (activated * up).astype(BF16)
    slope = sig * (1.0 + gate * (1.0 - sig))
    out_ref[:, :width] = (grad_hidden * up * slope).astype(BF16)
    out_ref[:, width : 2 * width] = (grad_hidden * activated).astype(BF16)
    out_ref[:, 2 * width : 3 * width] = hidden
    route = jnp.sum(hidden.astype(F32) * unscaled, axis=1, keepdims=True)
    coarse = route.astype(BF16).astype(F32)
    lanes = (mine_ref.shape[0], 128)
    out_ref[:, 3 * width :] = jnp.where(
        iota(lanes, 1) == 0, coarse, jnp.where(iota(lanes, 1) == 1, route - coarse, 0.0)
    ).astype(BF16)


def weights_kernel(place_ref, all_ref, in_ref, cot_ref, *refs):
    out_refs, grads_ref = refs[:-1], refs[-1]
    groups, slots, cols = in_ref.shape
    width = grads_ref.shape[1]
    owners = len(out_refs)
    share = width // owners
    rows_in = in_ref[...].reshape(groups * slots, cols)
    scaled = jnp.concatenate([scaled_rows(cot_ref, group) for group in range(groups)], axis=0)
    grads_ref[0] = dot(all_ref[:, :width], rows_in, 0, 0).astype(BF16)
    grads_ref[1] = dot(all_ref[:, width : 2 * width], rows_in, 0, 0).astype(BF16)
    grads_ref[2] = dot(all_ref[:, 2 * width : 3 * width], scaled, 0, 0).astype(BF16)
    for ahead in range(owners):
        owner = lax.rem(place_ref[0] + ahead, owners)
        start = pl.multiple_of(owner * share, 64)
        for kind in range(3):
            out_refs[ahead][kind * share : (kind + 1) * share, :] = grads_ref[
                kind, pl.ds(start, share), :
            ]


def rows_kernel(all_ref, gatew_ref, upw_ref, back_ref):
    width = gatew_ref.shape[1]
    groups, slots, cols = back_ref.shape
    slots = slots - 16
    rows_grad = dot(all_ref[:, :width], gatew_ref[...], 1, 1)
    rows_grad = rows_grad + dot(all_ref[:, width : 2 * width], upw_ref[...], 1, 1)
    back_ref[:, :slots, :] = rows_grad.astype(BF16).reshape(groups, slots, cols)
    route = all_ref[:, 3 * width :].astype(F32)
    for group in range(groups):
        turned = route[group * slots : (group + 1) * slots].T
        line = jnp.concatenate([turned[0:1], turned[1:2]], axis=1)
        back_ref[group, slots:, :] = jnp.broadcast_to(line, (16, cols)).astype(BF16)


def totals_kernel(*refs):
    part_refs, out_refs = refs[:-3], refs[-3:]
    share = out_refs[0].shape[0]
    for kind, out_ref in enumerate(out_refs):
        span = slice(kind * share, (kind + 1) * share)
        value = part_refs[0][span, :].astype(F32)
        for part_ref in part_refs[1:]:
            value = value + part_ref[span, :].astype(F32)
        out_ref[...] = value.astype(BF16)


def scan_kernel(got_ref, out_ref):
    places, half = got_ref.shape[0], out_ref.shape[1] // 2
    width = got_ref.shape[2]
    decay = [
        jnp.exp(
            got_ref[j, 2 * half : 2 * half + 1, :].astype(F32)
            + got_ref[j, 2 * half + 1 : 2 * half + 2, :].astype(F32)
        )
        for j in range(places)
    ]
    state = jnp.zeros((half, width), F32)
    for j in range(places):
        out_ref[j, :half, :] = state.astype(BF16)
        state = decay[j] * state + got_ref[j, :half, :].astype(F32)
    state = jnp.zeros((half, width), F32)
    for j in reversed(range(places)):
        out_ref[j, half:, :] = state.astype(BF16)
        state = decay[j] * state + got_ref[j, half : 2 * half, :].astype(F32)


def whole(kernel, outs, scratch=(), inputs=0, scalars=0, late=0, limit=None):
    specs = [pl.BlockSpec(memory_space=pltpu.SMEM)] * scalars
    specs += [pl.BlockSpec(memory_space=pltpu.VMEM)] * inputs
    specs += [pl.BlockSpec(memory_space=pl.ANY)] * late
    return pl.pallas_call(
        kernel,
        out_shape=[jax.ShapeDtypeStruct(shape, kind) for shape, kind in outs],
        in_specs=specs,
        out_specs=[pl.BlockSpec(memory_space=pltpu.VMEM)] * len(outs),
        scratch_shapes=[pltpu.VMEM(shape, kind) for shape, kind in scratch],
        compiler_params=pltpu.CompilerParams(vmem_limit_bytes=limit),
    )


def with_last_rows(main, tail, after):
    rows = tail.shape[0]
    given = jnp.pad(after, ((rows - after.shape[0], 0), (0, 0)))
    return lax.dynamic_update_slice(
        main, (tail + given).astype(BF16), (main.shape[0] - rows, 0)
    )


def body(
    mamba_in,
    shared_in,
    dt_raw,
    dt_bias,
    a_log,
    d_skip,
    conv_x,
    conv_bc,
    mamba_cot,
    moe_in,
    moe_cot,
    slot_tok,
    slot_count,
    route_w,
    w_gate,
    w_up,
    w_down,
    gate_act,
    up_act,
):
    dp_count, expert_places, ctx_places = (
        lax.axis_size("dp"),
        lax.axis_size("expert"),
        lax.axis_size("ctx"),
    )
    place = lax.axis_index("ctx").astype(jnp.int32).reshape(1)
    rim_rows = conv_x.shape[0] - 1
    head_rows = mamba_in[0]
    shared_rows = shared_in[0]
    cot_rows = mamba_cot[0]
    raw_step = dt_raw[0]
    length, split_at = head_rows.shape
    shared_width = shared_rows.shape[1]
    state_width = shared_width // 2
    heads_here = dt_bias.shape[0]
    part = split_at // ctx_places
    before = passed_along(
        jnp.concatenate([head_rows[length - rim_rows :], shared_rows[length - rim_rows :]], axis=1),
        "ctx",
        1,
    )
    col_width = moe_in.shape[2]
    token_count = moe_in.shape[1]
    expert_count = slot_tok.shape[2]
    slot_width = slot_tok.shape[3]
    hidden_width = w_gate.shape[2]
    own = gate_act.shape[2]
    slot_ids = slot_tok[0, 0]
    live_slots = jnp.arange(slot_width, dtype=jnp.int32)[None, :] < slot_count[0, 0][:, None]
    chosen = jnp.where(live_slots, slot_ids, -1).reshape(-1)
    token_index = jnp.arange(token_count, dtype=jnp.int32)
    table = jnp.where(chosen[:, None] == token_index[None, :], 1.0, 0.0).astype(BF16)
    send_cot = jnp.dot(table, moe_cot[0], preferred_element_type=F32).astype(BF16)
    send_weight = jnp.where(live_slots, route_w[0, 0], jnp.zeros((), BF16))
    send_weight = jnp.pad(send_weight[:, None, :], ((0, 0), (0, 15), (0, col_width - slot_width)))
    send_cot = send_cot.reshape(expert_count, slot_width, col_width)
    got_cot = exchange(jnp.concatenate([send_cot, send_weight], axis=1), "expert")
    send_in = jnp.dot(table, moe_in[0], preferred_element_type=F32).astype(BF16)
    rows_in = exchange(send_in.reshape(expert_count, slot_width, col_width), "expert")

    gains = jnp.stack([dt_bias, a_log, d_skip])
    pad_heads = ((8 + length, split_at), F32)
    pad_shared = ((8 + length, shared_width), F32)
    (states,) = whole(
        front_kernel,
        [((ctx_places, 2 * part + 16, state_width), BF16)],
        [pad_heads, pad_shared],
        inputs=8,
    )(head_rows, shared_rows, before, raw_step, gains, conv_x, conv_bc, cot_rows)
    three, one = (3 * own, hidden_width), (own, hidden_width)
    left2, right2, left1, right1, centre, opposite = whole(
        unscaled_kernel,
        [(three, BF16)] * 5 + [(one, BF16)],
        [((ctx_places * own, col_width), BF16)],
        inputs=2,
        scalars=1,
        late=1,
    )(place, got_cot, w_down[0], states)
    opposite = shift(opposite, 3)
    left1 = (left1.astype(F32) + shift(left2, -1).astype(F32)).astype(BF16)
    right1 = (right1.astype(F32) + shift(right2, 1).astype(F32)).astype(BF16)
    centre = centre.astype(F32) + shift(left1, -1).astype(F32) + shift(right1, 1).astype(F32)
    far_left = shift(centre[:own].astype(BF16), -FAR)
    far_right = shift((centre[2 * own :] + opposite.astype(F32)).astype(BF16), FAR)
    mine = centre[own : 2 * own] + far_left.astype(F32) + far_right.astype(F32)
    rows_weight = got_cot[:, slot_width, :slot_width].reshape(-1).astype(F32)
    weight_own = lax.dynamic_slice_in_dim(rows_weight, place[0] * own, own, 0)
    (own_rows,) = whole(
        own_rows_kernel, [((own, 3 * hidden_width + 128), BF16)], inputs=4, late=1
    )(mine, weight_own[:, None], gate_act[0, 0], up_act[0, 0], rows_in)
    everything = lax.all_gather(own_rows, "ctx", axis=0, tiled=True)

    (entered,) = whole(
        scan_kernel, [((ctx_places, 2 * part, state_width), BF16)], inputs=1
    )(exchange(after(states, own_rows), "ctx"))

    main_heads, tail_heads, rim_heads, grad_bc, grad_step, taps_heads, grad_rate = whole(
        back_kernel,
        [
            ((length, split_at), BF16),
            ((16, split_at), F32),
            ((8, split_at), F32),
            ((expert_places, length, shared_width), BF16),
            ((heads_here, length), F32),
            ((rim_rows + 1, split_at), F32),
            ((1, 128), F32),
        ],
        [pad_heads, pad_shared, ((16 + length, split_at), F32), ((heads_here, length), F32)],
        inputs=9,
        limit=48 * 2**20,
    )(
        head_rows, shared_rows, before, raw_step, gains, conv_x, conv_bc, cot_rows,
        exchange(entered, "ctx"),
    )
    after_heads = passed_along(rim_heads[:rim_rows], "ctx", -1)
    grad_mamba_in = with_last_rows(main_heads, tail_heads, after_heads)
    main_shared, tail_shared, rim_shared, taps_shared = whole(
        shared_kernel,
        [
            ((length, shared_width), BF16),
            ((16, shared_width), F32),
            ((8, shared_width), F32),
            ((rim_rows + 1, shared_width), F32),
        ],
        [pad_shared, ((16 + length, shared_width), F32)],
        inputs=4,
    )(shared_rows, before, conv_bc, exchange(grad_bc, "expert"))
    after_shared = passed_along(rim_shared[:rim_rows], "ctx", -1)
    grad_shared_in = with_last_rows(main_shared, tail_shared, after_shared)
    small = jnp.concatenate(
        [
            taps_heads,
            taps_shared,
            jnp.broadcast_to(grad_rate, (dp_count, 128)),
            jnp.zeros((dp_count, 128), F32),
        ],
        axis=1,
    )
    small = jnp.sum(exchange(small.reshape(dp_count, 8, 128), "dp"), axis=0)
    small = jnp.sum(exchange(copies(small, ctx_places), "ctx"), axis=0).reshape(1, -1)
    taps_heads = small[:, :split_at]
    taps_shared = small[:, split_at : split_at + shared_width]
    rate_total = small[0, split_at + shared_width :][:heads_here]

    share = hidden_width // dp_count
    block = ((3 * share, col_width), BF16)
    owner = lax.axis_index("dp").astype(jnp.int32).reshape(1)
    parts = whole(
        weights_kernel,
        [block] * dp_count,
        [((3, hidden_width, col_width), BF16)],
        inputs=3,
        scalars=1,
        limit=56 * 2**20,
    )(owner, everything, rows_in, got_cot)
    parts = [parts[0]] + [
        lax.ppermute(parts[k], "dp", [(i, (i + k) % dp_count) for i in range(dp_count)])
        for k in range(1, dp_count)
    ]
    (back,) = whole(
        rows_kernel,
        [((expert_count, slot_width + 16, col_width), BF16)],
        inputs=3,
        limit=48 * 2**20,
    )(everything, w_gate[0], w_up[0])
    back = exchange(back, "expert")
    gate_total, up_total, down_total = whole(
        totals_kernel, [((share, col_width), BF16)] * 3, inputs=dp_count
    )(*parts)
    grad_tokens = lax.dot_general(
        table,
        back[:, :slot_width].reshape(-1, col_width),
        (((0,), (0,)), ((), ())),
        preferred_element_type=F32,
    )
    route_got = back[:, slot_width].astype(F32)
    route_total = jnp.where(
        live_slots, route_got[:, :slot_width] + route_got[:, slot_width:], 0.0
    )
    return (
        grad_mamba_in[None],
        grad_shared_in[None],
        grad_step[None],
        taps_heads,
        taps_shared,
        rate_total,
        grad_tokens.astype(BF16)[None],
        route_total[None, None],
        gate_total.T[None],
        up_total.T[None],
        down_total[None],
    )


def solution(mesh):
    placed = (
        P("dp", "ctx", "expert"),
        P("dp", "ctx", None),
        P("dp", "expert", "ctx"),
        P("expert"),
        P("expert"),
        P("expert"),
        P(None, "expert"),
        P(),
        P("dp", "ctx", "expert"),
        P("dp", "expert", "ctx"),
        P("dp", "expert", "ctx"),
        P("dp", "expert", None, None),
        P("dp", "expert", None),
        P("dp", "expert", None, None),
        P("expert", "ctx", None),
        P("expert", "ctx", None),
        P("expert", None, "ctx"),
        P("dp", "expert", "ctx", None),
        P("dp", "expert", "ctx", None),
    )
    return jax.shard_map(
        body,
        mesh=mesh,
        in_specs=placed,
        out_specs=(
            P("dp", "ctx", "expert"),
            P("dp", "ctx", None),
            P("dp", "expert", "ctx"),
            P("dp", "expert"),
            P("dp", None),
            P("expert"),
            P("dp", "expert", "ctx"),
            P("dp", "expert", None, None),
            P("expert", "ctx", "dp"),
            P("expert", "ctx", "dp"),
            P("expert", "dp", "ctx"),
        ),
        check_vma=False,
    )
```

```python
import jax
import jax.numpy as jnp
from jax import lax
from jax.experimental import pallas as pl
from jax.experimental.pallas import tpu as pltpu
from jax.sharding import PartitionSpec as P

PRECISE = lax.Precision.HIGHEST
F32 = jnp.float32
BF16 = jnp.bfloat16


def passed_along(value, axis, steps):
    count = lax.axis_size(axis)
    first, last = (max(0, -steps), min(count, count - steps))
    return lax.ppermute(value, axis, [(source, source + steps) for source in range(first, last)])


def exchange(value, axis):
    return lax.all_to_all(value, axis, split_axis=0, concat_axis=0, tiled=True)


def shift(value, distance):
    count = lax.axis_size("ctx")
    return lax.ppermute(value, "ctx", [(i, (i + distance) % count) for i in range(count)])


def after(value, *earlier):
    return lax.optimization_barrier((value,) + earlier)[0]


def copies(value, count):
    return jnp.broadcast_to(value[None], (count,) + value.shape)


def dot(a, b, ca, cb, precise=False):
    return lax.dot_general(
        a,
        b,
        (((ca,), (cb,)), ((), ())),
        precision=PRECISE if precise else None,
        preferred_element_type=F32,
    )


def iota(shape, axis):
    return lax.broadcasted_iota(jnp.int32, shape, axis)


def conv_pre(rows_ref, before, taps_ref, pad_ref):
    length, width = rows_ref.shape
    taps = taps_ref.shape[0]
    pad_ref[0:8, :] = jnp.zeros((8, width), F32)
    pad_ref[8 - (taps - 1) : 8, :] = before.astype(F32)
    pad_ref[8:, :] = rows_ref[...].astype(F32)
    pre = None
    for k in range(taps):
        start = 8 - (taps - 1) + k
        term = taps_ref[k : k + 1, :] * pad_ref[start : start + length, :]
        pre = term if pre is None else pre + term
    sig = jax.nn.sigmoid(pre)
    return pre, sig


def conv_pull(grad_pre, taps_ref, pad_ref, dv_ref):
    length, width = grad_pre.shape
    taps = taps_ref.shape[0]
    dv_ref[0:8, :] = jnp.zeros((8, width), F32)
    dv_ref[8 : 8 + length, :] = grad_pre
    dv_ref[8 + length :, :] = jnp.zeros((8, width), F32)
    rows = None
    rim = None
    sums = []
    for k in range(taps):
        weight = taps_ref[k : k + 1, :]
        start = 8 + (taps - 1) - k
        term = weight * dv_ref[start : start + length, :]
        rows = term if rows is None else rows + term
        edge = weight * dv_ref[8 - k : 16 - k, :]
        rim = edge if rim is None else rim + edge
        start = 8 - (taps - 1) + k
        sums.append(jnp.sum(grad_pre * pad_ref[start : start + length, :], axis=0, keepdims=True))
    rim = jnp.where(iota(rim.shape, 0) < taps - 1, rim, 0.0)
    return rows, rim, sums


def gain_column(gains_ref, which):
    heads = gains_ref.shape[1]
    eye = iota((heads, heads), 0) == iota((heads, heads), 1)
    return jnp.sum(jnp.where(eye, gains_ref[which : which + 1, :], 0.0), axis=1, keepdims=True)


def steps_of(raw_ref, gains_ref):
    shifted = raw_ref[...] + gain_column(gains_ref, 0)
    step = jnp.maximum(shifted, 0.0) + jnp.log1p(jnp.exp(-jnp.abs(shifted)))
    rate = jnp.exp(gain_column(gains_ref, 1))
    log_decay = -rate * step
    length = shifted.shape[1]
    square = (length, length)
    upto = jnp.where(iota(square, 0) <= iota(square, 1), 1.0, 0.0)
    cumulative = dot(log_decay, upto, 1, 0, True)
    return shifted, step, rate, log_decay, upto, cumulative


def head_spread(heads, width):
    spread = (heads, heads * width)
    return jnp.where(iota(spread, 1) // width == iota(spread, 0), 1.0, 0.0)


def front_kernel(
    rows_ref, shared_ref, before_ref, raw_ref, gains_ref, tapsx_ref,
    tapsbc_ref, cot_ref, out_ref, padh_ref, pads_ref,
):
    heads = raw_ref.shape[0]
    width = rows_ref.shape[1] // heads
    states = shared_ref.shape[1] // 2
    places = out_ref.shape[0]
    part = heads * width // places
    pre, sig = conv_pre(rows_ref, before_ref[:, : rows_ref.shape[1]], tapsx_ref, padh_ref)
    x = pre * sig
    before_s = before_ref[:, rows_ref.shape[1] :]
    pre_s, sig_s = conv_pre(shared_ref, before_s, tapsbc_ref, pads_ref)
    bc = (pre_s * sig_s).astype(BF16)
    _, step, _, _, _, cumulative = steps_of(raw_ref, gains_ref)
    length = step.shape[1]
    ending = cumulative[:, length - 1 :]
    spread = head_spread(heads, width)
    weight = dot(jnp.exp(ending - cumulative) * step, spread, 0, 0, True)
    grown = dot(jnp.exp(cumulative), spread, 0, 0, True)
    fresh = dot((x * weight).astype(BF16), bc[:, :states], 0, 0)
    pulls = dot((cot_ref[...].astype(F32) * grown).astype(BF16), bc[:, states:], 0, 0)
    out_ref[:, :part, :] = fresh.astype(BF16).reshape(places, part, states)
    out_ref[:, part : 2 * part, :] = pulls.astype(BF16).reshape(places, part, states)
    coarse = ending.astype(BF16).astype(F32)
    fine = ending - coarse
    per_head = places // heads
    mark = (16, states)
    for place in range(places):
        head = place // per_head
        marks = jnp.where(
            iota(mark, 0) == 0,
            jnp.broadcast_to(coarse[head : head + 1], mark),
            jnp.broadcast_to(fine[head : head + 1], mark),
        )
        out_ref[place, 2 * part :, :] = marks.astype(BF16)


def back_kernel(
    rows_ref, shared_ref, before_ref, raw_ref, gains_ref,
    tapsx_ref, tapsbc_ref, cot_ref, got_ref,
    main_ref, tail_ref, rim_ref, bc_ref, raw_out_ref, taps_out_ref, rate_out_ref,
    padh_ref, pads_ref, dv_ref, sums_ref,
):
    heads, length = raw_ref.shape
    width = rows_ref.shape[1] // heads
    states = shared_ref.shape[1] // 2
    part = got_ref.shape[1] // 2
    pre, sig = conv_pre(rows_ref, before_ref[:, : rows_ref.shape[1]], tapsx_ref, padh_ref)
    x = pre * sig
    before_s = before_ref[:, rows_ref.shape[1] :]
    pre_s, sig_s = conv_pre(shared_ref, before_s, tapsbc_ref, pads_ref)
    bc = (pre_s * sig_s).astype(BF16)
    b_rows, c_rows = bc[:, :states], bc[:, states:]
    shifted, step, rate, log_decay, upto, cumulative = steps_of(raw_ref, gains_ref)
    ending = cumulative[:, length - 1 :]
    spread = head_spread(heads, width)
    weight = dot(jnp.exp(ending - cumulative) * step, spread, 0, 0, True)
    grown = dot(jnp.exp(cumulative), spread, 0, 0, True)
    step_cols = dot(step, spread, 0, 0, True)
    skip_cols = jnp.sum(gain_column(gains_ref, 2) * spread, axis=0, keepdims=True)
    state_in = got_ref[:, :part, :].reshape(heads * width, states)
    pull_out = got_ref[:, part:, :].reshape(heads * width, states)
    cot = cot_ref[...]
    cot_wide = cot.astype(F32)
    b_pull = dot(b_rows, pull_out, 1, 1)
    c_state = dot(c_rows, state_in, 1, 1)
    cot_grown = cot_wide * grown
    x_weight = x * weight
    grad_c = dot(cot_grown.astype(BF16), state_in, 1, 0)
    grad_b = dot(x_weight.astype(BF16), pull_out, 1, 0)
    lane = (heads * width, 128)
    lane_of, head_of = iota(lane, 1), iota(lane, 0) // width
    pick = jnp.where((lane_of == head_of) | (lane_of == 2 * heads + head_of), 1.0, 0.0)
    pick_next = jnp.where(lane_of == heads + head_of, 1.0, 0.0)
    columns = dot(x_weight * b_pull, pick, 1, 0, True)
    columns = columns + dot(cot_grown * c_state, pick_next, 1, 0, True)
    scores = dot(b_rows, c_rows, 1, 1)
    square = (length, length)
    earlier = iota(square, 0) <= iota(square, 1)
    cumulative_cols = dot(upto, log_decay, 0, 1, True)
    x_step = (x * step_cols).astype(BF16)
    pair = max(1, 128 // width)
    block = pair * width
    lane_head = iota((length, block), 1) // width
    column_lane = iota((length, 128), 1)
    grad_scores = jnp.zeros(square, F32)
    inner = []
    for base in range(0, heads, pair):
        at = base * width
        x_pair = x_step[:, at : at + block]
        cot_pair = cot[:, at : at + block]
        sum_pair = None
        for i in range(pair):
            head = base + i
            cot_one = jnp.where(lane_head == i, cot_pair, jnp.zeros((), BF16))
            grad_mix = dot(x_pair, cot_one, 1, 1)
            gap = cumulative[head : head + 1, :] - cumulative_cols[:, head : head + 1]
            decay = jnp.exp(jnp.where(earlier, gap, -1e30))
            mix = decay * scores
            grad_scores = grad_scores + decay * grad_mix
            moved = mix * grad_mix
            sums_ref[head : head + 1, :] = jnp.sum(moved, axis=0, keepdims=True)
            columns = columns + jnp.where(
                column_lane == head, jnp.sum(moved, axis=1, keepdims=True), 0.0
            )
            term = dot(mix.astype(BF16), cot_one, 1, 0)
            sum_pair = term if sum_pair is None else sum_pair + term
        inner.append(sum_pair)
    inner = jnp.concatenate(inner, axis=1)
    grad_scores = grad_scores.astype(BF16)
    grad_b = grad_b + dot(grad_scores, c_rows, 1, 0)
    grad_c = grad_c + dot(grad_scores, b_rows, 0, 0)
    grad_bc = jnp.concatenate([grad_b, grad_c], axis=1).astype(BF16)
    for copy in range(bc_ref.shape[0]):
        bc_ref[copy] = grad_bc
    turned = columns.T
    left = turned[:heads]
    came = sums_ref[...] + turned[heads : 2 * heads]
    state_pull = state_in.astype(F32) * pull_out.astype(F32)
    state_pull = jnp.sum(state_pull.reshape(heads, width, states), axis=1)
    state_pull = jnp.exp(ending) * jnp.sum(state_pull, axis=1, keepdims=True)
    to_last = jnp.sum(turned[2 * heads : 3 * heads], axis=1, keepdims=True)
    grad_decay = dot(came - left, upto, 1, 1, True) + to_last + state_pull
    grad_step = left / step - rate * grad_decay
    raw_out_ref[...] = grad_step * jax.nn.sigmoid(shifted)
    grad_rate = jnp.sum(grad_decay * log_decay, axis=1, keepdims=True)
    eye = jnp.where(iota((heads, 128), 0) == iota((heads, 128), 1), 1.0, 0.0)
    rate_out_ref[...] = jnp.sum(grad_rate * eye, axis=0, keepdims=True)
    grad_x = inner * step_cols + skip_cols * cot_wide + weight * b_pull
    grad_pre = grad_x * (sig * (1.0 + pre * (1.0 - sig)))
    rows, rim, sums = conv_pull(grad_pre, tapsx_ref, padh_ref, dv_ref)
    main_ref[...] = rows.astype(BF16)
    tail_ref[...] = rows[length - 16 :]
    rim_ref[...] = rim
    for k, total in enumerate(sums):
        taps_out_ref[k : k + 1, :] = total


def shared_kernel(
    shared_ref, before_ref, tapsbc_ref, got_ref,
    main_ref, tail_ref, rim_ref, taps_out_ref, pads_ref, dv_ref,
):
    length = shared_ref.shape[0]
    before = before_ref[:, before_ref.shape[1] - shared_ref.shape[1] :]
    pre, sig = conv_pre(shared_ref, before, tapsbc_ref, pads_ref)
    total = got_ref[0].astype(F32)
    for source in range(1, got_ref.shape[0]):
        total = total + got_ref[source].astype(F32)
    grad_pre = total * (sig * (1.0 + pre * (1.0 - sig)))
    rows, rim, sums = conv_pull(grad_pre, tapsbc_ref, pads_ref, dv_ref)
    main_ref[...] = rows.astype(BF16)
    tail_ref[...] = rows[length - 16 :]
    rim_ref[...] = rim
    for k, value in enumerate(sums):
        taps_out_ref[k : k + 1, :] = value


FAR = 5
CENTRE = (-FAR, 0, FAR)
OPPOSITE = 8


def shifted_by(distance):
    return tuple(distance + step for step in CENTRE)


def rows_of(cot_ref, block, rows):
    per_group = (cot_ref.shape[1] - 16) // rows
    start = pl.multiple_of((block % per_group) * rows, rows)
    return cot_ref[block // per_group, pl.ds(start, rows), :]


def unscaled_kernel(place_ref, cot_ref, down_ref, earlier_ref, *refs):
    del earlier_ref
    out_refs, rows_ref = refs[:-1], refs[-1]
    places = rows_ref.shape[0] // out_refs[-1].shape[0]
    rows = out_refs[-1].shape[0]
    place = place_ref[0]
    at = 0
    for distances in (shifted_by(-2), shifted_by(2), shifted_by(-1), shifted_by(1), CENTRE, (OPPOSITE,)):
        for distance in distances:
            block = lax.rem(place + distance + places, places)
            rows_ref[at : at + rows, :] = rows_of(cot_ref, block, rows)
            at += rows
    product = dot(rows_ref[...], down_ref[...], 1, 1).astype(BF16)
    at = 0
    for out_ref in out_refs:
        out_ref[...] = product[at : at + out_ref.shape[0]]
        at += out_ref.shape[0]


def scaled_rows(cot_ref, group):
    slots = cot_ref.shape[1] - 16
    weight = cot_ref[group, slots:, :slots].astype(F32).T[:, 0:1]
    return (cot_ref[group, :slots, :].astype(F32) * weight).astype(BF16)


def own_rows_kernel(mine_ref, weight_ref, gate_ref, up_ref, earlier_ref, out_ref):
    del earlier_ref
    width = mine_ref.shape[1]
    unscaled = mine_ref[...].astype(F32)
    gate = gate_ref[...].astype(F32)
    up = up_ref[...].astype(F32)
    grad_hidden = weight_ref[...] * unscaled
    sig = jax.nn.sigmoid(gate)
    activated = gate * sig
    hidden = (activated * up).astype(BF16)
    slope = sig * (1.0 + gate * (1.0 - sig))
    out_ref[:, :width] = (grad_hidden * up * slope).astype(BF16)
    out_ref[:, width : 2 * width] = (grad_hidden * activated).astype(BF16)
    out_ref[:, 2 * width : 3 * width] = hidden
    route = jnp.sum(hidden.astype(F32) * unscaled, axis=1, keepdims=True)
    coarse = route.astype(BF16).astype(F32)
    lanes = (mine_ref.shape[0], 128)
    out_ref[:, 3 * width :] = jnp.where(
        iota(lanes, 1) == 0, coarse, jnp.where(iota(lanes, 1) == 1, route - coarse, 0.0)
    ).astype(BF16)


def rows_kernel(
    place_ref, all_ref, in_ref, cot_ref, gatew_ref, upw_ref, earlier_ref, back_ref, *refs
):
    del earlier_ref
    out_refs, grads_ref = refs[:-1], refs[-1]
    groups, slots, cols = in_ref.shape
    width = gatew_ref.shape[1]
    owners = len(out_refs)
    share = width // owners
    rows_grad = dot(all_ref[:, :width], gatew_ref[...], 1, 1)
    rows_grad = rows_grad + dot(all_ref[:, width : 2 * width], upw_ref[...], 1, 1)
    back_ref[:, :slots, :] = rows_grad.astype(BF16).reshape(groups, slots, cols)
    route = all_ref[:, 3 * width :].astype(F32)
    for group in range(groups):
        turned = route[group * slots : (group + 1) * slots].T
        line = jnp.concatenate([turned[0:1], turned[1:2]], axis=1)
        back_ref[group, slots:, :] = jnp.broadcast_to(line, (16, cols)).astype(BF16)
    rows_in = in_ref[...].reshape(groups * slots, cols)
    scaled = jnp.concatenate([scaled_rows(cot_ref, group) for group in range(groups)], axis=0)
    grads_ref[0] = dot(all_ref[:, :width], rows_in, 0, 0).astype(BF16)
    grads_ref[1] = dot(all_ref[:, width : 2 * width], rows_in, 0, 0).astype(BF16)
    grads_ref[2] = dot(all_ref[:, 2 * width : 3 * width], scaled, 0, 0).astype(BF16)
    for ahead in range(owners):
        owner = lax.rem(place_ref[0] + ahead, owners)
        start = pl.multiple_of(owner * share, 64)
        for kind in range(3):
            out_refs[ahead][kind * share : (kind + 1) * share, :] = grads_ref[
                kind, pl.ds(start, share), :
            ]


def totals_kernel(*refs):
    part_refs, out_refs = refs[:-3], refs[-3:]
    share = out_refs[0].shape[0]
    for kind, out_ref in enumerate(out_refs):
        span = slice(kind * share, (kind + 1) * share)
        value = part_refs[0][span, :].astype(F32)
        for part_ref in part_refs[1:]:
            value = value + part_ref[span, :].astype(F32)
        out_ref[...] = value.astype(BF16)


def scan_kernel(got_ref, out_ref):
    places, half = got_ref.shape[0], out_ref.shape[1] // 2
    width = got_ref.shape[2]
    decay = [
        jnp.exp(
            got_ref[j, 2 * half : 2 * half + 1, :].astype(F32)
            + got_ref[j, 2 * half + 1 : 2 * half + 2, :].astype(F32)
        )
        for j in range(places)
    ]
    state = jnp.zeros((half, width), F32)
    for j in range(places):
        out_ref[j, :half, :] = state.astype(BF16)
        state = decay[j] * state + got_ref[j, :half, :].astype(F32)
    state = jnp.zeros((half, width), F32)
    for j in reversed(range(places)):
        out_ref[j, half:, :] = state.astype(BF16)
        state = decay[j] * state + got_ref[j, half : 2 * half, :].astype(F32)


def whole(kernel, outs, scratch=(), inputs=0, scalars=0, late=0, limit=None):
    specs = [pl.BlockSpec(memory_space=pltpu.SMEM)] * scalars
    specs += [pl.BlockSpec(memory_space=pltpu.VMEM)] * inputs
    specs += [pl.BlockSpec(memory_space=pl.ANY)] * late
    return pl.pallas_call(
        kernel,
        out_shape=[jax.ShapeDtypeStruct(shape, kind) for shape, kind in outs],
        in_specs=specs,
        out_specs=[pl.BlockSpec(memory_space=pltpu.VMEM)] * len(outs),
        scratch_shapes=[pltpu.VMEM(shape, kind) for shape, kind in scratch],
        compiler_params=pltpu.CompilerParams(vmem_limit_bytes=limit),
    )


def with_last_rows(main, tail, after):
    rows = tail.shape[0]
    given = jnp.pad(after, ((rows - after.shape[0], 0), (0, 0)))
    return lax.dynamic_update_slice(
        main, (tail + given).astype(BF16), (main.shape[0] - rows, 0)
    )


def body(
    mamba_in,
    shared_in,
    dt_raw,
    dt_bias,
    a_log,
    d_skip,
    conv_x,
    conv_bc,
    mamba_cot,
    moe_in,
    moe_cot,
    slot_tok,
    slot_count,
    route_w,
    w_gate,
    w_up,
    w_down,
    gate_act,
    up_act,
):
    dp_count, expert_places, ctx_places = (
        lax.axis_size("dp"),
        lax.axis_size("expert"),
        lax.axis_size("ctx"),
    )
    place = lax.axis_index("ctx").astype(jnp.int32).reshape(1)
    rim_rows = conv_x.shape[0] - 1
    head_rows = mamba_in[0]
    shared_rows = shared_in[0]
    cot_rows = mamba_cot[0]
    raw_step = dt_raw[0]
    length, split_at = head_rows.shape
    shared_width = shared_rows.shape[1]
    state_width = shared_width // 2
    heads_here = dt_bias.shape[0]
    part = split_at // ctx_places
    before = passed_along(
        jnp.concatenate([head_rows[length - rim_rows :], shared_rows[length - rim_rows :]], axis=1),
        "ctx",
        1,
    )
    col_width = moe_in.shape[2]
    token_count = moe_in.shape[1]
    expert_count = slot_tok.shape[2]
    slot_width = slot_tok.shape[3]
    hidden_width = w_gate.shape[2]
    own = gate_act.shape[2]
    slot_ids = slot_tok[0, 0]
    live_slots = jnp.arange(slot_width, dtype=jnp.int32)[None, :] < slot_count[0, 0][:, None]
    chosen = jnp.where(live_slots, slot_ids, -1).reshape(-1)
    token_index = jnp.arange(token_count, dtype=jnp.int32)
    table = jnp.where(chosen[:, None] == token_index[None, :], 1.0, 0.0).astype(BF16)
    send_cot = jnp.dot(table, moe_cot[0], preferred_element_type=F32).astype(BF16)
    send_weight = jnp.where(live_slots, route_w[0, 0], jnp.zeros((), BF16))
    send_weight = jnp.pad(send_weight[:, None, :], ((0, 0), (0, 15), (0, col_width - slot_width)))
    send_cot = send_cot.reshape(expert_count, slot_width, col_width)
    got_cot = exchange(jnp.concatenate([send_cot, send_weight], axis=1), "expert")
    send_in = jnp.dot(table, moe_in[0], preferred_element_type=F32).astype(BF16)

    gains = jnp.stack([dt_bias, a_log, d_skip])
    pad_heads = ((8 + length, split_at), F32)
    pad_shared = ((8 + length, shared_width), F32)
    (states,) = whole(
        front_kernel,
        [((ctx_places, 2 * part + 16, state_width), BF16)],
        [pad_heads, pad_shared],
        inputs=8,
    )(head_rows, shared_rows, before, raw_step, gains, conv_x, conv_bc, cot_rows)
    three, one = (3 * own, hidden_width), (own, hidden_width)
    left2, right2, left1, right1, centre, opposite = whole(
        unscaled_kernel,
        [(three, BF16)] * 5 + [(one, BF16)],
        [((ctx_places * own, col_width), BF16)],
        inputs=2,
        scalars=1,
        late=1,
    )(place, got_cot, w_down[0], states)
    opposite = shift(opposite, 3)
    left1 = (left1.astype(F32) + shift(left2, -1).astype(F32)).astype(BF16)
    right1 = (right1.astype(F32) + shift(right2, 1).astype(F32)).astype(BF16)
    got_states = exchange(after(states, left1, right1), "ctx")
    centre = centre.astype(F32) + shift(left1, -1).astype(F32) + shift(right1, 1).astype(F32)
    far_left = shift(centre[:own].astype(BF16), -FAR)
    far_right = shift((centre[2 * own :] + opposite.astype(F32)).astype(BF16), FAR)
    mine = centre[own : 2 * own] + far_left.astype(F32) + far_right.astype(F32)
    rows_weight = got_cot[:, slot_width, :slot_width].reshape(-1).astype(F32)
    weight_own = lax.dynamic_slice_in_dim(rows_weight, place[0] * own, own, 0)
    (own_rows,) = whole(
        own_rows_kernel, [((own, 3 * hidden_width + 128), BF16)], inputs=4, late=1
    )(mine, weight_own[:, None], gate_act[0, 0], up_act[0, 0], got_states)
    everything = lax.all_gather(own_rows, "ctx", axis=0, tiled=True)

    (entered,) = whole(
        scan_kernel, [((ctx_places, 2 * part, state_width), BF16)], inputs=1
    )(got_states)

    entered = exchange(entered, "ctx")
    send_in = after(send_in.reshape(expert_count, slot_width, col_width), entered)
    rows_in = exchange(send_in, "expert")

    main_heads, tail_heads, rim_heads, grad_bc, grad_step, taps_heads, grad_rate = whole(
        back_kernel,
        [
            ((length, split_at), BF16),
            ((16, split_at), F32),
            ((8, split_at), F32),
            ((expert_places, length, shared_width), BF16),
            ((heads_here, length), F32),
            ((rim_rows + 1, split_at), F32),
            ((1, 128), F32),
        ],
        [pad_heads, pad_shared, ((16 + length, split_at), F32), ((heads_here, length), F32)],
        inputs=9,
        limit=48 * 2**20,
    )(
        head_rows, shared_rows, before, raw_step, gains, conv_x, conv_bc, cot_rows,
        entered,
    )
    grad_bc = after(grad_bc, rows_in)
    after_heads = passed_along(rim_heads[:rim_rows], "ctx", -1)
    grad_mamba_in = with_last_rows(main_heads, tail_heads, after_heads)
    main_shared, tail_shared, rim_shared, taps_shared = whole(
        shared_kernel,
        [
            ((length, shared_width), BF16),
            ((16, shared_width), F32),
            ((8, shared_width), F32),
            ((rim_rows + 1, shared_width), F32),
        ],
        [pad_shared, ((16 + length, shared_width), F32)],
        inputs=4,
    )(shared_rows, before, conv_bc, exchange(grad_bc, "expert"))
    after_shared = passed_along(rim_shared[:rim_rows], "ctx", -1)
    grad_shared_in = with_last_rows(main_shared, tail_shared, after_shared)
    small = jnp.concatenate(
        [
            taps_heads,
            taps_shared,
            jnp.broadcast_to(grad_rate, (dp_count, 128)),
            jnp.zeros((dp_count, 128), F32),
        ],
        axis=1,
    )
    small = jnp.sum(exchange(small.reshape(dp_count, 8, 128), "dp"), axis=0)
    small = jnp.sum(exchange(copies(small, ctx_places), "ctx"), axis=0).reshape(1, -1)
    taps_heads = small[:, :split_at]
    taps_shared = small[:, split_at : split_at + shared_width]
    rate_total = small[0, split_at + shared_width :][:heads_here]

    share = hidden_width // dp_count
    block = ((3 * share, col_width), BF16)
    owner = lax.axis_index("dp").astype(jnp.int32).reshape(1)
    back, *parts = whole(
        rows_kernel,
        [((expert_count, slot_width + 16, col_width), BF16)] + [block] * dp_count,
        [((3, hidden_width, col_width), BF16)],
        inputs=5,
        scalars=1,
        late=1,
        limit=56 * 2**20,
    )(owner, everything, rows_in, got_cot, w_gate[0], w_up[0], small)
    back = exchange(back, "expert")
    parts = [parts[0]] + [
        lax.ppermute(parts[k], "dp", [(i, (i + k) % dp_count) for i in range(dp_count)])
        for k in range(1, dp_count)
    ]
    gate_total, up_total, down_total = whole(
        totals_kernel, [((share, col_width), BF16)] * 3, inputs=dp_count
    )(*parts)
    grad_tokens = lax.dot_general(
        table,
        back[:, :slot_width].reshape(-1, col_width),
        (((0,), (0,)), ((), ())),
        preferred_element_type=F32,
    )
    route_got = back[:, slot_width].astype(F32)
    route_total = jnp.where(
        live_slots, route_got[:, :slot_width] + route_got[:, slot_width:], 0.0
    )
    return (
        grad_mamba_in[None],
        grad_shared_in[None],
        grad_step[None],
        taps_heads,
        taps_shared,
        rate_total,
        grad_tokens.astype(BF16)[None],
        route_total[None, None],
        gate_total.T[None],
        up_total.T[None],
        down_total[None],
    )


def solution(mesh):
    placed = (
        P("dp", "ctx", "expert"),
        P("dp", "ctx", None),
        P("dp", "expert", "ctx"),
        P("expert"),
        P("expert"),
        P("expert"),
        P(None, "expert"),
        P(),
        P("dp", "ctx", "expert"),
        P("dp", "expert", "ctx"),
        P("dp", "expert", "ctx"),
        P("dp", "expert", None, None),
        P("dp", "expert", None),
        P("dp", "expert", None, None),
        P("expert", "ctx", None),
        P("expert", "ctx", None),
        P("expert", None, "ctx"),
        P("dp", "expert", "ctx", None),
        P("dp", "expert", "ctx", None),
    )
    return jax.shard_map(
        body,
        mesh=mesh,
        in_specs=placed,
        out_specs=(
            P("dp", "ctx", "expert"),
            P("dp", "ctx", None),
            P("dp", "expert", "ctx"),
            P("dp", "expert"),
            P("dp", None),
            P("expert"),
            P("dp", "expert", "ctx"),
            P("dp", "expert", None, None),
            P("expert", "ctx", "dp"),
            P("expert", "ctx", "dp"),
            P("expert", "dp", "ctx"),
        ),
        check_vma=False,
    )
```

```python
import jax
import jax.numpy as jnp
from jax import lax
from jax.experimental import pallas as pl
from jax.experimental.pallas import tpu as pltpu
from jax.sharding import PartitionSpec as P

PRECISE = lax.Precision.HIGHEST
F32 = jnp.float32
BF16 = jnp.bfloat16


def passed_along(value, axis, steps):
    count = lax.axis_size(axis)
    first, last = (max(0, -steps), min(count, count - steps))
    return lax.ppermute(value, axis, [(source, source + steps) for source in range(first, last)])


def exchange(value, axis):
    return lax.all_to_all(value, axis, split_axis=0, concat_axis=0, tiled=True)


def after(value, *earlier):
    return lax.optimization_barrier((value,) + earlier)[0]


def copies(value, count):
    return jnp.broadcast_to(value[None], (count,) + value.shape)


def dot(a, b, ca, cb, precise=False):
    return lax.dot_general(
        a,
        b,
        (((ca,), (cb,)), ((), ())),
        precision=PRECISE if precise else None,
        preferred_element_type=F32,
    )


def iota(shape, axis):
    return lax.broadcasted_iota(jnp.int32, shape, axis)


def conv_pre(rows_ref, before, taps_ref, pad_ref):
    length, width = rows_ref.shape
    taps = taps_ref.shape[0]
    pad_ref[0:8, :] = jnp.zeros((8, width), F32)
    pad_ref[8 - (taps - 1) : 8, :] = before.astype(F32)
    pad_ref[8:, :] = rows_ref[...].astype(F32)
    pre = None
    for k in range(taps):
        start = 8 - (taps - 1) + k
        term = taps_ref[k : k + 1, :] * pad_ref[start : start + length, :]
        pre = term if pre is None else pre + term
    sig = jax.nn.sigmoid(pre)
    return pre, sig


def conv_pull(grad_pre, taps_ref, pad_ref, dv_ref):
    length, width = grad_pre.shape
    taps = taps_ref.shape[0]
    dv_ref[0:8, :] = jnp.zeros((8, width), F32)
    dv_ref[8 : 8 + length, :] = grad_pre
    dv_ref[8 + length :, :] = jnp.zeros((8, width), F32)
    rows = None
    rim = None
    sums = []
    for k in range(taps):
        weight = taps_ref[k : k + 1, :]
        start = 8 + (taps - 1) - k
        term = weight * dv_ref[start : start + length, :]
        rows = term if rows is None else rows + term
        edge = weight * dv_ref[8 - k : 16 - k, :]
        rim = edge if rim is None else rim + edge
        start = 8 - (taps - 1) + k
        sums.append(jnp.sum(grad_pre * pad_ref[start : start + length, :], axis=0, keepdims=True))
    rim = jnp.where(iota(rim.shape, 0) < taps - 1, rim, 0.0)
    return rows, rim, sums


def gain_column(gains_ref, which):
    heads = gains_ref.shape[1]
    eye = iota((heads, heads), 0) == iota((heads, heads), 1)
    return jnp.sum(jnp.where(eye, gains_ref[which : which + 1, :], 0.0), axis=1, keepdims=True)


def steps_of(raw_ref, gains_ref):
    shifted = raw_ref[...] + gain_column(gains_ref, 0)
    step = jnp.maximum(shifted, 0.0) + jnp.log1p(jnp.exp(-jnp.abs(shifted)))
    rate = jnp.exp(gain_column(gains_ref, 1))
    log_decay = -rate * step
    length = shifted.shape[1]
    square = (length, length)
    upto = jnp.where(iota(square, 0) <= iota(square, 1), 1.0, 0.0)
    cumulative = dot(log_decay, upto, 1, 0, True)
    return shifted, step, rate, log_decay, upto, cumulative


def head_spread(heads, width):
    spread = (heads, heads * width)
    return jnp.where(iota(spread, 1) // width == iota(spread, 0), 1.0, 0.0)


def front_kernel(
    rows_ref, shared_ref, before_ref, raw_ref, gains_ref, tapsx_ref,
    tapsbc_ref, cot_ref, out_ref, padh_ref, pads_ref,
):
    heads = raw_ref.shape[0]
    width = rows_ref.shape[1] // heads
    states = shared_ref.shape[1] // 2
    places = out_ref.shape[0]
    part = heads * width // places
    pre, sig = conv_pre(rows_ref, before_ref[:, : rows_ref.shape[1]], tapsx_ref, padh_ref)
    x = pre * sig
    before_s = before_ref[:, rows_ref.shape[1] :]
    pre_s, sig_s = conv_pre(shared_ref, before_s, tapsbc_ref, pads_ref)
    bc = (pre_s * sig_s).astype(BF16)
    _, step, _, _, _, cumulative = steps_of(raw_ref, gains_ref)
    length = step.shape[1]
    ending = cumulative[:, length - 1 :]
    spread = head_spread(heads, width)
    weight = dot(jnp.exp(ending - cumulative) * step, spread, 0, 0, True)
    grown = dot(jnp.exp(cumulative), spread, 0, 0, True)
    fresh = dot((x * weight).astype(BF16), bc[:, :states], 0, 0)
    pulls = dot((cot_ref[...].astype(F32) * grown).astype(BF16), bc[:, states:], 0, 0)
    out_ref[:, :part, :] = fresh.astype(BF16).reshape(places, part, states)
    out_ref[:, part : 2 * part, :] = pulls.astype(BF16).reshape(places, part, states)
    coarse = ending.astype(BF16).astype(F32)
    fine = ending - coarse
    per_head = places // heads
    mark = (16, states)
    for place in range(places):
        head = place // per_head
        marks = jnp.where(
            iota(mark, 0) == 0,
            jnp.broadcast_to(coarse[head : head + 1], mark),
            jnp.broadcast_to(fine[head : head + 1], mark),
        )
        out_ref[place, 2 * part :, :] = marks.astype(BF16)


def back_kernel(
    rows_ref, shared_ref, before_ref, raw_ref, gains_ref,
    tapsx_ref, tapsbc_ref, cot_ref, got_ref,
    main_ref, tail_ref, rim_ref, bc_ref, raw_out_ref, taps_out_ref, rate_out_ref,
    padh_ref, pads_ref, dv_ref, sums_ref,
):
    heads, length = raw_ref.shape
    width = rows_ref.shape[1] // heads
    states = shared_ref.shape[1] // 2
    part = got_ref.shape[1] // 2
    pre, sig = conv_pre(rows_ref, before_ref[:, : rows_ref.shape[1]], tapsx_ref, padh_ref)
    x = pre * sig
    before_s = before_ref[:, rows_ref.shape[1] :]
    pre_s, sig_s = conv_pre(shared_ref, before_s, tapsbc_ref, pads_ref)
    bc = (pre_s * sig_s).astype(BF16)
    b_rows, c_rows = bc[:, :states], bc[:, states:]
    shifted, step, rate, log_decay, upto, cumulative = steps_of(raw_ref, gains_ref)
    ending = cumulative[:, length - 1 :]
    spread = head_spread(heads, width)
    weight = dot(jnp.exp(ending - cumulative) * step, spread, 0, 0, True)
    grown = dot(jnp.exp(cumulative), spread, 0, 0, True)
    step_cols = dot(step, spread, 0, 0, True)
    skip_cols = jnp.sum(gain_column(gains_ref, 2) * spread, axis=0, keepdims=True)
    state_in = got_ref[:, :part, :].reshape(heads * width, states)
    pull_out = got_ref[:, part:, :].reshape(heads * width, states)
    cot = cot_ref[...]
    cot_wide = cot.astype(F32)
    b_pull = dot(b_rows, pull_out, 1, 1)
    c_state = dot(c_rows, state_in, 1, 1)
    cot_grown = cot_wide * grown
    x_weight = x * weight
    grad_c = dot(cot_grown.astype(BF16), state_in, 1, 0)
    grad_b = dot(x_weight.astype(BF16), pull_out, 1, 0)
    lane = (heads * width, 128)
    lane_of, head_of = iota(lane, 1), iota(lane, 0) // width
    pick = jnp.where((lane_of == head_of) | (lane_of == 2 * heads + head_of), 1.0, 0.0)
    pick_next = jnp.where(lane_of == heads + head_of, 1.0, 0.0)
    columns = dot(x_weight * b_pull, pick, 1, 0, True)
    columns = columns + dot(cot_grown * c_state, pick_next, 1, 0, True)
    scores = dot(b_rows, c_rows, 1, 1)
    square = (length, length)
    earlier = iota(square, 0) <= iota(square, 1)
    cumulative_cols = dot(upto, log_decay, 0, 1, True)
    x_step = (x * step_cols).astype(BF16)
    pair = max(1, 128 // width)
    block = pair * width
    lane_head = iota((length, block), 1) // width
    column_lane = iota((length, 128), 1)
    grad_scores = jnp.zeros(square, F32)
    inner = []
    for base in range(0, heads, pair):
        at = base * width
        x_pair = x_step[:, at : at + block]
        cot_pair = cot[:, at : at + block]
        sum_pair = None
        for i in range(pair):
            head = base + i
            cot_one = jnp.where(lane_head == i, cot_pair, jnp.zeros((), BF16))
            grad_mix = dot(x_pair, cot_one, 1, 1)
            gap = cumulative[head : head + 1, :] - cumulative_cols[:, head : head + 1]
            decay = jnp.exp(jnp.where(earlier, gap, -1e30))
            mix = decay * scores
            grad_scores = grad_scores + decay * grad_mix
            moved = mix * grad_mix
            sums_ref[head : head + 1, :] = jnp.sum(moved, axis=0, keepdims=True)
            columns = columns + jnp.where(
                column_lane == head, jnp.sum(moved, axis=1, keepdims=True), 0.0
            )
            term = dot(mix.astype(BF16), cot_one, 1, 0)
            sum_pair = term if sum_pair is None else sum_pair + term
        inner.append(sum_pair)
    inner = jnp.concatenate(inner, axis=1)
    grad_scores = grad_scores.astype(BF16)
    grad_b = grad_b + dot(grad_scores, c_rows, 1, 0)
    grad_c = grad_c + dot(grad_scores, b_rows, 0, 0)
    grad_bc = jnp.concatenate([grad_b, grad_c], axis=1).astype(BF16)
    for copy in range(bc_ref.shape[0]):
        bc_ref[copy] = grad_bc
    turned = columns.T
    left = turned[:heads]
    came = sums_ref[...] + turned[heads : 2 * heads]
    state_pull = state_in.astype(F32) * pull_out.astype(F32)
    state_pull = jnp.sum(state_pull.reshape(heads, width, states), axis=1)
    state_pull = jnp.exp(ending) * jnp.sum(state_pull, axis=1, keepdims=True)
    to_last = jnp.sum(turned[2 * heads : 3 * heads], axis=1, keepdims=True)
    grad_decay = dot(came - left, upto, 1, 1, True) + to_last + state_pull
    grad_step = left / step - rate * grad_decay
    raw_out_ref[...] = grad_step * jax.nn.sigmoid(shifted)
    grad_rate = jnp.sum(grad_decay * log_decay, axis=1, keepdims=True)
    eye = jnp.where(iota((heads, 128), 0) == iota((heads, 128), 1), 1.0, 0.0)
    rate_out_ref[...] = jnp.sum(grad_rate * eye, axis=0, keepdims=True)
    grad_x = inner * step_cols + skip_cols * cot_wide + weight * b_pull
    grad_pre = grad_x * (sig * (1.0 + pre * (1.0 - sig)))
    rows, rim, sums = conv_pull(grad_pre, tapsx_ref, padh_ref, dv_ref)
    main_ref[...] = rows.astype(BF16)
    tail_ref[...] = rows[length - 16 :]
    rim_ref[...] = rim
    for k, total in enumerate(sums):
        taps_out_ref[k : k + 1, :] = total


def shared_kernel(
    shared_ref, before_ref, tapsbc_ref, got_ref,
    main_ref, tail_ref, rim_ref, taps_out_ref, pads_ref, dv_ref,
):
    length = shared_ref.shape[0]
    before = before_ref[:, before_ref.shape[1] - shared_ref.shape[1] :]
    pre, sig = conv_pre(shared_ref, before, tapsbc_ref, pads_ref)
    total = got_ref[0].astype(F32)
    for source in range(1, got_ref.shape[0]):
        total = total + got_ref[source].astype(F32)
    grad_pre = total * (sig * (1.0 + pre * (1.0 - sig)))
    rows, rim, sums = conv_pull(grad_pre, tapsbc_ref, pads_ref, dv_ref)
    main_ref[...] = rows.astype(BF16)
    tail_ref[...] = rows[length - 16 :]
    rim_ref[...] = rim
    for k, value in enumerate(sums):
        taps_out_ref[k : k + 1, :] = value


def scaled_rows(cot_ref, group):
    slots = cot_ref.shape[1] - 16
    weight = cot_ref[group, slots:, :slots].astype(F32).T[:, 0:1]
    return (cot_ref[group, :slots, :].astype(F32) * weight).astype(BF16)


def own_rows_kernel(mine_ref, weight_ref, gate_ref, up_ref, first_ref, second_ref, out_ref):
    del first_ref, second_ref
    width = mine_ref.shape[1]
    unscaled = mine_ref[...].astype(F32)
    gate = gate_ref[...].astype(F32)
    up = up_ref[...].astype(F32)
    grad_hidden = weight_ref[...] * unscaled
    sig = jax.nn.sigmoid(gate)
    activated = gate * sig
    hidden = (activated * up).astype(BF16)
    slope = sig * (1.0 + gate * (1.0 - sig))
    out_ref[:, :width] = (grad_hidden * up * slope).astype(BF16)
    out_ref[:, width : 2 * width] = (grad_hidden * activated).astype(BF16)
    out_ref[:, 2 * width : 3 * width] = hidden
    route = jnp.sum(hidden.astype(F32) * unscaled, axis=1, keepdims=True)
    coarse = route.astype(BF16).astype(F32)
    lanes = (mine_ref.shape[0], 128)
    out_ref[:, 3 * width :] = jnp.where(
        iota(lanes, 1) == 0, coarse, jnp.where(iota(lanes, 1) == 1, route - coarse, 0.0)
    ).astype(BF16)


def rows_kernel(
    place_ref, all_ref, in_ref, cot_ref, gatew_ref, upw_ref, earlier_ref, back_ref, *refs
):
    del earlier_ref
    out_refs, grads_ref = refs[:-1], refs[-1]
    groups, slots, cols = in_ref.shape
    width = gatew_ref.shape[1]
    owners = len(out_refs)
    share = width // owners
    rows_grad = dot(all_ref[:, :width], gatew_ref[...], 1, 1)
    rows_grad = rows_grad + dot(all_ref[:, width : 2 * width], upw_ref[...], 1, 1)
    back_ref[:, :slots, :] = rows_grad.astype(BF16).reshape(groups, slots, cols)
    route = all_ref[:, 3 * width :].astype(F32)
    for group in range(groups):
        turned = route[group * slots : (group + 1) * slots].T
        line = jnp.concatenate([turned[0:1], turned[1:2]], axis=1)
        back_ref[group, slots:, :] = jnp.broadcast_to(line, (16, cols)).astype(BF16)
    rows_in = in_ref[...].reshape(groups * slots, cols)
    scaled = jnp.concatenate([scaled_rows(cot_ref, group) for group in range(groups)], axis=0)
    grads_ref[0] = dot(all_ref[:, :width], rows_in, 0, 0).astype(BF16)
    grads_ref[1] = dot(all_ref[:, width : 2 * width], rows_in, 0, 0).astype(BF16)
    grads_ref[2] = dot(all_ref[:, 2 * width : 3 * width], scaled, 0, 0).astype(BF16)
    for ahead in range(owners):
        owner = lax.rem(place_ref[0] + ahead, owners)
        start = pl.multiple_of(owner * share, 64)
        for kind in range(3):
            out_refs[ahead][kind * share : (kind + 1) * share, :] = grads_ref[
                kind, pl.ds(start, share), :
            ]


def totals_kernel(*refs):
    part_refs, out_refs = refs[:-3], refs[-3:]
    share = out_refs[0].shape[0]
    for kind, out_ref in enumerate(out_refs):
        span = slice(kind * share, (kind + 1) * share)
        value = part_refs[0][span, :].astype(F32)
        for part_ref in part_refs[1:]:
            value = value + part_ref[span, :].astype(F32)
        out_ref[...] = value.astype(BF16)


def scan_kernel(got_ref, out_ref):
    places, half = got_ref.shape[0], out_ref.shape[1] // 2
    width = got_ref.shape[2]
    decay = [
        jnp.exp(
            got_ref[j, 2 * half : 2 * half + 1, :].astype(F32)
            + got_ref[j, 2 * half + 1 : 2 * half + 2, :].astype(F32)
        )
        for j in range(places)
    ]
    state = jnp.zeros((half, width), F32)
    for j in range(places):
        out_ref[j, :half, :] = state.astype(BF16)
        state = decay[j] * state + got_ref[j, :half, :].astype(F32)
    state = jnp.zeros((half, width), F32)
    for j in reversed(range(places)):
        out_ref[j, half:, :] = state.astype(BF16)
        state = decay[j] * state + got_ref[j, half : 2 * half, :].astype(F32)


def whole(kernel, outs, scratch=(), inputs=0, scalars=0, late=0, limit=None):
    specs = [pl.BlockSpec(memory_space=pltpu.SMEM)] * scalars
    specs += [pl.BlockSpec(memory_space=pltpu.VMEM)] * inputs
    specs += [pl.BlockSpec(memory_space=pl.ANY)] * late
    return pl.pallas_call(
        kernel,
        out_shape=[jax.ShapeDtypeStruct(shape, kind) for shape, kind in outs],
        in_specs=specs,
        out_specs=[pl.BlockSpec(memory_space=pltpu.VMEM)] * len(outs),
        scratch_shapes=[pltpu.VMEM(shape, kind) for shape, kind in scratch],
        compiler_params=pltpu.CompilerParams(vmem_limit_bytes=limit),
    )


def with_last_rows(main, tail, after):
    rows = tail.shape[0]
    given = jnp.pad(after, ((rows - after.shape[0], 0), (0, 0)))
    return lax.dynamic_update_slice(
        main, (tail + given).astype(BF16), (main.shape[0] - rows, 0)
    )


def body(
    mamba_in,
    shared_in,
    dt_raw,
    dt_bias,
    a_log,
    d_skip,
    conv_x,
    conv_bc,
    mamba_cot,
    moe_in,
    moe_cot,
    slot_tok,
    slot_count,
    route_w,
    w_gate,
    w_up,
    w_down,
    gate_act,
    up_act,
):
    dp_count, expert_places, ctx_places = (
        lax.axis_size("dp"),
        lax.axis_size("expert"),
        lax.axis_size("ctx"),
    )
    place = lax.axis_index("ctx").astype(jnp.int32).reshape(1)
    rim_rows = conv_x.shape[0] - 1
    head_rows = mamba_in[0]
    shared_rows = shared_in[0]
    cot_rows = mamba_cot[0]
    raw_step = dt_raw[0]
    length, split_at = head_rows.shape
    shared_width = shared_rows.shape[1]
    state_width = shared_width // 2
    heads_here = dt_bias.shape[0]
    part = split_at // ctx_places
    before = passed_along(
        jnp.concatenate([head_rows[length - rim_rows :], shared_rows[length - rim_rows :]], axis=1),
        "ctx",
        1,
    )
    col_width = moe_in.shape[2]
    token_count = moe_in.shape[1]
    expert_count = slot_tok.shape[2]
    slot_width = slot_tok.shape[3]
    hidden_width = w_gate.shape[2]
    own = gate_act.shape[2]
    slot_ids = slot_tok[0, 0]
    live_slots = jnp.arange(slot_width, dtype=jnp.int32)[None, :] < slot_count[0, 0][:, None]
    chosen = jnp.where(live_slots, slot_ids, -1).reshape(-1)
    token_index = jnp.arange(token_count, dtype=jnp.int32)
    table = jnp.where(chosen[:, None] == token_index[None, :], 1.0, 0.0).astype(BF16)
    send_cot = jnp.dot(table, moe_cot[0], preferred_element_type=F32).astype(BF16)
    send_weight = jnp.where(live_slots, route_w[0, 0], jnp.zeros((), BF16))
    send_weight = jnp.pad(send_weight[:, None, :], ((0, 0), (0, 15), (0, col_width - slot_width)))
    send_cot = send_cot.reshape(expert_count, slot_width, col_width)
    got_cot = exchange(jnp.concatenate([send_cot, send_weight], axis=1), "expert")
    send_in = jnp.dot(table, moe_in[0], preferred_element_type=F32).astype(BF16)

    gains = jnp.stack([dt_bias, a_log, d_skip])
    pad_heads = ((8 + length, split_at), F32)
    pad_shared = ((8 + length, shared_width), F32)
    (states,) = whole(
        front_kernel,
        [((ctx_places, 2 * part + 16, state_width), BF16)],
        [pad_heads, pad_shared],
        inputs=8,
    )(head_rows, shared_rows, before, raw_step, gains, conv_x, conv_bc, cot_rows)
    unscaled = jnp.dot(
        after(got_cot, states)[:, :slot_width].reshape(-1, col_width), w_down[0].T, preferred_element_type=F32
    ).astype(BF16)
    mine = lax.psum_scatter(unscaled, "ctx", scatter_dimension=0, tiled=True)
    got_states = exchange(after(states, unscaled), "ctx")
    (entered,) = whole(
        scan_kernel, [((ctx_places, 2 * part, state_width), BF16)], inputs=1
    )(got_states)

    entered = exchange(entered, "ctx")
    send_in = after(send_in.reshape(expert_count, slot_width, col_width), entered)
    rows_in = exchange(send_in, "expert")

    main_heads, tail_heads, rim_heads, grad_bc, grad_step, taps_heads, grad_rate = whole(
        back_kernel,
        [
            ((length, split_at), BF16),
            ((16, split_at), F32),
            ((8, split_at), F32),
            ((expert_places, length, shared_width), BF16),
            ((heads_here, length), F32),
            ((rim_rows + 1, split_at), F32),
            ((1, 128), F32),
        ],
        [pad_heads, pad_shared, ((16 + length, split_at), F32), ((heads_here, length), F32)],
        inputs=9,
        limit=48 * 2**20,
    )(
        head_rows, shared_rows, before, raw_step, gains, conv_x, conv_bc, cot_rows,
        entered,
    )
    rows_weight = got_cot[:, slot_width, :slot_width].reshape(-1).astype(F32)
    weight_own = lax.dynamic_slice_in_dim(rows_weight, place[0] * own, own, 0)
    (own_rows,) = whole(
        own_rows_kernel, [((own, 3 * hidden_width + 128), BF16)], inputs=4, late=2
    )(mine, weight_own[:, None], gate_act[0, 0], up_act[0, 0], grad_step, rows_in)
    everything = lax.all_gather(own_rows, "ctx", axis=0, tiled=True)
    grad_bc = after(grad_bc, rows_in)
    after_heads = passed_along(rim_heads[:rim_rows], "ctx", -1)
    grad_mamba_in = with_last_rows(main_heads, tail_heads, after_heads)
    main_shared, tail_shared, rim_shared, taps_shared = whole(
        shared_kernel,
        [
            ((length, shared_width), BF16),
            ((16, shared_width), F32),
            ((8, shared_width), F32),
            ((rim_rows + 1, shared_width), F32),
        ],
        [pad_shared, ((16 + length, shared_width), F32)],
        inputs=4,
    )(shared_rows, before, conv_bc, exchange(grad_bc, "expert"))
    after_shared = passed_along(rim_shared[:rim_rows], "ctx", -1)
    grad_shared_in = with_last_rows(main_shared, tail_shared, after_shared)
    small = jnp.concatenate(
        [
            taps_heads,
            taps_shared,
            jnp.broadcast_to(grad_rate, (dp_count, 128)),
            jnp.zeros((dp_count, 128), F32),
        ],
        axis=1,
    )
    small = jnp.sum(exchange(small.reshape(dp_count, 8, 128), "dp"), axis=0)
    small = jnp.sum(exchange(copies(small, ctx_places), "ctx"), axis=0).reshape(1, -1)
    taps_heads = small[:, :split_at]
    taps_shared = small[:, split_at : split_at + shared_width]
    rate_total = small[0, split_at + shared_width :][:heads_here]

    share = hidden_width // dp_count
    block = ((3 * share, col_width), BF16)
    owner = lax.axis_index("dp").astype(jnp.int32).reshape(1)
    back, *parts = whole(
        rows_kernel,
        [((expert_count, slot_width + 16, col_width), BF16)] + [block] * dp_count,
        [((3, hidden_width, col_width), BF16)],
        inputs=5,
        scalars=1,
        late=1,
        limit=56 * 2**20,
    )(owner, everything, rows_in, got_cot, w_gate[0], w_up[0], small)
    back = exchange(back, "expert")
    parts = [parts[0]] + [
        lax.ppermute(parts[k], "dp", [(i, (i + k) % dp_count) for i in range(dp_count)])
        for k in range(1, dp_count)
    ]
    gate_total, up_total, down_total = whole(
        totals_kernel, [((share, col_width), BF16)] * 3, inputs=dp_count
    )(*parts)
    grad_tokens = lax.dot_general(
        table,
        back[:, :slot_width].reshape(-1, col_width),
        (((0,), (0,)), ((), ())),
        preferred_element_type=F32,
    )
    route_got = back[:, slot_width].astype(F32)
    route_total = jnp.where(
        live_slots, route_got[:, :slot_width] + route_got[:, slot_width:], 0.0
    )
    return (
        grad_mamba_in[None],
        grad_shared_in[None],
        grad_step[None],
        taps_heads,
        taps_shared,
        rate_total,
        grad_tokens.astype(BF16)[None],
        route_total[None, None],
        gate_total.T[None],
        up_total.T[None],
        down_total[None],
    )


def solution(mesh):
    placed = (
        P("dp", "ctx", "expert"),
        P("dp", "ctx", None),
        P("dp", "expert", "ctx"),
        P("expert"),
        P("expert"),
        P("expert"),
        P(None, "expert"),
        P(),
        P("dp", "ctx", "expert"),
        P("dp", "expert", "ctx"),
        P("dp", "expert", "ctx"),
        P("dp", "expert", None, None),
        P("dp", "expert", None),
        P("dp", "expert", None, None),
        P("expert", "ctx", None),
        P("expert", "ctx", None),
        P("expert", None, "ctx"),
        P("dp", "expert", "ctx", None),
        P("dp", "expert", "ctx", None),
    )
    return jax.shard_map(
        body,
        mesh=mesh,
        in_specs=placed,
        out_specs=(
            P("dp", "ctx", "expert"),
            P("dp", "ctx", None),
            P("dp", "expert", "ctx"),
            P("dp", "expert"),
            P("dp", None),
            P("expert"),
            P("dp", "expert", "ctx"),
            P("dp", "expert", None, None),
            P("expert", "ctx", "dp"),
            P("expert", "ctx", "dp"),
            P("expert", "dp", "ctx"),
        ),
        check_vma=False,
    )
```

```python
import jax
import jax.numpy as jnp
from jax import lax
from jax.experimental import pallas as pl
from jax.experimental.pallas import tpu as pltpu
from jax.sharding import PartitionSpec as P

PRECISE = lax.Precision.HIGHEST
F32 = jnp.float32
BF16 = jnp.bfloat16


def passed_along(value, axis, steps):
    count = lax.axis_size(axis)
    first, last = (max(0, -steps), min(count, count - steps))
    return lax.ppermute(value, axis, [(source, source + steps) for source in range(first, last)])


def exchange(value, axis):
    return lax.all_to_all(value, axis, split_axis=0, concat_axis=0, tiled=True)


def shift(value, distance):
    count = lax.axis_size("ctx")
    return lax.ppermute(value, "ctx", [(i, (i + distance) % count) for i in range(count)])


def after(value, *earlier):
    return lax.optimization_barrier((value,) + earlier)[0]


def copies(value, count):
    return jnp.broadcast_to(value[None], (count,) + value.shape)


def dot(a, b, ca, cb, precise=False):
    return lax.dot_general(
        a,
        b,
        (((ca,), (cb,)), ((), ())),
        precision=PRECISE if precise else None,
        preferred_element_type=F32,
    )


def iota(shape, axis):
    return lax.broadcasted_iota(jnp.int32, shape, axis)


def conv_pre(rows_ref, before, taps_ref, pad_ref):
    length, width = rows_ref.shape
    taps = taps_ref.shape[0]
    pad_ref[0:8, :] = jnp.zeros((8, width), F32)
    pad_ref[8 - (taps - 1) : 8, :] = before.astype(F32)
    pad_ref[8:, :] = rows_ref[...].astype(F32)
    pre = None
    for k in range(taps):
        start = 8 - (taps - 1) + k
        term = taps_ref[k : k + 1, :] * pad_ref[start : start + length, :]
        pre = term if pre is None else pre + term
    sig = jax.nn.sigmoid(pre)
    return pre, sig


def conv_pull(grad_pre, taps_ref, pad_ref, dv_ref):
    length, width = grad_pre.shape
    taps = taps_ref.shape[0]
    dv_ref[0:8, :] = jnp.zeros((8, width), F32)
    dv_ref[8 : 8 + length, :] = grad_pre
    dv_ref[8 + length :, :] = jnp.zeros((8, width), F32)
    rows = None
    rim = None
    sums = []
    for k in range(taps):
        weight = taps_ref[k : k + 1, :]
        start = 8 + (taps - 1) - k
        term = weight * dv_ref[start : start + length, :]
        rows = term if rows is None else rows + term
        edge = weight * dv_ref[8 - k : 16 - k, :]
        rim = edge if rim is None else rim + edge
        start = 8 - (taps - 1) + k
        sums.append(jnp.sum(grad_pre * pad_ref[start : start + length, :], axis=0, keepdims=True))
    rim = jnp.where(iota(rim.shape, 0) < taps - 1, rim, 0.0)
    return rows, rim, sums


def gain_column(gains_ref, which):
    heads = gains_ref.shape[1]
    eye = iota((heads, heads), 0) == iota((heads, heads), 1)
    return jnp.sum(jnp.where(eye, gains_ref[which : which + 1, :], 0.0), axis=1, keepdims=True)


def steps_of(raw_ref, gains_ref):
    shifted = raw_ref[...] + gain_column(gains_ref, 0)
    step = jnp.maximum(shifted, 0.0) + jnp.log1p(jnp.exp(-jnp.abs(shifted)))
    rate = jnp.exp(gain_column(gains_ref, 1))
    log_decay = -rate * step
    length = shifted.shape[1]
    square = (length, length)
    upto = jnp.where(iota(square, 0) <= iota(square, 1), 1.0, 0.0)
    cumulative = dot(log_decay, upto, 1, 0, True)
    return shifted, step, rate, log_decay, upto, cumulative


def head_spread(heads, width):
    spread = (heads, heads * width)
    return jnp.where(iota(spread, 1) // width == iota(spread, 0), 1.0, 0.0)


def front_kernel(
    rows_ref, shared_ref, before_ref, raw_ref, gains_ref, tapsx_ref,
    tapsbc_ref, cot_ref, out_ref, padh_ref, pads_ref,
):
    heads = raw_ref.shape[0]
    width = rows_ref.shape[1] // heads
    states = shared_ref.shape[1] // 2
    places = out_ref.shape[0]
    part = heads * width // places
    pre, sig = conv_pre(rows_ref, before_ref[:, : rows_ref.shape[1]], tapsx_ref, padh_ref)
    x = pre * sig
    before_s = before_ref[:, rows_ref.shape[1] :]
    pre_s, sig_s = conv_pre(shared_ref, before_s, tapsbc_ref, pads_ref)
    bc = (pre_s * sig_s).astype(BF16)
    _, step, _, _, _, cumulative = steps_of(raw_ref, gains_ref)
    length = step.shape[1]
    ending = cumulative[:, length - 1 :]
    spread = head_spread(heads, width)
    weight = dot(jnp.exp(ending - cumulative) * step, spread, 0, 0, True)
    grown = dot(jnp.exp(cumulative), spread, 0, 0, True)
    fresh = dot((x * weight).astype(BF16), bc[:, :states], 0, 0)
    pulls = dot((cot_ref[...].astype(F32) * grown).astype(BF16), bc[:, states:], 0, 0)
    out_ref[:, :part, :] = fresh.astype(BF16).reshape(places, part, states)
    out_ref[:, part : 2 * part, :] = pulls.astype(BF16).reshape(places, part, states)
    coarse = ending.astype(BF16).astype(F32)
    fine = ending - coarse
    per_head = places // heads
    mark = (16, states)
    for place in range(places):
        head = place // per_head
        marks = jnp.where(
            iota(mark, 0) == 0,
            jnp.broadcast_to(coarse[head : head + 1], mark),
            jnp.broadcast_to(fine[head : head + 1], mark),
        )
        out_ref[place, 2 * part :, :] = marks.astype(BF16)


def back_kernel(
    rows_ref, shared_ref, before_ref, raw_ref, gains_ref,
    tapsx_ref, tapsbc_ref, cot_ref, got_ref,
    main_ref, tail_ref, rim_ref, bc_ref, raw_out_ref, taps_out_ref, rate_out_ref,
    padh_ref, pads_ref, dv_ref, sums_ref,
):
    heads, length = raw_ref.shape
    width = rows_ref.shape[1] // heads
    states = shared_ref.shape[1] // 2
    part = got_ref.shape[1] // 2
    pre, sig = conv_pre(rows_ref, before_ref[:, : rows_ref.shape[1]], tapsx_ref, padh_ref)
    x = pre * sig
    before_s = before_ref[:, rows_ref.shape[1] :]
    pre_s, sig_s = conv_pre(shared_ref, before_s, tapsbc_ref, pads_ref)
    bc = (pre_s * sig_s).astype(BF16)
    b_rows, c_rows = bc[:, :states], bc[:, states:]
    shifted, step, rate, log_decay, upto, cumulative = steps_of(raw_ref, gains_ref)
    ending = cumulative[:, length - 1 :]
    spread = head_spread(heads, width)
    weight = dot(jnp.exp(ending - cumulative) * step, spread, 0, 0, True)
    grown = dot(jnp.exp(cumulative), spread, 0, 0, True)
    step_cols = dot(step, spread, 0, 0, True)
    skip_cols = jnp.sum(gain_column(gains_ref, 2) * spread, axis=0, keepdims=True)
    state_in = got_ref[:, :part, :].reshape(heads * width, states)
    pull_out = got_ref[:, part:, :].reshape(heads * width, states)
    cot = cot_ref[...]
    cot_wide = cot.astype(F32)
    b_pull = dot(b_rows, pull_out, 1, 1)
    c_state = dot(c_rows, state_in, 1, 1)
    cot_grown = cot_wide * grown
    x_weight = x * weight
    grad_c = dot(cot_grown.astype(BF16), state_in, 1, 0)
    grad_b = dot(x_weight.astype(BF16), pull_out, 1, 0)
    lane = (heads * width, 128)
    lane_of, head_of = iota(lane, 1), iota(lane, 0) // width
    pick = jnp.where((lane_of == head_of) | (lane_of == 2 * heads + head_of), 1.0, 0.0)
    pick_next = jnp.where(lane_of == heads + head_of, 1.0, 0.0)
    columns = dot(x_weight * b_pull, pick, 1, 0, True)
    columns = columns + dot(cot_grown * c_state, pick_next, 1, 0, True)
    scores = dot(b_rows, c_rows, 1, 1)
    square = (length, length)
    earlier = iota(square, 0) <= iota(square, 1)
    cumulative_cols = dot(upto, log_decay, 0, 1, True)
    x_step = (x * step_cols).astype(BF16)
    pair = max(1, 128 // width)
    block = pair * width
    lane_head = iota((length, block), 1) // width
    column_lane = iota((length, 128), 1)
    grad_scores = jnp.zeros(square, F32)
    inner = []
    for base in range(0, heads, pair):
        at = base * width
        x_pair = x_step[:, at : at + block]
        cot_pair = cot[:, at : at + block]
        sum_pair = None
        for i in range(pair):
            head = base + i
            cot_one = jnp.where(lane_head == i, cot_pair, jnp.zeros((), BF16))
            grad_mix = dot(x_pair, cot_one, 1, 1)
            gap = cumulative[head : head + 1, :] - cumulative_cols[:, head : head + 1]
            decay = jnp.exp(jnp.where(earlier, gap, -1e30))
            mix = decay * scores
            grad_scores = grad_scores + decay * grad_mix
            moved = mix * grad_mix
            sums_ref[head : head + 1, :] = jnp.sum(moved, axis=0, keepdims=True)
            columns = columns + jnp.where(
                column_lane == head, jnp.sum(moved, axis=1, keepdims=True), 0.0
            )
            term = dot(mix.astype(BF16), cot_one, 1, 0)
            sum_pair = term if sum_pair is None else sum_pair + term
        inner.append(sum_pair)
    inner = jnp.concatenate(inner, axis=1)
    grad_scores = grad_scores.astype(BF16)
    grad_b = grad_b + dot(grad_scores, c_rows, 1, 0)
    grad_c = grad_c + dot(grad_scores, b_rows, 0, 0)
    grad_bc = jnp.concatenate([grad_b, grad_c], axis=1).astype(BF16)
    for copy in range(bc_ref.shape[0]):
        bc_ref[copy] = grad_bc
    turned = columns.T
    left = turned[:heads]
    came = sums_ref[...] + turned[heads : 2 * heads]
    state_pull = state_in.astype(F32) * pull_out.astype(F32)
    state_pull = jnp.sum(state_pull.reshape(heads, width, states), axis=1)
    state_pull = jnp.exp(ending) * jnp.sum(state_pull, axis=1, keepdims=True)
    to_last = jnp.sum(turned[2 * heads : 3 * heads], axis=1, keepdims=True)
    grad_decay = dot(came - left, upto, 1, 1, True) + to_last + state_pull
    grad_step = left / step - rate * grad_decay
    raw_out_ref[...] = grad_step * jax.nn.sigmoid(shifted)
    grad_rate = jnp.sum(grad_decay * log_decay, axis=1, keepdims=True)
    eye = jnp.where(iota((heads, 128), 0) == iota((heads, 128), 1), 1.0, 0.0)
    rate_out_ref[...] = jnp.sum(grad_rate * eye, axis=0, keepdims=True)
    grad_x = inner * step_cols + skip_cols * cot_wide + weight * b_pull
    grad_pre = grad_x * (sig * (1.0 + pre * (1.0 - sig)))
    rows, rim, sums = conv_pull(grad_pre, tapsx_ref, padh_ref, dv_ref)
    main_ref[...] = rows.astype(BF16)
    tail_ref[...] = rows[length - 16 :]
    rim_ref[...] = rim
    for k, total in enumerate(sums):
        taps_out_ref[k : k + 1, :] = total


def shared_kernel(
    shared_ref, before_ref, tapsbc_ref, got_ref,
    main_ref, tail_ref, rim_ref, taps_out_ref, pads_ref, dv_ref,
):
    length = shared_ref.shape[0]
    before = before_ref[:, before_ref.shape[1] - shared_ref.shape[1] :]
    pre, sig = conv_pre(shared_ref, before, tapsbc_ref, pads_ref)
    total = got_ref[0].astype(F32)
    for source in range(1, got_ref.shape[0]):
        total = total + got_ref[source].astype(F32)
    grad_pre = total * (sig * (1.0 + pre * (1.0 - sig)))
    rows, rim, sums = conv_pull(grad_pre, tapsbc_ref, pads_ref, dv_ref)
    main_ref[...] = rows.astype(BF16)
    tail_ref[...] = rows[length - 16 :]
    rim_ref[...] = rim
    for k, value in enumerate(sums):
        taps_out_ref[k : k + 1, :] = value


FAR = 5
CENTRE = (-FAR, 0, FAR)
OPPOSITE = 8


def shifted_by(distance):
    return tuple(distance + step for step in CENTRE)


def rows_of(cot_ref, block, rows):
    per_group = (cot_ref.shape[1] - 16) // rows
    start = pl.multiple_of((block % per_group) * rows, rows)
    return cot_ref[block // per_group, pl.ds(start, rows), :]


def unscaled_kernel(place_ref, cot_ref, down_ref, earlier_ref, *refs):
    del earlier_ref
    out_refs, rows_ref = refs[:-1], refs[-1]
    places = rows_ref.shape[0] // out_refs[-1].shape[0]
    rows = out_refs[-1].shape[0]
    place = place_ref[0]
    at = 0
    for distances in (shifted_by(-2), shifted_by(2), shifted_by(-1), shifted_by(1), CENTRE, (OPPOSITE,)):
        for distance in distances:
            block = lax.rem(place + distance + places, places)
            rows_ref[at : at + rows, :] = rows_of(cot_ref, block, rows)
            at += rows
    product = dot(rows_ref[...], down_ref[...], 1, 1).astype(BF16)
    at = 0
    for out_ref in out_refs:
        out_ref[...] = product[at : at + out_ref.shape[0]]
        at += out_ref.shape[0]


def scaled_rows(cot_ref, group):
    slots = cot_ref.shape[1] - 16
    weight = cot_ref[group, slots:, :slots].astype(F32).T[:, 0:1]
    return (cot_ref[group, :slots, :].astype(F32) * weight).astype(BF16)


def own_rows_kernel(mine_ref, weight_ref, gate_ref, up_ref, earlier_ref, out_ref):
    del earlier_ref
    width = mine_ref.shape[1]
    unscaled = mine_ref[...].astype(F32)
    gate = gate_ref[...].astype(F32)
    up = up_ref[...].astype(F32)
    grad_hidden = weight_ref[...] * unscaled
    sig = jax.nn.sigmoid(gate)
    activated = gate * sig
    hidden = (activated * up).astype(BF16)
    slope = sig * (1.0 + gate * (1.0 - sig))
    out_ref[:, :width] = (grad_hidden * up * slope).astype(BF16)
    out_ref[:, width : 2 * width] = (grad_hidden * activated).astype(BF16)
    out_ref[:, 2 * width : 3 * width] = hidden
    route = jnp.sum(hidden.astype(F32) * unscaled, axis=1, keepdims=True)
    coarse = route.astype(BF16).astype(F32)
    lanes = (mine_ref.shape[0], 128)
    out_ref[:, 3 * width :] = jnp.where(
        iota(lanes, 1) == 0, coarse, jnp.where(iota(lanes, 1) == 1, route - coarse, 0.0)
    ).astype(BF16)


def rows_kernel(
    place_ref, all_ref, in_ref, cot_ref, gatew_ref, upw_ref, earlier_ref, back_ref, *refs
):
    del earlier_ref
    out_refs, grads_ref = refs[:-1], refs[-1]
    groups, slots, cols = in_ref.shape
    width = gatew_ref.shape[1]
    owners = len(out_refs)
    share = width // owners
    rows_grad = dot(all_ref[:, :width], gatew_ref[...], 1, 1)
    rows_grad = rows_grad + dot(all_ref[:, width : 2 * width], upw_ref[...], 1, 1)
    back_ref[:, :slots, :] = rows_grad.astype(BF16).reshape(groups, slots, cols)
    route = all_ref[:, 3 * width :].astype(F32)
    for group in range(groups):
        turned = route[group * slots : (group + 1) * slots].T
        line = jnp.concatenate([turned[0:1], turned[1:2]], axis=1)
        back_ref[group, slots:, :] = jnp.broadcast_to(line, (16, cols)).astype(BF16)
    rows_in = in_ref[...].reshape(groups * slots, cols)
    scaled = jnp.concatenate([scaled_rows(cot_ref, group) for group in range(groups)], axis=0)
    grads_ref[0] = dot(all_ref[:, :width], rows_in, 0, 0).astype(BF16)
    grads_ref[1] = dot(all_ref[:, width : 2 * width], rows_in, 0, 0).astype(BF16)
    grads_ref[2] = dot(all_ref[:, 2 * width : 3 * width], scaled, 0, 0).astype(BF16)
    for ahead in range(owners):
        owner = lax.rem(place_ref[0] + ahead, owners)
        start = pl.multiple_of(owner * share, 64)
        for kind in range(3):
            out_refs[ahead][kind * share : (kind + 1) * share, :] = grads_ref[
                kind, pl.ds(start, share), :
            ]


def totals_kernel(*refs):
    part_refs, out_refs = refs[:-3], refs[-3:]
    share = out_refs[0].shape[0]
    for kind, out_ref in enumerate(out_refs):
        span = slice(kind * share, (kind + 1) * share)
        value = part_refs[0][span, :].astype(F32)
        for part_ref in part_refs[1:]:
            value = value + part_ref[span, :].astype(F32)
        out_ref[...] = value.astype(BF16)


def scan_kernel(got_ref, out_ref):
    places, half = got_ref.shape[0], out_ref.shape[1] // 2
    width = got_ref.shape[2]
    decay = [
        jnp.exp(
            got_ref[j, 2 * half : 2 * half + 1, :].astype(F32)
            + got_ref[j, 2 * half + 1 : 2 * half + 2, :].astype(F32)
        )
        for j in range(places)
    ]
    state = jnp.zeros((half, width), F32)
    for j in range(places):
        out_ref[j, :half, :] = state.astype(BF16)
        state = decay[j] * state + got_ref[j, :half, :].astype(F32)
    state = jnp.zeros((half, width), F32)
    for j in reversed(range(places)):
        out_ref[j, half:, :] = state.astype(BF16)
        state = decay[j] * state + got_ref[j, half : 2 * half, :].astype(F32)


def whole(kernel, outs, scratch=(), inputs=0, scalars=0, late=0, limit=None):
    specs = [pl.BlockSpec(memory_space=pltpu.SMEM)] * scalars
    specs += [pl.BlockSpec(memory_space=pltpu.VMEM)] * inputs
    specs += [pl.BlockSpec(memory_space=pl.ANY)] * late
    return pl.pallas_call(
        kernel,
        out_shape=[jax.ShapeDtypeStruct(shape, kind) for shape, kind in outs],
        in_specs=specs,
        out_specs=[pl.BlockSpec(memory_space=pltpu.VMEM)] * len(outs),
        scratch_shapes=[pltpu.VMEM(shape, kind) for shape, kind in scratch],
        compiler_params=pltpu.CompilerParams(vmem_limit_bytes=limit),
    )


def with_last_rows(main, tail, after):
    rows = tail.shape[0]
    given = jnp.pad(after, ((rows - after.shape[0], 0), (0, 0)))
    return lax.dynamic_update_slice(
        main, (tail + given).astype(BF16), (main.shape[0] - rows, 0)
    )


def body(
    mamba_in,
    shared_in,
    dt_raw,
    dt_bias,
    a_log,
    d_skip,
    conv_x,
    conv_bc,
    mamba_cot,
    moe_in,
    moe_cot,
    slot_tok,
    slot_count,
    route_w,
    w_gate,
    w_up,
    w_down,
    gate_act,
    up_act,
):
    dp_count, expert_places, ctx_places = (
        lax.axis_size("dp"),
        lax.axis_size("expert"),
        lax.axis_size("ctx"),
    )
    place = lax.axis_index("ctx").astype(jnp.int32).reshape(1)
    rim_rows = conv_x.shape[0] - 1
    head_rows = mamba_in[0]
    shared_rows = shared_in[0]
    cot_rows = mamba_cot[0]
    raw_step = dt_raw[0]
    length, split_at = head_rows.shape
    shared_width = shared_rows.shape[1]
    state_width = shared_width // 2
    heads_here = dt_bias.shape[0]
    part = split_at // ctx_places
    before = passed_along(
        jnp.concatenate([head_rows[length - rim_rows :], shared_rows[length - rim_rows :]], axis=1),
        "ctx",
        1,
    )
    col_width = moe_in.shape[2]
    token_count = moe_in.shape[1]
    expert_count = slot_tok.shape[2]
    slot_width = slot_tok.shape[3]
    hidden_width = w_gate.shape[2]
    own = gate_act.shape[2]
    slot_ids = slot_tok[0, 0]
    live_slots = jnp.arange(slot_width, dtype=jnp.int32)[None, :] < slot_count[0, 0][:, None]
    chosen = jnp.where(live_slots, slot_ids, -1).reshape(-1)
    token_index = jnp.arange(token_count, dtype=jnp.int32)
    table = jnp.where(chosen[:, None] == token_index[None, :], 1.0, 0.0).astype(BF16)
    send_cot = jnp.dot(table, moe_cot[0], preferred_element_type=F32).astype(BF16)
    send_weight = jnp.where(live_slots, route_w[0, 0], jnp.zeros((), BF16))
    send_weight = jnp.pad(send_weight[:, None, :], ((0, 0), (0, 15), (0, col_width - slot_width)))
    send_cot = send_cot.reshape(expert_count, slot_width, col_width)
    got_cot = exchange(jnp.concatenate([send_cot, send_weight], axis=1), "expert")
    send_in = jnp.dot(table, moe_in[0], preferred_element_type=F32).astype(BF16)
    rows_in = exchange(send_in.reshape(expert_count, slot_width, col_width), "expert")

    gains = jnp.stack([dt_bias, a_log, d_skip])
    pad_heads = ((8 + length, split_at), F32)
    pad_shared = ((8 + length, shared_width), F32)
    (states,) = whole(
        front_kernel,
        [((ctx_places, 2 * part + 16, state_width), BF16)],
        [pad_heads, pad_shared],
        inputs=8,
    )(head_rows, shared_rows, before, raw_step, gains, conv_x, conv_bc, cot_rows)
    three, one = (3 * own, hidden_width), (own, hidden_width)
    left2, right2, left1, right1, centre, opposite = whole(
        unscaled_kernel,
        [(three, BF16)] * 5 + [(one, BF16)],
        [((ctx_places * own, col_width), BF16)],
        inputs=2,
        scalars=1,
        late=1,
    )(place, got_cot, w_down[0], states)
    opposite = shift(opposite, 3)
    left1 = (left1.astype(F32) + shift(left2, -1).astype(F32)).astype(BF16)
    right1 = (right1.astype(F32) + shift(right2, 1).astype(F32)).astype(BF16)
    centre = centre.astype(F32) + shift(left1, -1).astype(F32) + shift(right1, 1).astype(F32)
    far_left = shift(centre[:own].astype(BF16), -FAR)
    far_right = shift((centre[2 * own :] + opposite.astype(F32)).astype(BF16), FAR)
    mine = centre[own : 2 * own] + far_left.astype(F32) + far_right.astype(F32)
    rows_weight = got_cot[:, slot_width, :slot_width].reshape(-1).astype(F32)
    weight_own = lax.dynamic_slice_in_dim(rows_weight, place[0] * own, own, 0)
    (own_rows,) = whole(
        own_rows_kernel, [((own, 3 * hidden_width + 128), BF16)], inputs=4, late=1
    )(mine, weight_own[:, None], gate_act[0, 0], up_act[0, 0], rows_in)
    everything = lax.all_gather(own_rows, "ctx", axis=0, tiled=True)

    got_states = exchange(after(states, own_rows), "ctx")
    (entered,) = whole(
        scan_kernel, [((ctx_places, 2 * part, state_width), BF16)], inputs=1
    )(got_states)

    entered = exchange(entered, "ctx")
    main_heads, tail_heads, rim_heads, grad_bc, grad_step, taps_heads, grad_rate = whole(
        back_kernel,
        [
            ((length, split_at), BF16),
            ((16, split_at), F32),
            ((8, split_at), F32),
            ((expert_places, length, shared_width), BF16),
            ((heads_here, length), F32),
            ((rim_rows + 1, split_at), F32),
            ((1, 128), F32),
        ],
        [pad_heads, pad_shared, ((16 + length, split_at), F32), ((heads_here, length), F32)],
        inputs=9,
        limit=48 * 2**20,
    )(
        head_rows, shared_rows, before, raw_step, gains, conv_x, conv_bc, cot_rows,
        entered,
    )
    after_heads = passed_along(rim_heads[:rim_rows], "ctx", -1)
    grad_mamba_in = with_last_rows(main_heads, tail_heads, after_heads)
    main_shared, tail_shared, rim_shared, taps_shared = whole(
        shared_kernel,
        [
            ((length, shared_width), BF16),
            ((16, shared_width), F32),
            ((8, shared_width), F32),
            ((rim_rows + 1, shared_width), F32),
        ],
        [pad_shared, ((16 + length, shared_width), F32)],
        inputs=4,
    )(shared_rows, before, conv_bc, exchange(grad_bc, "expert"))
    after_shared = passed_along(rim_shared[:rim_rows], "ctx", -1)
    grad_shared_in = with_last_rows(main_shared, tail_shared, after_shared)
    small = jnp.concatenate(
        [
            taps_heads,
            taps_shared,
            jnp.broadcast_to(grad_rate, (dp_count, 128)),
            jnp.zeros((dp_count, 128), F32),
        ],
        axis=1,
    )
    small = exchange(copies(small.reshape(dp_count * 8, 128), ctx_places), "ctx")

    share = hidden_width // dp_count
    block = ((3 * share, col_width), BF16)
    owner = lax.axis_index("dp").astype(jnp.int32).reshape(1)
    back, *parts = whole(
        rows_kernel,
        [((expert_count, slot_width + 16, col_width), BF16)] + [block] * dp_count,
        [((3, hidden_width, col_width), BF16)],
        inputs=5,
        scalars=1,
        late=1,
        limit=56 * 2**20,
    )(owner, everything, rows_in, got_cot, w_gate[0], w_up[0], main_shared)
    small = after(small, back, parts[0])
    back = exchange(after(back, small), "expert")
    small = jnp.sum(small, axis=0).reshape(dp_count, 8, 128)
    places = jnp.arange(dp_count, dtype=jnp.int32)[:, None, None]
    small = [
        jnp.sum(jnp.where(places == lax.rem(owner[0] + k, dp_count), small, 0.0), axis=0)
        for k in range(dp_count)
    ]
    small = small[0] + sum(
        lax.ppermute(small[k], "dp", [(i, (i + k) % dp_count) for i in range(dp_count)])
        for k in range(1, dp_count)
    )
    small = small.reshape(1, -1)
    taps_heads = small[:, :split_at]
    taps_shared = small[:, split_at : split_at + shared_width]
    rate_total = small[0, split_at + shared_width :][:heads_here]
    parts = [parts[0]] + [
        lax.ppermute(parts[k], "dp", [(i, (i + k) % dp_count) for i in range(dp_count)])
        for k in range(1, dp_count)
    ]
    gate_total, up_total, down_total = whole(
        totals_kernel, [((share, col_width), BF16)] * 3, inputs=dp_count
    )(*parts)
    grad_tokens = lax.dot_general(
        table,
        back[:, :slot_width].reshape(-1, col_width),
        (((0,), (0,)), ((), ())),
        preferred_element_type=F32,
    )
    route_got = back[:, slot_width].astype(F32)
    route_total = jnp.where(
        live_slots, route_got[:, :slot_width] + route_got[:, slot_width:], 0.0
    )
    return (
        grad_mamba_in[None],
        grad_shared_in[None],
        grad_step[None],
        taps_heads,
        taps_shared,
        rate_total,
        grad_tokens.astype(BF16)[None],
        route_total[None, None],
        gate_total.T[None],
        up_total.T[None],
        down_total[None],
    )


def solution(mesh):
    placed = (
        P("dp", "ctx", "expert"),
        P("dp", "ctx", None),
        P("dp", "expert", "ctx"),
        P("expert"),
        P("expert"),
        P("expert"),
        P(None, "expert"),
        P(),
        P("dp", "ctx", "expert"),
        P("dp", "expert", "ctx"),
        P("dp", "expert", "ctx"),
        P("dp", "expert", None, None),
        P("dp", "expert", None),
        P("dp", "expert", None, None),
        P("expert", "ctx", None),
        P("expert", "ctx", None),
        P("expert", None, "ctx"),
        P("dp", "expert", "ctx", None),
        P("dp", "expert", "ctx", None),
    )
    return jax.shard_map(
        body,
        mesh=mesh,
        in_specs=placed,
        out_specs=(
            P("dp", "ctx", "expert"),
            P("dp", "ctx", None),
            P("dp", "expert", "ctx"),
            P("dp", "expert"),
            P("dp", None),
            P("expert"),
            P("dp", "expert", "ctx"),
            P("dp", "expert", None, None),
            P("expert", "ctx", "dp"),
            P("expert", "ctx", "dp"),
            P("expert", "dp", "ctx"),
        ),
        check_vma=False,
    )
```

```python
import jax
import jax.numpy as jnp
from jax import lax
from jax.experimental import pallas as pl
from jax.experimental.pallas import tpu as pltpu
from jax.sharding import PartitionSpec as P

PRECISE = lax.Precision.HIGHEST
F32 = jnp.float32
BF16 = jnp.bfloat16


def passed_along(value, axis, steps):
    count = lax.axis_size(axis)
    first, last = (max(0, -steps), min(count, count - steps))
    return lax.ppermute(value, axis, [(source, source + steps) for source in range(first, last)])


def exchange(value, axis):
    return lax.all_to_all(value, axis, split_axis=0, concat_axis=0, tiled=True)


def after(value, *earlier):
    return lax.optimization_barrier((value,) + earlier)[0]


def copies(value, count):
    return jnp.broadcast_to(value[None], (count,) + value.shape)


def dot(a, b, ca, cb, precise=False):
    return lax.dot_general(
        a,
        b,
        (((ca,), (cb,)), ((), ())),
        precision=PRECISE if precise else None,
        preferred_element_type=F32,
    )


def iota(shape, axis):
    return lax.broadcasted_iota(jnp.int32, shape, axis)


def conv_pre(rows_ref, before, taps_ref, pad_ref):
    length, width = rows_ref.shape
    taps = taps_ref.shape[0]
    pad_ref[0:8, :] = jnp.zeros((8, width), F32)
    pad_ref[8 - (taps - 1) : 8, :] = before.astype(F32)
    pad_ref[8:, :] = rows_ref[...].astype(F32)
    pre = None
    for k in range(taps):
        start = 8 - (taps - 1) + k
        term = taps_ref[k : k + 1, :] * pad_ref[start : start + length, :]
        pre = term if pre is None else pre + term
    sig = jax.nn.sigmoid(pre)
    return pre, sig


def conv_pull(grad_pre, taps_ref, pad_ref, dv_ref):
    length, width = grad_pre.shape
    taps = taps_ref.shape[0]
    dv_ref[0:8, :] = jnp.zeros((8, width), F32)
    dv_ref[8 : 8 + length, :] = grad_pre
    dv_ref[8 + length :, :] = jnp.zeros((8, width), F32)
    rows = None
    rim = None
    sums = []
    for k in range(taps):
        weight = taps_ref[k : k + 1, :]
        start = 8 + (taps - 1) - k
        term = weight * dv_ref[start : start + length, :]
        rows = term if rows is None else rows + term
        edge = weight * dv_ref[8 - k : 16 - k, :]
        rim = edge if rim is None else rim + edge
        start = 8 - (taps - 1) + k
        sums.append(jnp.sum(grad_pre * pad_ref[start : start + length, :], axis=0, keepdims=True))
    rim = jnp.where(iota(rim.shape, 0) < taps - 1, rim, 0.0)
    return rows, rim, sums


def gain_column(gains_ref, which):
    heads = gains_ref.shape[1]
    eye = iota((heads, heads), 0) == iota((heads, heads), 1)
    return jnp.sum(jnp.where(eye, gains_ref[which : which + 1, :], 0.0), axis=1, keepdims=True)


def steps_of(raw_ref, gains_ref):
    shifted = raw_ref[...] + gain_column(gains_ref, 0)
    step = jnp.maximum(shifted, 0.0) + jnp.log1p(jnp.exp(-jnp.abs(shifted)))
    rate = jnp.exp(gain_column(gains_ref, 1))
    log_decay = -rate * step
    length = shifted.shape[1]
    square = (length, length)
    upto = jnp.where(iota(square, 0) <= iota(square, 1), 1.0, 0.0)
    cumulative = dot(log_decay, upto, 1, 0, True)
    return shifted, step, rate, log_decay, upto, cumulative


def head_spread(heads, width):
    spread = (heads, heads * width)
    return jnp.where(iota(spread, 1) // width == iota(spread, 0), 1.0, 0.0)


def front_kernel(
    rows_ref, shared_ref, before_ref, raw_ref, gains_ref, tapsx_ref,
    tapsbc_ref, cot_ref, out_ref, padh_ref, pads_ref,
):
    heads = raw_ref.shape[0]
    width = rows_ref.shape[1] // heads
    states = shared_ref.shape[1] // 2
    places = out_ref.shape[0]
    part = heads * width // places
    pre, sig = conv_pre(rows_ref, before_ref[:, : rows_ref.shape[1]], tapsx_ref, padh_ref)
    x = pre * sig
    before_s = before_ref[:, rows_ref.shape[1] :]
    pre_s, sig_s = conv_pre(shared_ref, before_s, tapsbc_ref, pads_ref)
    bc = (pre_s * sig_s).astype(BF16)
    _, step, _, _, _, cumulative = steps_of(raw_ref, gains_ref)
    length = step.shape[1]
    ending = cumulative[:, length - 1 :]
    spread = head_spread(heads, width)
    weight = dot(jnp.exp(ending - cumulative) * step, spread, 0, 0, True)
    grown = dot(jnp.exp(cumulative), spread, 0, 0, True)
    fresh = dot((x * weight).astype(BF16), bc[:, :states], 0, 0)
    pulls = dot((cot_ref[...].astype(F32) * grown).astype(BF16), bc[:, states:], 0, 0)
    out_ref[:, :part, :] = fresh.astype(BF16).reshape(places, part, states)
    out_ref[:, part : 2 * part, :] = pulls.astype(BF16).reshape(places, part, states)
    coarse = ending.astype(BF16).astype(F32)
    fine = ending - coarse
    per_head = places // heads
    mark = (16, states)
    for place in range(places):
        head = place // per_head
        marks = jnp.where(
            iota(mark, 0) == 0,
            jnp.broadcast_to(coarse[head : head + 1], mark),
            jnp.broadcast_to(fine[head : head + 1], mark),
        )
        out_ref[place, 2 * part :, :] = marks.astype(BF16)


def back_kernel(
    rows_ref, shared_ref, before_ref, raw_ref, gains_ref,
    tapsx_ref, tapsbc_ref, cot_ref, got_ref,
    main_ref, tail_ref, rim_ref, bc_ref, raw_out_ref, taps_out_ref, rate_out_ref,
    padh_ref, pads_ref, dv_ref, sums_ref,
):
    heads, length = raw_ref.shape
    width = rows_ref.shape[1] // heads
    states = shared_ref.shape[1] // 2
    part = got_ref.shape[1] // 2
    pre, sig = conv_pre(rows_ref, before_ref[:, : rows_ref.shape[1]], tapsx_ref, padh_ref)
    x = pre * sig
    before_s = before_ref[:, rows_ref.shape[1] :]
    pre_s, sig_s = conv_pre(shared_ref, before_s, tapsbc_ref, pads_ref)
    bc = (pre_s * sig_s).astype(BF16)
    b_rows, c_rows = bc[:, :states], bc[:, states:]
    shifted, step, rate, log_decay, upto, cumulative = steps_of(raw_ref, gains_ref)
    ending = cumulative[:, length - 1 :]
    spread = head_spread(heads, width)
    weight = dot(jnp.exp(ending - cumulative) * step, spread, 0, 0, True)
    grown = dot(jnp.exp(cumulative), spread, 0, 0, True)
    step_cols = dot(step, spread, 0, 0, True)
    skip_cols = jnp.sum(gain_column(gains_ref, 2) * spread, axis=0, keepdims=True)
    state_in = got_ref[:, :part, :].reshape(heads * width, states)
    pull_out = got_ref[:, part:, :].reshape(heads * width, states)
    cot = cot_ref[...]
    cot_wide = cot.astype(F32)
    b_pull = dot(b_rows, pull_out, 1, 1)
    c_state = dot(c_rows, state_in, 1, 1)
    cot_grown = cot_wide * grown
    x_weight = x * weight
    grad_c = dot(cot_grown.astype(BF16), state_in, 1, 0)
    grad_b = dot(x_weight.astype(BF16), pull_out, 1, 0)
    lane = (heads * width, 128)
    lane_of, head_of = iota(lane, 1), iota(lane, 0) // width
    pick = jnp.where((lane_of == head_of) | (lane_of == 2 * heads + head_of), 1.0, 0.0)
    pick_next = jnp.where(lane_of == heads + head_of, 1.0, 0.0)
    columns = dot(x_weight * b_pull, pick, 1, 0, True)
    columns = columns + dot(cot_grown * c_state, pick_next, 1, 0, True)
    scores = dot(b_rows, c_rows, 1, 1)
    square = (length, length)
    earlier = iota(square, 0) <= iota(square, 1)
    cumulative_cols = dot(upto, log_decay, 0, 1, True)
    x_step = (x * step_cols).astype(BF16)
    pair = max(1, 128 // width)
    block = pair * width
    lane_head = iota((length, block), 1) // width
    column_lane = iota((length, 128), 1)
    grad_scores = jnp.zeros(square, F32)
    inner = []
    for base in range(0, heads, pair):
        at = base * width
        x_pair = x_step[:, at : at + block]
        cot_pair = cot[:, at : at + block]
        sum_pair = None
        for i in range(pair):
            head = base + i
            cot_one = jnp.where(lane_head == i, cot_pair, jnp.zeros((), BF16))
            grad_mix = dot(x_pair, cot_one, 1, 1)
            gap = cumulative[head : head + 1, :] - cumulative_cols[:, head : head + 1]
            decay = jnp.exp(jnp.where(earlier, gap, -1e30))
            mix = decay * scores
            grad_scores = grad_scores + decay * grad_mix
            moved = mix * grad_mix
            sums_ref[head : head + 1, :] = jnp.sum(moved, axis=0, keepdims=True)
            columns = columns + jnp.where(
                column_lane == head, jnp.sum(moved, axis=1, keepdims=True), 0.0
            )
            term = dot(mix.astype(BF16), cot_one, 1, 0)
            sum_pair = term if sum_pair is None else sum_pair + term
        inner.append(sum_pair)
    inner = jnp.concatenate(inner, axis=1)
    grad_scores = grad_scores.astype(BF16)
    grad_b = grad_b + dot(grad_scores, c_rows, 1, 0)
    grad_c = grad_c + dot(grad_scores, b_rows, 0, 0)
    grad_bc = jnp.concatenate([grad_b, grad_c], axis=1).astype(BF16)
    for copy in range(bc_ref.shape[0]):
        bc_ref[copy] = grad_bc
    turned = columns.T
    left = turned[:heads]
    came = sums_ref[...] + turned[heads : 2 * heads]
    state_pull = state_in.astype(F32) * pull_out.astype(F32)
    state_pull = jnp.sum(state_pull.reshape(heads, width, states), axis=1)
    state_pull = jnp.exp(ending) * jnp.sum(state_pull, axis=1, keepdims=True)
    to_last = jnp.sum(turned[2 * heads : 3 * heads], axis=1, keepdims=True)
    grad_decay = dot(came - left, upto, 1, 1, True) + to_last + state_pull
    grad_step = left / step - rate * grad_decay
    raw_out_ref[...] = grad_step * jax.nn.sigmoid(shifted)
    grad_rate = jnp.sum(grad_decay * log_decay, axis=1, keepdims=True)
    eye = jnp.where(iota((heads, 128), 0) == iota((heads, 128), 1), 1.0, 0.0)
    rate_out_ref[...] = jnp.sum(grad_rate * eye, axis=0, keepdims=True)
    grad_x = inner * step_cols + skip_cols * cot_wide + weight * b_pull
    grad_pre = grad_x * (sig * (1.0 + pre * (1.0 - sig)))
    rows, rim, sums = conv_pull(grad_pre, tapsx_ref, padh_ref, dv_ref)
    main_ref[...] = rows.astype(BF16)
    tail_ref[...] = rows[length - 16 :]
    rim_ref[...] = rim
    for k, total in enumerate(sums):
        taps_out_ref[k : k + 1, :] = total


def shared_kernel(
    shared_ref, before_ref, tapsbc_ref, got_ref,
    main_ref, tail_ref, rim_ref, taps_out_ref, pads_ref, dv_ref,
):
    length = shared_ref.shape[0]
    before = before_ref[:, before_ref.shape[1] - shared_ref.shape[1] :]
    pre, sig = conv_pre(shared_ref, before, tapsbc_ref, pads_ref)
    total = got_ref[0].astype(F32)
    for source in range(1, got_ref.shape[0]):
        total = total + got_ref[source].astype(F32)
    grad_pre = total * (sig * (1.0 + pre * (1.0 - sig)))
    rows, rim, sums = conv_pull(grad_pre, tapsbc_ref, pads_ref, dv_ref)
    main_ref[...] = rows.astype(BF16)
    tail_ref[...] = rows[length - 16 :]
    rim_ref[...] = rim
    for k, value in enumerate(sums):
        taps_out_ref[k : k + 1, :] = value


def send_kernel(count_ref, slots_ref, weight_ref, cot_ref, out_ref):
    groups, slots = slots_ref.shape
    tokens, cols = cot_ref.shape
    chosen = []
    for group in range(groups):
        live = iota((1, slots), 1) < count_ref[group]
        ids = jnp.where(live, slots_ref[group : group + 1, :], -1)
        chosen.append(jnp.where(iota((tokens, slots), 0) == ids, 1.0, 0.0).astype(BF16))
        line = jnp.where(live, weight_ref[group : group + 1, :].astype(F32), 0.0)
        tile = jnp.concatenate([line, jnp.zeros((1, cols - slots), F32)], axis=1)
        out_ref[group, slots:, :] = jnp.broadcast_to(tile, (16, cols)).astype(BF16)
    rows = dot(jnp.concatenate(chosen, axis=1), cot_ref[...], 0, 0)
    out_ref[:, :slots, :] = rows.astype(BF16).reshape(groups, slots, cols)


def scaled_rows(cot_ref, group):
    slots = cot_ref.shape[1] - 16
    weight = cot_ref[group, slots:, :slots].astype(F32).T[:, 0:1]
    return (cot_ref[group, :slots, :].astype(F32) * weight).astype(BF16)


def own_rows_kernel(mine_ref, weight_ref, gate_ref, up_ref, first_ref, second_ref, out_ref):
    del first_ref, second_ref
    width = mine_ref.shape[1]
    unscaled = mine_ref[...].astype(F32)
    gate = gate_ref[...].astype(F32)
    up = up_ref[...].astype(F32)
    grad_hidden = weight_ref[...] * unscaled
    sig = jax.nn.sigmoid(gate)
    activated = gate * sig
    hidden = (activated * up).astype(BF16)
    slope = sig * (1.0 + gate * (1.0 - sig))
    out_ref[:, :width] = (grad_hidden * up * slope).astype(BF16)
    out_ref[:, width : 2 * width] = (grad_hidden * activated).astype(BF16)
    out_ref[:, 2 * width : 3 * width] = hidden
    route = jnp.sum(hidden.astype(F32) * unscaled, axis=1, keepdims=True)
    coarse = route.astype(BF16).astype(F32)
    lanes = (mine_ref.shape[0], 128)
    out_ref[:, 3 * width :] = jnp.where(
        iota(lanes, 1) == 0, coarse, jnp.where(iota(lanes, 1) == 1, route - coarse, 0.0)
    ).astype(BF16)


def rows_kernel(
    place_ref, all_ref, in_ref, cot_ref, gatew_ref, upw_ref, earlier_ref, back_ref, *refs
):
    del earlier_ref
    out_refs, grads_ref = refs[:-1], refs[-1]
    groups, slots, cols = in_ref.shape
    width = gatew_ref.shape[1]
    owners = len(out_refs)
    share = width // owners
    rows_grad = dot(all_ref[:, :width], gatew_ref[...], 1, 1)
    rows_grad = rows_grad + dot(all_ref[:, width : 2 * width], upw_ref[...], 1, 1)
    back_ref[:, :slots, :] = rows_grad.astype(BF16).reshape(groups, slots, cols)
    route = all_ref[:, 3 * width :].astype(F32)
    for group in range(groups):
        turned = route[group * slots : (group + 1) * slots].T
        line = jnp.concatenate([turned[0:1], turned[1:2]], axis=1)
        back_ref[group, slots:, :] = jnp.broadcast_to(line, (16, cols)).astype(BF16)
    rows_in = in_ref[...].reshape(groups * slots, cols)
    scaled = jnp.concatenate([scaled_rows(cot_ref, group) for group in range(groups)], axis=0)
    grads_ref[0] = dot(all_ref[:, :width], rows_in, 0, 0).astype(BF16)
    grads_ref[1] = dot(all_ref[:, width : 2 * width], rows_in, 0, 0).astype(BF16)
    grads_ref[2] = dot(all_ref[:, 2 * width : 3 * width], scaled, 0, 0).astype(BF16)
    for ahead in range(owners):
        owner = lax.rem(place_ref[0] + ahead, owners)
        start = pl.multiple_of(owner * share, 64)
        for kind in range(3):
            out_refs[ahead][kind * share : (kind + 1) * share, :] = grads_ref[
                kind, pl.ds(start, share), :
            ]


def totals_kernel(*refs):
    part_refs, out_refs = refs[:-4], refs[-3:]
    share = out_refs[0].shape[0]
    for kind, out_ref in enumerate(out_refs):
        span = slice(kind * share, (kind + 1) * share)
        value = part_refs[0][span, :].astype(F32)
        for part_ref in part_refs[1:]:
            value = value + part_ref[span, :].astype(F32)
        out_ref[...] = value.astype(BF16)


def scan_kernel(got_ref, out_ref):
    places, half = got_ref.shape[0], out_ref.shape[1] // 2
    width = got_ref.shape[2]
    decay = [
        jnp.exp(
            got_ref[j, 2 * half : 2 * half + 1, :].astype(F32)
            + got_ref[j, 2 * half + 1 : 2 * half + 2, :].astype(F32)
        )
        for j in range(places)
    ]
    state = jnp.zeros((half, width), F32)
    for j in range(places):
        out_ref[j, :half, :] = state.astype(BF16)
        state = decay[j] * state + got_ref[j, :half, :].astype(F32)
    state = jnp.zeros((half, width), F32)
    for j in reversed(range(places)):
        out_ref[j, half:, :] = state.astype(BF16)
        state = decay[j] * state + got_ref[j, half : 2 * half, :].astype(F32)


def whole(kernel, outs, scratch=(), inputs=0, scalars=0, late=0, limit=None):
    specs = [pl.BlockSpec(memory_space=pltpu.SMEM)] * scalars
    specs += [pl.BlockSpec(memory_space=pltpu.VMEM)] * inputs
    specs += [pl.BlockSpec(memory_space=pl.ANY)] * late
    return pl.pallas_call(
        kernel,
        out_shape=[jax.ShapeDtypeStruct(shape, kind) for shape, kind in outs],
        in_specs=specs,
        out_specs=[pl.BlockSpec(memory_space=pltpu.VMEM)] * len(outs),
        scratch_shapes=[pltpu.VMEM(shape, kind) for shape, kind in scratch],
        compiler_params=pltpu.CompilerParams(vmem_limit_bytes=limit),
    )


def with_last_rows(main, tail, after):
    rows = tail.shape[0]
    given = jnp.pad(after, ((rows - after.shape[0], 0), (0, 0)))
    return lax.dynamic_update_slice(
        main, (tail + given).astype(BF16), (main.shape[0] - rows, 0)
    )


def body(
    mamba_in,
    shared_in,
    dt_raw,
    dt_bias,
    a_log,
    d_skip,
    conv_x,
    conv_bc,
    mamba_cot,
    moe_in,
    moe_cot,
    slot_tok,
    slot_count,
    route_w,
    w_gate,
    w_up,
    w_down,
    gate_act,
    up_act,
):
    dp_count, expert_places, ctx_places = (
        lax.axis_size("dp"),
        lax.axis_size("expert"),
        lax.axis_size("ctx"),
    )
    place = lax.axis_index("ctx").astype(jnp.int32).reshape(1)
    rim_rows = conv_x.shape[0] - 1
    head_rows = mamba_in[0]
    shared_rows = shared_in[0]
    cot_rows = mamba_cot[0]
    raw_step = dt_raw[0]
    length, split_at = head_rows.shape
    shared_width = shared_rows.shape[1]
    state_width = shared_width // 2
    heads_here = dt_bias.shape[0]
    part = split_at // ctx_places
    before = passed_along(
        jnp.concatenate([head_rows[length - rim_rows :], shared_rows[length - rim_rows :]], axis=1),
        "ctx",
        1,
    )
    col_width = moe_in.shape[2]
    token_count = moe_in.shape[1]
    expert_count = slot_tok.shape[2]
    slot_width = slot_tok.shape[3]
    hidden_width = w_gate.shape[2]
    own = gate_act.shape[2]
    slot_ids = slot_tok[0, 0]
    live_slots = jnp.arange(slot_width, dtype=jnp.int32)[None, :] < slot_count[0, 0][:, None]
    chosen = jnp.where(live_slots, slot_ids, -1).reshape(-1)
    token_index = jnp.arange(token_count, dtype=jnp.int32)
    table = jnp.where(chosen[:, None] == token_index[None, :], 1.0, 0.0).astype(BF16)
    (send_cot,) = whole(
        send_kernel,
        [((expert_count, slot_width + 16, col_width), BF16)],
        inputs=3,
        scalars=1,
    )(slot_count[0, 0], slot_ids, route_w[0, 0], moe_cot[0])
    got_cot = exchange(send_cot, "expert")
    send_in = jnp.dot(table, moe_in[0], preferred_element_type=F32).astype(BF16)

    gains = jnp.stack([dt_bias, a_log, d_skip])
    pad_heads = ((8 + length, split_at), F32)
    pad_shared = ((8 + length, shared_width), F32)
    (states,) = whole(
        front_kernel,
        [((ctx_places, 2 * part + 16, state_width), BF16)],
        [pad_heads, pad_shared],
        inputs=8,
    )(head_rows, shared_rows, before, raw_step, gains, conv_x, conv_bc, cot_rows)
    unscaled = jnp.dot(
        after(got_cot, states)[:, :slot_width].reshape(-1, col_width), w_down[0].T, preferred_element_type=F32
    ).astype(BF16)
    mine = lax.psum_scatter(unscaled, "ctx", scatter_dimension=0, tiled=True)
    got_states = exchange(after(states, unscaled), "ctx")
    (entered,) = whole(
        scan_kernel, [((ctx_places, 2 * part, state_width), BF16)], inputs=1
    )(got_states)

    entered = exchange(entered, "ctx")
    send_in = after(send_in.reshape(expert_count, slot_width, col_width), entered)
    rows_in = exchange(send_in, "expert")

    main_heads, tail_heads, rim_heads, grad_bc, grad_step, taps_heads, grad_rate = whole(
        back_kernel,
        [
            ((length, split_at), BF16),
            ((16, split_at), F32),
            ((8, split_at), F32),
            ((expert_places, length, shared_width), BF16),
            ((heads_here, length), F32),
            ((rim_rows + 1, split_at), F32),
            ((1, 128), F32),
        ],
        [pad_heads, pad_shared, ((16 + length, split_at), F32), ((heads_here, length), F32)],
        inputs=9,
        limit=48 * 2**20,
    )(
        head_rows, shared_rows, before, raw_step, gains, conv_x, conv_bc, cot_rows,
        entered,
    )
    rows_weight = got_cot[:, slot_width, :slot_width].reshape(-1).astype(F32)
    weight_own = lax.dynamic_slice_in_dim(rows_weight, place[0] * own, own, 0)
    (own_rows,) = whole(
        own_rows_kernel, [((own, 3 * hidden_width + 128), BF16)], inputs=4, late=2
    )(mine, weight_own[:, None], gate_act[0, 0], up_act[0, 0], grad_step, rows_in)
    everything = lax.all_gather(own_rows, "ctx", axis=0, tiled=True)
    grad_bc = after(grad_bc, rows_in)
    after_heads = passed_along(rim_heads[:rim_rows], "ctx", -1)
    grad_mamba_in = with_last_rows(main_heads, tail_heads, after_heads)
    main_shared, tail_shared, rim_shared, taps_shared = whole(
        shared_kernel,
        [
            ((length, shared_width), BF16),
            ((16, shared_width), F32),
            ((8, shared_width), F32),
            ((rim_rows + 1, shared_width), F32),
        ],
        [pad_shared, ((16 + length, shared_width), F32)],
        inputs=4,
    )(shared_rows, before, conv_bc, exchange(grad_bc, "expert"))
    after_shared = passed_along(rim_shared[:rim_rows], "ctx", -1)
    grad_shared_in = with_last_rows(main_shared, tail_shared, after_shared)
    small = jnp.concatenate(
        [
            taps_heads,
            taps_shared,
            jnp.broadcast_to(grad_rate, (dp_count, 128)),
            jnp.zeros((dp_count, 128), F32),
        ],
        axis=1,
    )
    small = jnp.sum(exchange(small.reshape(dp_count, 8, 128), "dp"), axis=0)
    small = jnp.sum(exchange(copies(small, ctx_places), "ctx"), axis=0).reshape(1, -1)
    taps_heads = small[:, :split_at]
    taps_shared = small[:, split_at : split_at + shared_width]
    rate_total = small[0, split_at + shared_width :][:heads_here]

    share = hidden_width // dp_count
    block = ((3 * share, col_width), BF16)
    owner = lax.axis_index("dp").astype(jnp.int32).reshape(1)
    back, *parts = whole(
        rows_kernel,
        [((expert_count, slot_width + 16, col_width), BF16)] + [block] * dp_count,
        [((3, hidden_width, col_width), BF16)],
        inputs=5,
        scalars=1,
        late=1,
        limit=56 * 2**20,
    )(owner, everything, rows_in, got_cot, w_gate[0], w_up[0], small)
    back = exchange(back, "expert")
    parts = [parts[0]] + [
        lax.ppermute(parts[k], "dp", [(i, (i + k) % dp_count) for i in range(dp_count)])
        for k in range(1, dp_count)
    ]
    grad_tokens = lax.dot_general(
        table,
        back[:, :slot_width].reshape(-1, col_width),
        (((0,), (0,)), ((), ())),
        preferred_element_type=F32,
    ).astype(BF16)
    gate_total, up_total, down_total = whole(
        totals_kernel, [((share, col_width), BF16)] * 3, inputs=dp_count, late=1
    )(*parts, grad_tokens)
    route_got = back[:, slot_width].astype(F32)
    route_total = jnp.where(
        live_slots, route_got[:, :slot_width] + route_got[:, slot_width:], 0.0
    )
    return (
        grad_mamba_in[None],
        grad_shared_in[None],
        grad_step[None],
        taps_heads,
        taps_shared,
        rate_total,
        grad_tokens[None],
        route_total[None, None],
        gate_total.T[None],
        up_total.T[None],
        down_total[None],
    )


def solution(mesh):
    placed = (
        P("dp", "ctx", "expert"),
        P("dp", "ctx", None),
        P("dp", "expert", "ctx"),
        P("expert"),
        P("expert"),
        P("expert"),
        P(None, "expert"),
        P(),
        P("dp", "ctx", "expert"),
        P("dp", "expert", "ctx"),
        P("dp", "expert", "ctx"),
        P("dp", "expert", None, None),
        P("dp", "expert", None),
        P("dp", "expert", None, None),
        P("expert", "ctx", None),
        P("expert", "ctx", None),
        P("expert", None, "ctx"),
        P("dp", "expert", "ctx", None),
        P("dp", "expert", "ctx", None),
    )
    return jax.shard_map(
        body,
        mesh=mesh,
        in_specs=placed,
        out_specs=(
            P("dp", "ctx", "expert"),
            P("dp", "ctx", None),
            P("dp", "expert", "ctx"),
            P("dp", "expert"),
            P("dp", None),
            P("expert"),
            P("dp", "expert", "ctx"),
            P("dp", "expert", None, None),
            P("expert", "ctx", "dp"),
            P("expert", "ctx", "dp"),
            P("expert", "dp", "ctx"),
        ),
        check_vma=False,
    )
```

```python
import jax
import jax.numpy as jnp
from jax import lax
from jax.experimental import pallas as pl
from jax.experimental.pallas import tpu as pltpu
from jax.sharding import PartitionSpec as P

PRECISE = lax.Precision.HIGHEST
F32 = jnp.float32
BF16 = jnp.bfloat16


def passed_along(value, axis, steps):
    count = lax.axis_size(axis)
    first, last = (max(0, -steps), min(count, count - steps))
    return lax.ppermute(value, axis, [(source, source + steps) for source in range(first, last)])


def exchange(value, axis):
    return lax.all_to_all(value, axis, split_axis=0, concat_axis=0, tiled=True)


def after(value, *earlier):
    return lax.optimization_barrier((value,) + earlier)[0]


def copies(value, count):
    return jnp.broadcast_to(value[None], (count,) + value.shape)


def dot(a, b, ca, cb, precise=False):
    return lax.dot_general(
        a,
        b,
        (((ca,), (cb,)), ((), ())),
        precision=PRECISE if precise else None,
        preferred_element_type=F32,
    )


def iota(shape, axis):
    return lax.broadcasted_iota(jnp.int32, shape, axis)


def conv_pre(rows_ref, before, taps_ref, pad_ref):
    length, width = rows_ref.shape
    taps = taps_ref.shape[0]
    pad_ref[0:8, :] = jnp.zeros((8, width), F32)
    pad_ref[8 - (taps - 1) : 8, :] = before.astype(F32)
    pad_ref[8:, :] = rows_ref[...].astype(F32)
    pre = None
    for k in range(taps):
        start = 8 - (taps - 1) + k
        term = taps_ref[k : k + 1, :] * pad_ref[start : start + length, :]
        pre = term if pre is None else pre + term
    sig = jax.nn.sigmoid(pre)
    return pre, sig


def conv_pull(grad_pre, taps_ref, pad_ref, dv_ref):
    length, width = grad_pre.shape
    taps = taps_ref.shape[0]
    dv_ref[0:8, :] = jnp.zeros((8, width), F32)
    dv_ref[8 : 8 + length, :] = grad_pre
    dv_ref[8 + length :, :] = jnp.zeros((8, width), F32)
    rows = None
    rim = None
    sums = []
    for k in range(taps):
        weight = taps_ref[k : k + 1, :]
        start = 8 + (taps - 1) - k
        term = weight * dv_ref[start : start + length, :]
        rows = term if rows is None else rows + term
        edge = weight * dv_ref[8 - k : 16 - k, :]
        rim = edge if rim is None else rim + edge
        start = 8 - (taps - 1) + k
        sums.append(jnp.sum(grad_pre * pad_ref[start : start + length, :], axis=0, keepdims=True))
    rim = jnp.where(iota(rim.shape, 0) < taps - 1, rim, 0.0)
    return rows, rim, sums


def gain_column(gains_ref, which):
    heads = gains_ref.shape[1]
    eye = iota((heads, heads), 0) == iota((heads, heads), 1)
    return jnp.sum(jnp.where(eye, gains_ref[which : which + 1, :], 0.0), axis=1, keepdims=True)


def steps_of(raw_ref, gains_ref):
    shifted = raw_ref[...] + gain_column(gains_ref, 0)
    step = jnp.maximum(shifted, 0.0) + jnp.log1p(jnp.exp(-jnp.abs(shifted)))
    rate = jnp.exp(gain_column(gains_ref, 1))
    log_decay = -rate * step
    length = shifted.shape[1]
    square = (length, length)
    upto = jnp.where(iota(square, 0) <= iota(square, 1), 1.0, 0.0)
    cumulative = dot(log_decay, upto, 1, 0, True)
    return shifted, step, rate, log_decay, upto, cumulative


def head_spread(heads, width):
    spread = (heads, heads * width)
    return jnp.where(iota(spread, 1) // width == iota(spread, 0), 1.0, 0.0)


def front_kernel(
    rows_ref, shared_ref, before_ref, raw_ref, gains_ref, tapsx_ref,
    tapsbc_ref, cot_ref, out_ref, padh_ref, pads_ref,
):
    heads = raw_ref.shape[0]
    width = rows_ref.shape[1] // heads
    states = shared_ref.shape[1] // 2
    places = out_ref.shape[0]
    part = heads * width // places
    pre, sig = conv_pre(rows_ref, before_ref[:, : rows_ref.shape[1]], tapsx_ref, padh_ref)
    x = pre * sig
    before_s = before_ref[:, rows_ref.shape[1] :]
    pre_s, sig_s = conv_pre(shared_ref, before_s, tapsbc_ref, pads_ref)
    bc = (pre_s * sig_s).astype(BF16)
    _, step, _, _, _, cumulative = steps_of(raw_ref, gains_ref)
    length = step.shape[1]
    ending = cumulative[:, length - 1 :]
    spread = head_spread(heads, width)
    weight = dot(jnp.exp(ending - cumulative) * step, spread, 0, 0, True)
    grown = dot(jnp.exp(cumulative), spread, 0, 0, True)
    fresh = dot((x * weight).astype(BF16), bc[:, :states], 0, 0)
    pulls = dot((cot_ref[...].astype(F32) * grown).astype(BF16), bc[:, states:], 0, 0)
    out_ref[:, :part, :] = fresh.astype(BF16).reshape(places, part, states)
    out_ref[:, part : 2 * part, :] = pulls.astype(BF16).reshape(places, part, states)
    coarse = ending.astype(BF16).astype(F32)
    fine = ending - coarse
    per_head = places // heads
    mark = (16, states)
    for place in range(places):
        head = place // per_head
        marks = jnp.where(
            iota(mark, 0) == 0,
            jnp.broadcast_to(coarse[head : head + 1], mark),
            jnp.broadcast_to(fine[head : head + 1], mark),
        )
        out_ref[place, 2 * part :, :] = marks.astype(BF16)


def back_kernel(
    rows_ref, shared_ref, before_ref, raw_ref, gains_ref,
    tapsx_ref, tapsbc_ref, cot_ref, got_ref,
    main_ref, tail_ref, rim_ref, bc_ref, raw_out_ref, taps_out_ref, rate_out_ref,
    padh_ref, pads_ref, dv_ref, sums_ref,
):
    heads, length = raw_ref.shape
    width = rows_ref.shape[1] // heads
    states = shared_ref.shape[1] // 2
    part = got_ref.shape[1] // 2
    pre, sig = conv_pre(rows_ref, before_ref[:, : rows_ref.shape[1]], tapsx_ref, padh_ref)
    x = pre * sig
    before_s = before_ref[:, rows_ref.shape[1] :]
    pre_s, sig_s = conv_pre(shared_ref, before_s, tapsbc_ref, pads_ref)
    bc = (pre_s * sig_s).astype(BF16)
    b_rows, c_rows = bc[:, :states], bc[:, states:]
    shifted, step, rate, log_decay, upto, cumulative = steps_of(raw_ref, gains_ref)
    ending = cumulative[:, length - 1 :]
    spread = head_spread(heads, width)
    weight = dot(jnp.exp(ending - cumulative) * step, spread, 0, 0, True)
    grown = dot(jnp.exp(cumulative), spread, 0, 0, True)
    step_cols = dot(step, spread, 0, 0, True)
    skip_cols = jnp.sum(gain_column(gains_ref, 2) * spread, axis=0, keepdims=True)
    state_in = got_ref[:, :part, :].reshape(heads * width, states)
    pull_out = got_ref[:, part:, :].reshape(heads * width, states)
    cot = cot_ref[...]
    cot_wide = cot.astype(F32)
    b_pull = dot(b_rows, pull_out, 1, 1)
    c_state = dot(c_rows, state_in, 1, 1)
    cot_grown = cot_wide * grown
    x_weight = x * weight
    grad_c = dot(cot_grown.astype(BF16), state_in, 1, 0)
    grad_b = dot(x_weight.astype(BF16), pull_out, 1, 0)
    lane = (heads * width, 128)
    lane_of, head_of = iota(lane, 1), iota(lane, 0) // width
    pick = jnp.where((lane_of == head_of) | (lane_of == 2 * heads + head_of), 1.0, 0.0)
    pick_next = jnp.where(lane_of == heads + head_of, 1.0, 0.0)
    columns = dot(x_weight * b_pull, pick, 1, 0, True)
    columns = columns + dot(cot_grown * c_state, pick_next, 1, 0, True)
    scores = dot(b_rows, c_rows, 1, 1)
    square = (length, length)
    earlier = iota(square, 0) <= iota(square, 1)
    cumulative_cols = dot(upto, log_decay, 0, 1, True)
    x_step = (x * step_cols).astype(BF16)
    pair = max(1, 128 // width)
    block = pair * width
    lane_head = iota((length, block), 1) // width
    column_lane = iota((length, 128), 1)
    grad_scores = jnp.zeros(square, F32)
    inner = []
    for base in range(0, heads, pair):
        at = base * width
        x_pair = x_step[:, at : at + block]
        cot_pair = cot[:, at : at + block]
        sum_pair = None
        for i in range(pair):
            head = base + i
            cot_one = jnp.where(lane_head == i, cot_pair, jnp.zeros((), BF16))
            grad_mix = dot(x_pair, cot_one, 1, 1)
            gap = cumulative[head : head + 1, :] - cumulative_cols[:, head : head + 1]
            decay = jnp.exp(jnp.where(earlier, gap, -1e30))
            mix = decay * scores
            grad_scores = grad_scores + decay * grad_mix
            moved = mix * grad_mix
            sums_ref[head : head + 1, :] = jnp.sum(moved, axis=0, keepdims=True)
            columns = columns + jnp.where(
                column_lane == head, jnp.sum(moved, axis=1, keepdims=True), 0.0
            )
            term = dot(mix.astype(BF16), cot_one, 1, 0)
            sum_pair = term if sum_pair is None else sum_pair + term
        inner.append(sum_pair)
    inner = jnp.concatenate(inner, axis=1)
    grad_scores = grad_scores.astype(BF16)
    grad_b = grad_b + dot(grad_scores, c_rows, 1, 0)
    grad_c = grad_c + dot(grad_scores, b_rows, 0, 0)
    grad_bc = jnp.concatenate([grad_b, grad_c], axis=1).astype(BF16)
    for copy in range(bc_ref.shape[0]):
        bc_ref[copy] = grad_bc
    turned = columns.T
    left = turned[:heads]
    came = sums_ref[...] + turned[heads : 2 * heads]
    state_pull = state_in.astype(F32) * pull_out.astype(F32)
    state_pull = jnp.sum(state_pull.reshape(heads, width, states), axis=1)
    state_pull = jnp.exp(ending) * jnp.sum(state_pull, axis=1, keepdims=True)
    to_last = jnp.sum(turned[2 * heads : 3 * heads], axis=1, keepdims=True)
    grad_decay = dot(came - left, upto, 1, 1, True) + to_last + state_pull
    grad_step = left / step - rate * grad_decay
    raw_out_ref[...] = grad_step * jax.nn.sigmoid(shifted)
    grad_rate = jnp.sum(grad_decay * log_decay, axis=1, keepdims=True)
    eye = jnp.where(iota((heads, 128), 0) == iota((heads, 128), 1), 1.0, 0.0)
    rate_out_ref[...] = jnp.sum(grad_rate * eye, axis=0, keepdims=True)
    grad_x = inner * step_cols + skip_cols * cot_wide + weight * b_pull
    grad_pre = grad_x * (sig * (1.0 + pre * (1.0 - sig)))
    rows, rim, sums = conv_pull(grad_pre, tapsx_ref, padh_ref, dv_ref)
    main_ref[...] = rows.astype(BF16)
    tail_ref[...] = rows[length - 16 :]
    rim_ref[...] = rim
    for k, total in enumerate(sums):
        taps_out_ref[k : k + 1, :] = total


def shared_kernel(
    shared_ref, before_ref, tapsbc_ref, got_ref,
    main_ref, tail_ref, rim_ref, taps_out_ref, pads_ref, dv_ref,
):
    length = shared_ref.shape[0]
    before = before_ref[:, before_ref.shape[1] - shared_ref.shape[1] :]
    pre, sig = conv_pre(shared_ref, before, tapsbc_ref, pads_ref)
    total = got_ref[0].astype(F32)
    for source in range(1, got_ref.shape[0]):
        total = total + got_ref[source].astype(F32)
    grad_pre = total * (sig * (1.0 + pre * (1.0 - sig)))
    rows, rim, sums = conv_pull(grad_pre, tapsbc_ref, pads_ref, dv_ref)
    main_ref[...] = rows.astype(BF16)
    tail_ref[...] = rows[length - 16 :]
    rim_ref[...] = rim
    for k, value in enumerate(sums):
        taps_out_ref[k : k + 1, :] = value


def send_kernel(count_ref, slots_ref, weight_ref, cot_ref, out_ref):
    groups, slots = slots_ref.shape
    tokens, cols = cot_ref.shape
    chosen = []
    for group in range(groups):
        live = iota((1, slots), 1) < count_ref[group]
        ids = jnp.where(live, slots_ref[group : group + 1, :], -1)
        chosen.append(jnp.where(iota((tokens, slots), 0) == ids, 1.0, 0.0).astype(BF16))
        line = jnp.where(live, weight_ref[group : group + 1, :].astype(F32), 0.0)
        tile = jnp.concatenate([line, jnp.zeros((1, cols - slots), F32)], axis=1)
        out_ref[group, slots:, :] = jnp.broadcast_to(tile, (16, cols)).astype(BF16)
    rows = dot(jnp.concatenate(chosen, axis=1), cot_ref[...], 0, 0)
    out_ref[:, :slots, :] = rows.astype(BF16).reshape(groups, slots, cols)


def scaled_rows(cot_ref, group):
    slots = cot_ref.shape[1] - 16
    weight = cot_ref[group, slots:, :slots].astype(F32).T[:, 0:1]
    return (cot_ref[group, :slots, :].astype(F32) * weight).astype(BF16)


def own_rows_kernel(mine_ref, weight_ref, gate_ref, up_ref, first_ref, second_ref, out_ref):
    del first_ref, second_ref
    width = mine_ref.shape[1]
    unscaled = mine_ref[...].astype(F32)
    gate = gate_ref[...].astype(F32)
    up = up_ref[...].astype(F32)
    grad_hidden = weight_ref[...] * unscaled
    sig = jax.nn.sigmoid(gate)
    activated = gate * sig
    hidden = (activated * up).astype(BF16)
    slope = sig * (1.0 + gate * (1.0 - sig))
    out_ref[:, :width] = (grad_hidden * up * slope).astype(BF16)
    out_ref[:, width : 2 * width] = (grad_hidden * activated).astype(BF16)
    out_ref[:, 2 * width : 3 * width] = hidden
    route = jnp.sum(hidden.astype(F32) * unscaled, axis=1, keepdims=True)
    coarse = route.astype(BF16).astype(F32)
    lanes = (mine_ref.shape[0], 128)
    out_ref[:, 3 * width :] = jnp.where(
        iota(lanes, 1) == 0, coarse, jnp.where(iota(lanes, 1) == 1, route - coarse, 0.0)
    ).astype(BF16)


def rows_kernel(place_ref, all_ref, in_ref, cot_ref, gatew_ref, upw_ref, *refs):
    back_ref, out_refs, grads_ref = refs[-6], refs[-5:-1], refs[-1]
    groups, slots, cols = in_ref.shape
    width = gatew_ref.shape[1]
    owners = len(out_refs)
    share = width // owners
    rows_grad = dot(all_ref[:, :width], gatew_ref[...], 1, 1)
    rows_grad = rows_grad + dot(all_ref[:, width : 2 * width], upw_ref[...], 1, 1)
    back_ref[:, :slots, :] = rows_grad.astype(BF16).reshape(groups, slots, cols)
    route = all_ref[:, 3 * width :].astype(F32)
    for group in range(groups):
        turned = route[group * slots : (group + 1) * slots].T
        line = jnp.concatenate([turned[0:1], turned[1:2]], axis=1)
        back_ref[group, slots:, :] = jnp.broadcast_to(line, (16, cols)).astype(BF16)
    rows_in = in_ref[...].reshape(groups * slots, cols)
    scaled = jnp.concatenate([scaled_rows(cot_ref, group) for group in range(groups)], axis=0)
    grads_ref[0] = dot(all_ref[:, :width], rows_in, 0, 0).astype(BF16)
    grads_ref[1] = dot(all_ref[:, width : 2 * width], rows_in, 0, 0).astype(BF16)
    grads_ref[2] = dot(all_ref[:, 2 * width : 3 * width], scaled, 0, 0).astype(BF16)
    for ahead in range(owners):
        owner = lax.rem(place_ref[0] + ahead, owners)
        start = pl.multiple_of(owner * share, 64)
        for kind in range(3):
            out_refs[ahead][kind * share : (kind + 1) * share, :] = grads_ref[
                kind, pl.ds(start, share), :
            ]


def totals_kernel(*refs):
    part_refs, out_refs = refs[:-4], refs[-3:]
    share = out_refs[0].shape[0]
    for kind, out_ref in enumerate(out_refs):
        span = slice(kind * share, (kind + 1) * share)
        value = part_refs[0][span, :].astype(F32)
        for part_ref in part_refs[1:]:
            value = value + part_ref[span, :].astype(F32)
        out_ref[...] = value.astype(BF16)


def scan_kernel(got_ref, out_ref):
    places, half = got_ref.shape[0], out_ref.shape[1] // 2
    width = got_ref.shape[2]
    decay = [
        jnp.exp(
            got_ref[j, 2 * half : 2 * half + 1, :].astype(F32)
            + got_ref[j, 2 * half + 1 : 2 * half + 2, :].astype(F32)
        )
        for j in range(places)
    ]
    state = jnp.zeros((half, width), F32)
    for j in range(places):
        out_ref[j, :half, :] = state.astype(BF16)
        state = decay[j] * state + got_ref[j, :half, :].astype(F32)
    state = jnp.zeros((half, width), F32)
    for j in reversed(range(places)):
        out_ref[j, half:, :] = state.astype(BF16)
        state = decay[j] * state + got_ref[j, half : 2 * half, :].astype(F32)


def whole(kernel, outs, scratch=(), inputs=0, scalars=0, late=0, limit=None):
    specs = [pl.BlockSpec(memory_space=pltpu.SMEM)] * scalars
    specs += [pl.BlockSpec(memory_space=pltpu.VMEM)] * inputs
    specs += [pl.BlockSpec(memory_space=pl.ANY)] * late
    return pl.pallas_call(
        kernel,
        out_shape=[jax.ShapeDtypeStruct(shape, kind) for shape, kind in outs],
        in_specs=specs,
        out_specs=[pl.BlockSpec(memory_space=pltpu.VMEM)] * len(outs),
        scratch_shapes=[pltpu.VMEM(shape, kind) for shape, kind in scratch],
        compiler_params=pltpu.CompilerParams(vmem_limit_bytes=limit),
    )


def with_last_rows(main, tail, after):
    rows = tail.shape[0]
    given = jnp.pad(after, ((rows - after.shape[0], 0), (0, 0)))
    return lax.dynamic_update_slice(
        main, (tail + given).astype(BF16), (main.shape[0] - rows, 0)
    )


def body(
    mamba_in,
    shared_in,
    dt_raw,
    dt_bias,
    a_log,
    d_skip,
    conv_x,
    conv_bc,
    mamba_cot,
    moe_in,
    moe_cot,
    slot_tok,
    slot_count,
    route_w,
    w_gate,
    w_up,
    w_down,
    gate_act,
    up_act,
):
    dp_count, expert_places, ctx_places = (
        lax.axis_size("dp"),
        lax.axis_size("expert"),
        lax.axis_size("ctx"),
    )
    place = lax.axis_index("ctx").astype(jnp.int32).reshape(1)
    rim_rows = conv_x.shape[0] - 1
    head_rows = mamba_in[0]
    shared_rows = shared_in[0]
    cot_rows = mamba_cot[0]
    raw_step = dt_raw[0]
    length, split_at = head_rows.shape
    shared_width = shared_rows.shape[1]
    state_width = shared_width // 2
    heads_here = dt_bias.shape[0]
    part = split_at // ctx_places
    before = passed_along(
        jnp.concatenate([head_rows[length - rim_rows :], shared_rows[length - rim_rows :]], axis=1),
        "ctx",
        1,
    )
    col_width = moe_in.shape[2]
    token_count = moe_in.shape[1]
    expert_count = slot_tok.shape[2]
    slot_width = slot_tok.shape[3]
    hidden_width = w_gate.shape[2]
    own = gate_act.shape[2]
    slot_ids = slot_tok[0, 0]
    live_slots = jnp.arange(slot_width, dtype=jnp.int32)[None, :] < slot_count[0, 0][:, None]
    chosen = jnp.where(live_slots, slot_ids, -1).reshape(-1)
    token_index = jnp.arange(token_count, dtype=jnp.int32)
    table = jnp.where(chosen[:, None] == token_index[None, :], 1.0, 0.0).astype(BF16)
    (send_cot,) = whole(
        send_kernel,
        [((expert_count, slot_width + 16, col_width), BF16)],
        inputs=3,
        scalars=1,
    )(slot_count[0, 0], slot_ids, route_w[0, 0], moe_cot[0])
    got_cot = exchange(send_cot, "expert")
    send_in = jnp.dot(table, moe_in[0], preferred_element_type=F32).astype(BF16)

    gains = jnp.stack([dt_bias, a_log, d_skip])
    pad_heads = ((8 + length, split_at), F32)
    pad_shared = ((8 + length, shared_width), F32)
    (states,) = whole(
        front_kernel,
        [((ctx_places, 2 * part + 16, state_width), BF16)],
        [pad_heads, pad_shared],
        inputs=8,
    )(head_rows, shared_rows, before, raw_step, gains, conv_x, conv_bc, cot_rows)
    unscaled = jnp.dot(
        after(got_cot, states)[:, :slot_width].reshape(-1, col_width), w_down[0].T, preferred_element_type=F32
    ).astype(BF16)
    mine = lax.psum_scatter(unscaled, "ctx", scatter_dimension=0, tiled=True)
    got_states = exchange(after(states, unscaled), "ctx")
    (entered,) = whole(
        scan_kernel, [((ctx_places, 2 * part, state_width), BF16)], inputs=1
    )(got_states)

    entered = exchange(entered, "ctx")
    send_in = after(send_in.reshape(expert_count, slot_width, col_width), entered)
    rows_in = exchange(send_in, "expert")

    main_heads, tail_heads, rim_heads, grad_bc, grad_step, taps_heads, grad_rate = whole(
        back_kernel,
        [
            ((length, split_at), BF16),
            ((16, split_at), F32),
            ((8, split_at), F32),
            ((expert_places, length, shared_width), BF16),
            ((heads_here, length), F32),
            ((rim_rows + 1, split_at), F32),
            ((1, 128), F32),
        ],
        [pad_heads, pad_shared, ((16 + length, split_at), F32), ((heads_here, length), F32)],
        inputs=9,
        limit=48 * 2**20,
    )(
        head_rows, shared_rows, before, raw_step, gains, conv_x, conv_bc, cot_rows,
        entered,
    )
    rows_weight = got_cot[:, slot_width, :slot_width].reshape(-1).astype(F32)
    weight_own = lax.dynamic_slice_in_dim(rows_weight, place[0] * own, own, 0)
    (own_rows,) = whole(
        own_rows_kernel, [((own, 3 * hidden_width + 128), BF16)], inputs=4, late=2
    )(mine, weight_own[:, None], gate_act[0, 0], up_act[0, 0], grad_step, rows_in)
    everything = lax.all_gather(own_rows, "ctx", axis=0, tiled=True)
    grad_bc = after(grad_bc, rows_in)
    after_heads = passed_along(rim_heads[:rim_rows], "ctx", -1)
    grad_mamba_in = with_last_rows(main_heads, tail_heads, after_heads)
    main_shared, tail_shared, rim_shared, taps_shared = whole(
        shared_kernel,
        [
            ((length, shared_width), BF16),
            ((16, shared_width), F32),
            ((8, shared_width), F32),
            ((rim_rows + 1, shared_width), F32),
        ],
        [pad_shared, ((16 + length, shared_width), F32)],
        inputs=4,
    )(shared_rows, before, conv_bc, exchange(grad_bc, "expert"))
    after_shared = passed_along(rim_shared[:rim_rows], "ctx", -1)
    grad_shared_in = with_last_rows(main_shared, tail_shared, after_shared)
    small = jnp.concatenate(
        [
            taps_heads,
            taps_shared,
            jnp.broadcast_to(grad_rate, (dp_count, 128)),
            jnp.zeros((dp_count, 128), F32),
        ],
        axis=1,
    )
    small = jnp.sum(exchange(small.reshape(dp_count, 8, 128), "dp"), axis=0)
    small = jnp.sum(exchange(copies(small, ctx_places), "ctx"), axis=0).reshape(1, -1)
    taps_heads = small[:, :split_at]
    taps_shared = small[:, split_at : split_at + shared_width]
    rate_total = small[0, split_at + shared_width :][:heads_here]

    share = hidden_width // dp_count
    block = ((3 * share, col_width), BF16)
    owner = lax.axis_index("dp").astype(jnp.int32).reshape(1)
    back, *parts = whole(
        rows_kernel,
        [((expert_count, slot_width + 16, col_width), BF16)] + [block] * dp_count,
        [((3, hidden_width, col_width), BF16)],
        inputs=5,
        scalars=1,
        late=4,
        limit=56 * 2**20,
    )(
        owner, everything, rows_in, got_cot, w_gate[0], w_up[0], grad_mamba_in, grad_shared_in,
        taps_heads, taps_shared,
    )
    back = exchange(back, "expert")
    parts = [parts[0]] + [
        lax.ppermute(parts[k], "dp", [(i, (i + k) % dp_count) for i in range(dp_count)])
        for k in range(1, dp_count)
    ]
    grad_tokens = lax.dot_general(
        table,
        back[:, :slot_width].reshape(-1, col_width),
        (((0,), (0,)), ((), ())),
        preferred_element_type=F32,
    ).astype(BF16)
    gate_total, up_total, down_total = whole(
        totals_kernel, [((share, col_width), BF16)] * 3, inputs=dp_count, late=1
    )(*parts, grad_tokens)
    route_got = back[:, slot_width].astype(F32)
    route_total = jnp.where(
        live_slots, route_got[:, :slot_width] + route_got[:, slot_width:], 0.0
    )
    return (
        grad_mamba_in[None],
        grad_shared_in[None],
        grad_step[None],
        taps_heads,
        taps_shared,
        rate_total,
        grad_tokens[None],
        route_total[None, None],
        gate_total.T[None],
        up_total.T[None],
        down_total[None],
    )


def solution(mesh):
    placed = (
        P("dp", "ctx", "expert"),
        P("dp", "ctx", None),
        P("dp", "expert", "ctx"),
        P("expert"),
        P("expert"),
        P("expert"),
        P(None, "expert"),
        P(),
        P("dp", "ctx", "expert"),
        P("dp", "expert", "ctx"),
        P("dp", "expert", "ctx"),
        P("dp", "expert", None, None),
        P("dp", "expert", None),
        P("dp", "expert", None, None),
        P("expert", "ctx", None),
        P("expert", "ctx", None),
        P("expert", None, "ctx"),
        P("dp", "expert", "ctx", None),
        P("dp", "expert", "ctx", None),
    )
    return jax.shard_map(
        body,
        mesh=mesh,
        in_specs=placed,
        out_specs=(
            P("dp", "ctx", "expert"),
            P("dp", "ctx", None),
            P("dp", "expert", "ctx"),
            P("dp", "expert"),
            P("dp", None),
            P("expert"),
            P("dp", "expert", "ctx"),
            P("dp", "expert", None, None),
            P("expert", "ctx", "dp"),
            P("expert", "ctx", "dp"),
            P("expert", "dp", "ctx"),
        ),
        check_vma=False,
    )
```
